128 devices in a mesh: comp: 32 (over x, z_hi, y), band: 4 (over z_lo, core).
Axes of the slice: x: 4, y: 4, z: 4 (z_hi: 2, z_lo: 2; z = z_hi * 2 + z_lo), core: 2. Of those that a mesh axis runs over, the one named last changes fastest.
Arguments:
- spectrum: float32 [1152, 384, 256], P('comp', 'band'), as said below
- wet_mask: int32 [384, 256], P('band'), may hold values 0 or 1
- quad_matrix: bfloat16 [1152, 1152], replicated, may hold values from -0.1875 to 0.1875
- dissipation: float32 [1152], replicated, may hold values from 0.2 to 2
- circulation: float32 [3, 32, 4096], P(None, 'band', 'comp'), may hold values from -3 to 3
- source_points: int32 [3, 32, 4096], P(None, 'band', 'comp'), may hold values from 0 to 24575
Outputs:
- spectrum_out: float32 [1152, 384, 256], P('comp', 'band')
- circulation_out: float32 [3, 32, 4096], P(None, 'band', 'comp')
The draws below stay inside these ranges and needn't reach their ends.
Inputs may be any that keep to these rules, and one draw needn't show every extreme that they name: `spectrum`: every entry is positive. `source_points`: each entry numbers a wave point of the band that holds the cell's row, row by row within the band.
All inputs are finite; a program needn't handle non-finite values. No bound on the sum of `wet_mask` on one device may be relied on, other than what follows from the above.
Results may differ from the reference program's by a relative error of at most 0.007.
Values may be sent and summed in bfloat16 or wider, within the bound.
No kernel may reach another device: no remote copies, remote signals or barrier semaphores. Data moves between devices by JAX's collectives and lax.ppermute only.
A program may use at most 128 MiB of HBM per device.

```python
import math
import jax
import jax.numpy as jnp
from jax import lax

NF = 36
ND = 32
K = 1152
NY = 256
NX = 384
BAND_PTS = 24576
SUBSTEPS = 4
SRC_STEPS = 4
SW_STEPS = 8
TILE_X = 8
MX = 32
MY = 4096


def draw_spectrum(key, part):
    key_comp, key_point, key_jitter = jax.random.split(jax.random.fold_in(key, 11), 3)
    comp_low, comp_high, point_low, point_high, jitter_low, jitter_high = (0.3, 3.0, 0.5, 2.0, 0.5, 1.5)
    comp_scale = jnp.exp(jax.random.uniform(key_comp, (NF * ND, 1, 1), jnp.float32, math.log(comp_low), math.log(comp_high)))
    point_scale = jnp.exp(jax.random.uniform(key_point, (1, NX, NY), jnp.float32, math.log(point_low), math.log(point_high)))
    jitter = jax.random.uniform(key_jitter, (NF * ND, NX, NY), jnp.float32, jitter_low, jitter_high)
    return comp_scale * point_scale * jitter


def set_ends(array, stream_key, smallest, largest):
    spot = [jax.random.randint(jax.random.fold_in(stream_key, axis), (), 0, length) for axis, length in enumerate(array.shape)]
    longest = array.shape.index(max(array.shape))
    next_to = spot[:longest] + [(spot[longest] + 1) % array.shape[longest]] + spot[longest + 1:]
    return array.at[tuple(spot)].set(smallest).at[tuple(next_to)].set(largest)


def level_of(stream_key, extent, cuts, smallest, top_value):
    level, own = 1.0, jax.random.fold_in(stream_key, 6)
    for dim, blocks in cuts:
        heights = jnp.exp(jax.random.uniform(jax.random.fold_in(own, dim), (blocks,), jnp.float32, smallest / len(cuts), top_value / len(cuts)))
        level = level * jnp.repeat(heights, extent[dim] // blocks).reshape([-1 if axis == dim else 1 for axis in range(len(extent))])
    return level


def gaussian(stream_key, extent, scale, limit, cuts=(), kind=jnp.bfloat16):
    drawn = scale * jax.random.normal(stream_key, extent, jnp.float32)
    if cuts:
        drawn = drawn * level_of(stream_key, extent, cuts, -0.22, 0.18)
    return jnp.clip(drawn, -limit, limit).astype(kind)


def setup_inputs(seed: int = 0) -> dict:
    key_of = jax.random.split(jax.random.key(seed), 7)
    spectrum = draw_spectrum(jax.random.fold_in(key_of[6], 71), 0)
    wet_mask = set_ends((jax.random.randint(key_of[1], (NX, NY), 0, 8) < 7).astype(jnp.int32), jax.random.fold_in(key_of[1], 1), 0, 1)
    quad_matrix = gaussian(key_of[2], (K, K), K ** -0.5, 0.1875)
    dissipation = jnp.clip(jnp.exp(jax.random.uniform(key_of[3], (K,), jnp.float32, math.log(0.2), math.log(2.0))), 0.2, 2.0)
    circulation = gaussian(key_of[4], (3, MX, MY), 0.5, 3.0, ((1, 4), (2, 32)), jnp.float32)
    source_points = set_ends(jax.random.randint(key_of[5], (3, MX, MY), 0, BAND_PTS), jax.random.fold_in(key_of[5], 1), 0, BAND_PTS - 1).astype(jnp.int32)
    return {"spectrum": spectrum, "wet_mask": wet_mask, "quad_matrix": quad_matrix, "dissipation": dissipation, "circulation": circulation, "source_points": source_points}


step_source = 0.1
wave_speed = 0.35
friction = 0.05
forcing_gain = 0.15


def component_tables(offset, local_count, freqs, headings):
    indices = offset + jnp.arange(local_count, dtype=jnp.int32)
    frequency = (indices // headings).astype(jnp.float32)
    heading = (indices % headings).astype(jnp.float32)
    heading_angle = 2.0 * math.pi * (heading + 0.5) / headings
    fraction = (frequency + 0.5) / freqs
    group_speed = 0.25 + 0.4 * fraction
    wave_ratio = 0.5 + 0.5 * fraction
    cosine = jnp.cos(heading_angle)
    sine_part = jnp.sin(heading_angle)
    speed_east = group_speed * cosine
    speed_north = group_speed * sine_part
    stress_coef = jnp.stack([wave_ratio * (1.0 + cosine * cosine) - 0.5,
                             wave_ratio * sine_part * cosine,
                             wave_ratio * (1.0 + sine_part * sine_part) - 0.5])
    return speed_east, speed_north, stress_coef


def upwind(extended, speed_east, speed_north, wet_rows):
    middle = extended[:, 1:-1, :]
    west_cells = extended[:, :-2, :]
    east_cells = extended[:, 2:, :]
    padded = jnp.pad(middle, ((0, 0), (0, 0), (1, 1)))
    south_cells = padded[:, :, :-2]
    north_cells = padded[:, :, 2:]
    along_rows = speed_east[:, None, None]
    along_cols = speed_north[:, None, None]
    flux_rows = jnp.maximum(along_rows, 0.0) * (middle - west_cells) + jnp.minimum(along_rows, 0.0) * (east_cells - middle)
    flux_cols = jnp.maximum(along_cols, 0.0) * (middle - south_cells) + jnp.minimum(along_cols, 0.0) * (north_cells - middle)
    return (middle - flux_rows - flux_cols) * wet_rows


def rounded(values):
    return lax.optimization_barrier(values.astype(jnp.bfloat16)).astype(jnp.float32)


def sources(base, quad_matrix, dissipation):
    current = base
    for repeat in range(SRC_STEPS):
        product = jnp.dot(quad_matrix, current.astype(jnp.bfloat16), preferred_element_type=jnp.float32)
        energy_level = jnp.mean(current, axis=0, keepdims=True)
        current = current + step_source * current * (product - dissipation[:, None] * energy_level)
    return current


def diff_rows(extended):
    return 0.5 * (extended[2:, 1:-1] - extended[:-2, 1:-1])


def diff_cols(extended):
    return 0.5 * (extended[1:-1, 2:] - extended[1:-1, :-2])


def reference(spectrum, wet_mask, quad_matrix, dissipation, circulation, source_points):
    component_total = NF * ND
    speed_east, speed_north, stress_coef = component_tables(0, component_total, NF, ND)
    wetness = wet_mask.astype(jnp.float32)[None]
    per_frequency = spectrum.reshape(NF, ND, NX, NY)

    def propagate(packed):
        slab_block, east_part, north_part = packed
        for substep in range(SUBSTEPS):
            extended = jnp.pad(slab_block, ((0, 0), (1, 1), (0, 0)))
            slab_block = upwind(extended, east_part, north_part, wetness)
        return slab_block

    propagated = lax.map(propagate, (per_frequency, speed_east.reshape(NF, ND), speed_north.reshape(NF, ND)))
    propagated = propagated.reshape(component_total, NX, NY)
    per_row = jnp.moveaxis(propagated, 1, 0)

    def row_work(slab_row):
        base = rounded(slab_row)
        current = sources(base, quad_matrix, dissipation)
        increment = rounded(current - base)
        coupled = base + increment
        stress = jnp.dot(stress_coef, coupled, precision=lax.Precision.HIGHEST) / component_total
        return slab_row + increment, stress

    finished, row_stress = lax.map(row_work, per_row)
    new_spectrum = jnp.moveaxis(finished, 0, 1)
    stress_flat = jnp.moveaxis(row_stress, 0, 1).reshape(3, NX * NY)
    band_offset = (jnp.arange(MX, dtype=jnp.int32) // TILE_X) * BAND_PTS
    global_index = source_points + band_offset[None, :, None]
    picked = jnp.take(stress_flat, global_index.reshape(-1), axis=1).reshape(3, 3, MX, MY)
    cell_stress = 0.5 * picked[:, 0] + 0.3 * picked[:, 1] + 0.2 * picked[:, 2]
    rimmed = jnp.pad(cell_stress, ((0, 0), (1, 1), (1, 1)))
    force_down = -(diff_rows(rimmed[0]) + diff_cols(rimmed[1]))
    force_across = -(diff_rows(rimmed[1]) + diff_cols(rimmed[2]))
    height = circulation[0]
    flow_down = circulation[1]
    flow_across = circulation[2]
    for repeat in range(SW_STEPS):
        down_ext = jnp.pad(flow_down, 1)
        across_ext = jnp.pad(flow_across, 1)
        height = height - wave_speed * (diff_rows(down_ext) + diff_cols(across_ext))
        height_ext = jnp.pad(height, 1)
        flow_down = (1.0 - friction) * flow_down - wave_speed * diff_rows(height_ext) + forcing_gain * force_down
        flow_across = (1.0 - friction) * flow_across - wave_speed * diff_cols(height_ext) + forcing_gain * force_across
    return new_spectrum, jnp.stack([height, flow_down, flow_across])
```

```python
import functools
import math

import jax
import jax.numpy as jnp
from jax import lax
from jax.experimental import pallas as pl
from jax.experimental.pallas import tpu as pltpu
from jax.sharding import PartitionSpec as P

NF = 36
ND = 32
K = NF * ND
SUBSTEPS = 4
SRC_STEPS = 4
SW_STEPS = 8

step_source = 0.1
wave_speed = 0.35
friction = 0.05
forcing_gain = 0.15

LOCAL = 36
ROWS = 96
OWNERS = 32
GROUP = 16
RUN = 6
HALO = 4
KB = 4
MARGIN = 2 * SW_STEPS
TILES = 10


def component_tables(offset, local_count):
    indices = offset + jnp.arange(local_count, dtype=jnp.int32)
    frequency = (indices // ND).astype(jnp.float32)
    heading = (indices % ND).astype(jnp.float32)
    heading_angle = 2.0 * math.pi * (heading + 0.5) / ND
    fraction = (frequency + 0.5) / NF
    group_speed = 0.25 + 0.4 * fraction
    wave_ratio = 0.5 + 0.5 * fraction
    cosine = jnp.cos(heading_angle)
    sine_part = jnp.sin(heading_angle)
    speed_east = group_speed * cosine
    speed_north = group_speed * sine_part
    stress_coef = jnp.stack(
        [
            wave_ratio * (1.0 + cosine * cosine) - 0.5,
            wave_ratio * sine_part * cosine,
            wave_ratio * (1.0 + sine_part * sine_part) - 0.5,
        ]
    )
    return speed_east, speed_north, stress_coef


def propagate_kernel(
    speeds, spec_ref, top_ref, bot_ref, wet_ref, wtop_ref, wbot_ref,
    prop_ref, sent_ref, field, wet, half0, half1,
):
    ext = ROWS + 2 * HALO
    step = pl.program_id(0)

    @pl.when(step == 0)
    def _():
        wet[0:ROWS, :] = wet_ref[...].astype(jnp.float32)
        wet[ROWS:ROWS + HALO, :] = wbot_ref[0]
        wet[ROWS + HALO:ext, :] = wtop_ref[0]

    lane = lax.broadcasted_iota(jnp.int32, (ext, 128), 1)

    def advance(k, east, north):
        a = jnp.abs(speeds[0, step * KB + k])
        b = jnp.abs(speeds[1, step * KB + k])
        c = 1.0 - a - b
        left, right = field[:, :128], field[:, 128:]
        wl, wr = wet[:, :128], wet[:, 128:]
        for _ in range(SUBSTEPS):
            row_shift = 1 if east else ext - 1
            ul = pltpu.roll(left, row_shift, 0)
            ur = pltpu.roll(right, row_shift, 0)
            if north:
                rl = pltpu.roll(left, 1, 1)
                rr = pltpu.roll(right, 1, 1)
                sl = jnp.where(lane == 0, 0.0, rl)
                sr = jnp.where(lane == 0, rl, rr)
            else:
                rl = pltpu.roll(left, 127, 1)
                rr = pltpu.roll(right, 127, 1)
                sl = jnp.where(lane == 127, rr, rl)
                sr = jnp.where(lane == 127, 0.0, rr)
            left = wl * (c * left + a * ul + b * sl)
            right = wr * (c * right + a * ur + b * sr)
        left, right = left[:ROWS], right[:ROWS]
        prop_ref[k, :, :128] = left
        prop_ref[k, :, 128:] = right
        half0[pl.ds(k * ROWS, ROWS), :] = left
        half1[pl.ds(k * ROWS, ROWS), :] = right

    def one(k, carry):
        field[0:ROWS, :] = spec_ref[k]
        field[ROWS:ROWS + HALO, :] = bot_ref[k]
        field[ROWS + HALO:ext, :] = top_ref[k]
        ax = speeds[0, step * KB + k]
        ay = speeds[1, step * KB + k]
        for east in (True, False):
            for north in (True, False):
                hit_x = ax >= 0.0 if east else ax < 0.0
                hit_y = ay >= 0.0 if north else ay < 0.0
                pl.when(hit_x & hit_y)(functools.partial(advance, k, east, north))
        return carry

    lax.fori_loop(0, KB, one, 0)
    for h, half in enumerate((half0, half1)):
        for g in range(GROUP):
            picked = half[pl.ds(g, KB * RUN, stride=GROUP), :]
            sent_ref[h * GROUP + g] = picked.astype(jnp.bfloat16)


def propagate(speeds, spectrum, top, bottom, wet_mask):
    cols = spectrum.shape[2]
    smem = pl.BlockSpec(memory_space=pltpu.SMEM)
    edge = pl.BlockSpec((KB, HALO, cols), lambda i: (i, 0, 0))
    wet_edge = pl.BlockSpec((1, HALO, cols), lambda i: (LOCAL, 0, 0))
    body = pl.BlockSpec((KB, ROWS, cols), lambda i: (i, 0, 0))
    return pl.pallas_call(
        propagate_kernel,
        grid=(LOCAL // KB,),
        in_specs=[
            smem, body, edge, edge,
            pl.BlockSpec((ROWS, cols), lambda i: (0, 0)),
            wet_edge, wet_edge,
        ],
        out_specs=[body, pl.BlockSpec((OWNERS, KB * RUN, 128), lambda i: (0, i, 0))],
        out_shape=[
            jax.ShapeDtypeStruct((LOCAL, ROWS, cols), jnp.float32),
            jax.ShapeDtypeStruct((OWNERS, LOCAL * RUN, 128), jnp.bfloat16),
        ],
        scratch_shapes=[
            pltpu.VMEM((ROWS + 2 * HALO, cols), jnp.float32),
            pltpu.VMEM((ROWS + 2 * HALO, cols), jnp.float32),
            pltpu.VMEM((KB * ROWS, 128), jnp.float32),
            pltpu.VMEM((KB * ROWS, 128), jnp.float32),
        ],
        name="propagate",
    )(speeds, spectrum, top, bottom, wet_mask, top, bottom)


MB = 384
NB = 256


def source_kernel(recv_ref, quad_ref, diss_ref, coef_ref, out_ref, stress_ref, flat, cur, xb, level):
    total = recv_ref.shape[0]
    chunk = 1152

    def widen(i, carry):
        flat[pl.ds(i * chunk, chunk), :] = recv_ref[pl.ds(i * chunk, chunk), :].astype(jnp.float32)
        return carry

    lax.fori_loop(0, total // chunk, widen, 0)
    for j in range(RUN):
        base = flat[pl.ds(j, K, stride=RUN), :]
        cols = slice(j * 128, (j + 1) * 128)
        cur[:, cols] = base
        xb[0, :, cols] = base.astype(jnp.bfloat16)
        level[0, :, cols] = jnp.sum(base, axis=0, keepdims=True)

    def step(s, carry):
        old = s % 2
        new = 1 - old
        for n in range(RUN * 128 // NB):
            cols = slice(n * NB, (n + 1) * NB)
            mean = level[old, :, cols] * (1.0 / K)
            sums = jnp.zeros((1, NB), jnp.float32)
            for m in range(K // MB):
                rows = slice(m * MB, (m + 1) * MB)
                product = jnp.dot(
                    quad_ref[rows, :], xb[old, :, cols], preferred_element_type=jnp.float32
                )
                rate = jnp.concatenate([diss_ref[rows, :]] * (NB // 128), axis=1)
                now = cur[rows, cols]
                now = now + step_source * now * (product - rate * mean)
                cur[rows, cols] = now
                xb[new, rows, cols] = now.astype(jnp.bfloat16)
                sums = sums + jnp.sum(now, axis=0, keepdims=True)
            level[new, :, cols] = sums
        return carry

    lax.fori_loop(0, SRC_STEPS, step, 0)
    for j in range(RUN):
        base = flat[pl.ds(j, K, stride=RUN), :]
        cols = slice(j * 128, (j + 1) * 128)
        gain = (cur[:, cols] - base).astype(jnp.bfloat16).astype(jnp.float32)
        flat[pl.ds(j, K, stride=RUN), :] = gain
        coupled = base + gain
        for c in range(3):
            row = jnp.sum(coef_ref[c] * coupled, axis=0, keepdims=True) * (1.0 / K)
            stress_ref[c * 8 + j:c * 8 + j + 1, :] = row
    for c in range(3):
        stress_ref[c * 8 + RUN:c * 8 + 8, :] = jnp.zeros((8 - RUN, 128), jnp.float32)

    def narrow(i, carry):
        out_ref[pl.ds(i * chunk, chunk), :] = flat[pl.ds(i * chunk, chunk), :].astype(jnp.bfloat16)
        return carry

    lax.fori_loop(0, total // chunk, narrow, 0)


def sources(received, quad_matrix, rate_wide, coef_wide):
    points = RUN * 128
    return pl.pallas_call(
        source_kernel,
        out_shape=[
            jax.ShapeDtypeStruct(received.shape, jnp.bfloat16),
            jax.ShapeDtypeStruct((24, 128), jnp.float32),
        ],
        scratch_shapes=[
            pltpu.VMEM((K * RUN, 128), jnp.float32),
            pltpu.VMEM((K, points), jnp.float32),
            pltpu.VMEM((2, K, points), jnp.bfloat16),
            pltpu.VMEM((2, 1, points), jnp.float32),
        ],
        name="sources",
    )(received, quad_matrix, rate_wide, coef_wide)


def pick_kernel(table_ref, points_ref, out_ref):
    pieces = []
    for c in range(3):
        rows = table_ref[:, c * 8:(c + 1) * 8, :].reshape(OWNERS * 8, 128)
        turned = rows.T
        high = turned.astype(jnp.bfloat16)
        pieces.append(high)
        pieces.append((turned - high.astype(jnp.float32)).astype(jnp.bfloat16))
    table = jnp.concatenate(pieces, axis=0)
    slot = lax.broadcasted_iota(jnp.int32, (OWNERS * 8, 128), 0)
    within = lax.broadcasted_iota(jnp.int32, (128, 128), 0)
    weights = (0.5, 0.3, 0.2)
    for t in range(TILES):
        hots, lows = [], []
        for m in range(3):
            p = points_ref[m * TILES + t:m * TILES + t + 1, :]
            row = p >> 8
            col = p & 255
            hi = (((col >> 7) * GROUP + (row & (GROUP - 1))) << 3) + (row >> 4)
            hots.append(jnp.where(slot == hi, 1.0, 0.0).astype(jnp.bfloat16))
            lows.append(col & 127)
        hot = jnp.concatenate(hots, axis=1)
        found = jnp.dot(table, hot, preferred_element_type=jnp.float32)
        for c in range(3):
            both = found[2 * c * 128:(2 * c + 1) * 128] + found[(2 * c + 1) * 128:(2 * c + 2) * 128]
            acc = jnp.zeros((128, 128), jnp.float32)
            for m in range(3):
                acc = acc + jnp.where(
                    within == lows[m], both[:, m * 128:(m + 1) * 128] * weights[m], 0.0
                )
            out_ref[c, t:t + 1, :] = jnp.sum(acc, axis=0, keepdims=True)


def pick(table, points):
    return pl.pallas_call(
        pick_kernel,
        out_shape=jax.ShapeDtypeStruct((3, TILES, 128), jnp.float32),
        name="pick",
    )(table, points)


def finish_kernel(back_ref, prop_ref, out_ref, half0, half1):
    for h, half in enumerate((half0, half1)):
        for g in range(GROUP):
            half[pl.ds(g, KB * RUN, stride=GROUP), :] = back_ref[h * GROUP + g].astype(jnp.float32)
    for k in range(KB):
        rows = slice(k * ROWS, (k + 1) * ROWS)
        out_ref[k, :, :128] = prop_ref[k, :, :128] + half0[rows, :]
        out_ref[k, :, 128:] = prop_ref[k, :, 128:] + half1[rows, :]


def finish(back, propagated):
    cols = propagated.shape[2]
    body = pl.BlockSpec((KB, ROWS, cols), lambda i: (i, 0, 0))
    return pl.pallas_call(
        finish_kernel,
        grid=(LOCAL // KB,),
        in_specs=[pl.BlockSpec((OWNERS, KB * RUN, 128), lambda i: (0, i, 0)), body],
        out_specs=body,
        out_shape=jax.ShapeDtypeStruct(propagated.shape, jnp.float32),
        scratch_shapes=[
            pltpu.VMEM((KB * ROWS, 128), jnp.float32),
            pltpu.VMEM((KB * ROWS, 128), jnp.float32),
        ],
        name="finish",
    )(back, propagated)


def from_neighbours(low, high, axis):
    count = lax.axis_size(axis)
    ends = count - 1
    before = lax.ppermute(high, axis, [(i, (i + 1) % count) for i in range(ends)])
    after = lax.ppermute(low, axis, [((i + 1) % count, i) for i in range(ends)])
    return before, after


def diff_rows(extended):
    return 0.5 * (extended[2:, 1:-1] - extended[:-2, 1:-1])


def diff_cols(extended):
    return 0.5 * (extended[1:-1, 2:] - extended[1:-1, :-2])


def shallow_water(wide_state, wide_stress, tile_cols, tile_rows):
    groups = lax.axis_size("comp")
    wide_cols = wide_state.shape[2]
    global_col = (
        lax.axis_index("comp") * tile_cols - MARGIN + jnp.arange(wide_cols, dtype=jnp.int32)
    )
    within = (global_col >= 0) & (global_col < tile_cols * groups)
    inside = within.astype(jnp.float32)[None, :]
    rimmed = jnp.pad(jnp.where(within, wide_stress, 0.0), ((0, 0), (1, 1), (1, 1)))
    force_down = -(diff_rows(rimmed[0]) + diff_cols(rimmed[1]))
    force_across = -(diff_rows(rimmed[1]) + diff_cols(rimmed[2]))
    height, flow_down, flow_across = wide_state
    for _ in range(SW_STEPS):
        down_ext = jnp.pad(flow_down, 1)
        across_ext = jnp.pad(flow_across, 1)
        height = (height - wave_speed * (diff_rows(down_ext) + diff_cols(across_ext))) * inside
        height_ext = jnp.pad(height, 1)
        flow_down = (
            (1.0 - friction) * flow_down
            - wave_speed * diff_rows(height_ext)
            + forcing_gain * force_down
        ) * inside
        flow_across = (
            (1.0 - friction) * flow_across
            - wave_speed * diff_cols(height_ext)
            + forcing_gain * force_across
        ) * inside
    stacked = jnp.stack([height, flow_down, flow_across])
    row_start = lax.axis_index("band") * tile_rows
    own_rows = lax.dynamic_slice_in_dim(stacked, row_start, tile_rows, 1)
    return own_rows[:, :, MARGIN:MARGIN + tile_cols]


def on_device(spectrum, wet_mask, quad_matrix, dissipation, circulation, source_points):
    offset = lax.axis_index("comp") * LOCAL
    speed_east, speed_north, _ = component_tables(offset, LOCAL)
    speeds = jnp.stack([speed_east, speed_north])
    wetness = wet_mask.astype(jnp.float32)[None]
    low = jnp.concatenate([spectrum[:, :HALO], wetness[:, :HALO]], axis=0)
    high = jnp.concatenate([spectrum[:, -HALO:], wetness[:, -HALO:]], axis=0)
    top, bottom = from_neighbours(low, high, "band")
    propagated, sent = propagate(speeds, spectrum, top, bottom, wet_mask)
    received = lax.all_to_all(sent, "comp", 0, 0, tiled=True)

    tile_rows = circulation.shape[1]
    tile_cols = circulation.shape[2]
    both = jnp.concatenate([circulation, source_points.astype(jnp.float32)], axis=0)
    before, after = from_neighbours(both[:, :, :MARGIN], both[:, :, -MARGIN:], "comp")
    wide = jnp.concatenate([before, both, after], axis=2)
    left_points = before[3:].astype(jnp.int32).reshape(3, 1, 128)
    right_points = after[3:].astype(jnp.int32).reshape(3, 1, 128)
    points = jnp.concatenate([source_points, left_points, right_points], axis=1)
    points = points.reshape(3 * TILES, 128)

    full_coef = component_tables(0, K)[2]
    coef_wide = jnp.broadcast_to(full_coef[:, :, None], (3, K, 128))
    rate_wide = jnp.broadcast_to(dissipation[:, None], (K, 128))
    increments, stress = sources(received.reshape(K * RUN, 128), quad_matrix, rate_wide, coef_wide)
    table = lax.all_to_all(
        jnp.broadcast_to(stress[None], (OWNERS, 24, 128)), "comp", 0, 0, tiled=True
    )
    returned = lax.all_to_all(
        increments.reshape(OWNERS, LOCAL * RUN, 128), "comp", 0, 0, tiled=True
    )
    cells = pick(table, points)
    own = cells[:, :tile_rows]
    left = cells[:, tile_rows].reshape(3, tile_rows, MARGIN)
    right = cells[:, tile_rows + 1].reshape(3, tile_rows, MARGIN)
    wide_cells = jnp.concatenate([left, own, right], axis=2)
    everything = lax.all_gather(
        jnp.concatenate([wide[:3], wide_cells], axis=0), "band", axis=1, tiled=True
    )
    circulation_out = shallow_water(everything[:3], everything[3:], tile_cols, tile_rows)
    spectrum_out = finish(returned, propagated)
    return spectrum_out, circulation_out


def solution(mesh):
    in_specs = (
        P("comp", "band", None),
        P("band", None),
        P(),
        P(),
        P(None, "band", "comp"),
        P(None, "band", "comp"),
    )
    out_specs = (P("comp", "band", None), P(None, "band", "comp"))
    return jax.shard_map(
        on_device, mesh=mesh, in_specs=in_specs, out_specs=out_specs, check_vma=False
    )
```

```python
import math

import jax
import jax.numpy as jnp
from jax import lax
from jax.experimental import pallas as pl
from jax.experimental.pallas import tpu as pltpu
from jax.sharding import PartitionSpec as P


NF = 36
ND = 32
K = NF * ND
SUBSTEPS = 4
SRC_STEPS = 4
SW_STEPS = 8

step_source = 0.1
wave_speed = 0.35
friction = 0.05
forcing_gain = 0.15

LOCAL = 36
ROWS = 96
OWNERS = 32
GROUP = 16
RUN = 6
HALO = 4
KB = 4
MARGIN = 2 * SW_STEPS
TILES = 10


def component_tables(offset, local_count):
    indices = offset + jnp.arange(local_count, dtype=jnp.int32)
    frequency = (indices // ND).astype(jnp.float32)
    heading = (indices % ND).astype(jnp.float32)
    heading_angle = 2.0 * math.pi * (heading + 0.5) / ND
    fraction = (frequency + 0.5) / NF
    group_speed = 0.25 + 0.4 * fraction
    wave_ratio = 0.5 + 0.5 * fraction
    cosine = jnp.cos(heading_angle)
    sine_part = jnp.sin(heading_angle)
    speed_east = group_speed * cosine
    speed_north = group_speed * sine_part
    stress_coef = jnp.stack(
        [
            wave_ratio * (1.0 + cosine * cosine) - 0.5,
            wave_ratio * sine_part * cosine,
            wave_ratio * (1.0 + sine_part * sine_part) - 0.5,
        ]
    )
    return speed_east, speed_north, stress_coef


def in_hbm(array):
    return pltpu.with_memory_space_constraint(array, pltpu.HBM)


def in_vmem(array):
    return pltpu.with_memory_space_constraint(array, pltpu.VMEM)


def propagate_kernel(
    speeds, spec_hbm, top_ref, bot_ref, wet_ref, prop0_hbm, prop1_hbm, sent_hbm,
    spec_ref, load_sems, prop0, prop1, sent_ref, wet, left_a, right_a, left_b, right_b, keep_sems, sent_sems,
):
    ext = ROWS + 2 * HALO

    def keep(i):
        part = pl.ds(i * KB * ROWS, KB * ROWS)
        return [
            pltpu.make_async_copy(prop.at[part], hbm.at[part], keep_sems.at[h, i])
            for h, (prop, hbm) in enumerate(((prop0, prop0_hbm), (prop1, prop1_hbm)))
        ]

    def give(o):
        return pltpu.make_async_copy(sent_ref.at[o], sent_hbm.at[o], sent_sems.at[o])

    def load(i):
        part = pl.ds(i * KB, KB)
        return pltpu.make_async_copy(spec_hbm.at[part], spec_ref.at[part], load_sems.at[i])

    def start_load(i, carry):
        load(i).start()
        return carry

    lax.fori_loop(0, LOCAL // KB, start_load, 0)
    wet[0:ROWS, :] = wet_ref[...]
    wet[ROWS:ROWS + HALO, :] = bot_ref[LOCAL]
    wet[ROWS + HALO:ext, :] = top_ref[LOCAL]
    lane = lax.broadcasted_iota(jnp.int32, (ext, 128), 1)

    def advance(k, ahead, a, b, north):
        c = 1.0 - a - b
        edge = 0 if north else 127
        turn = 1 if north else 127
        side = jnp.where(lane == edge, 0.0, b)
        fields = ((left_a, right_a), (left_b, right_b))
        for s in range(SUBSTEPS):
            left_ref, right_ref = fields[s % 2]
            left, right = left_ref[8:8 + ext, :], right_ref[8:8 + ext, :]
            ul = left_ref[pl.ds(8 + ahead, ext), :]
            ur = right_ref[pl.ds(8 + ahead, ext), :]
            rl = pltpu.roll(left, turn, 1)
            rr = pltpu.roll(right, turn, 1)
            if north:
                across_l = side * rl
                across_r = b * jnp.where(lane == 0, rl, rr)
            else:
                across_l = b * jnp.where(lane == 127, rr, rl)
                across_r = side * rr
            left = wet[:, :128] * (c * left + a * ul + across_l)
            right = wet[:, 128:] * (c * right + a * ur + across_r)
            if s + 1 < SUBSTEPS:
                left_ref, right_ref = fields[(s + 1) % 2]
                for ref, value in ((left_ref, left), (right_ref, right)):
                    ref[8:8 + ext, :] = value
                    ref[7:8, :] = value[ext - 1:]
                    ref[8 + ext:9 + ext, :] = value[0:1]
        prop0[pl.ds(k * ROWS, ROWS), :] = left[:ROWS]
        prop1[pl.ds(k * ROWS, ROWS), :] = right[:ROWS]

    def one(k, carry):
        for h, ref in enumerate((left_a, right_a)):
            cols = slice(h * 128, (h + 1) * 128)
            top = top_ref[k, :, cols]
            ref[8:8 + ROWS, :] = spec_ref[k, :, cols]
            ref[8 + ROWS:8 + ROWS + HALO, :] = bot_ref[k, :, cols]
            ref[8 + ROWS + HALO:8 + ext, :] = top
            ref[7:8, :] = top[HALO - 1:]
            ref[8 + ext:9 + ext, :] = spec_ref[k, 0:1, cols]
        ax = speeds[0, k]
        ay = speeds[1, k]
        ahead = jnp.where(ax >= 0.0, -1, 1)
        a = jnp.abs(ax)
        b = jnp.abs(ay)

        @pl.when(ay >= 0.0)
        def _():
            advance(k, ahead, a, b, True)

        @pl.when(ay < 0.0)
        def _():
            advance(k, ahead, a, b, False)

        return carry

    def block(i, carry):
        load(i).wait()
        lax.fori_loop(i * KB, (i + 1) * KB, one, 0)
        for copy in keep(i):
            copy.start()
        return carry

    lax.fori_loop(0, LOCAL // KB, block, 0)

    def regroup(g, carry):
        for h, prop in enumerate((prop0, prop1)):
            o = h * GROUP + g
            picked = prop[pl.ds(g, LOCAL * RUN, stride=GROUP), :]
            sent_ref[o] = picked.astype(jnp.bfloat16)
            give(o).start()
        return carry

    lax.fori_loop(0, GROUP, regroup, 0)

    def settle_keep(i, carry):
        for copy in keep(i):
            copy.wait()
        return carry

    def settle_give(o, carry):
        give(o).wait()
        return carry

    lax.fori_loop(0, LOCAL // KB, settle_keep, 0)
    lax.fori_loop(0, OWNERS, settle_give, 0)


def propagate(speeds, spectrum, top, bottom, wetness):
    cols = spectrum.shape[2]
    ext = ROWS + 2 * HALO
    vmem = pl.BlockSpec(memory_space=pltpu.VMEM)
    hbm = pl.BlockSpec(memory_space=pltpu.HBM)
    return pl.pallas_call(
        propagate_kernel,
        in_specs=[pl.BlockSpec(memory_space=pltpu.SMEM), hbm] + [vmem] * 3,
        out_specs=[hbm] * 3,
        out_shape=[
            pltpu.HBM((LOCAL * ROWS, 128), jnp.float32),
            pltpu.HBM((LOCAL * ROWS, 128), jnp.float32),
            pltpu.HBM((OWNERS, LOCAL * RUN, 128), jnp.bfloat16),
        ],
        scratch_shapes=[
            pltpu.VMEM((LOCAL, ROWS, cols), jnp.float32),
            pltpu.SemaphoreType.DMA((LOCAL // KB,)),
            pltpu.VMEM((LOCAL * ROWS, 128), jnp.float32),
            pltpu.VMEM((LOCAL * ROWS, 128), jnp.float32),
            pltpu.VMEM((OWNERS, LOCAL * RUN, 128), jnp.bfloat16),
            pltpu.VMEM((ext, cols), jnp.float32),
        ]
        + [pltpu.VMEM((ext + 16, 128), jnp.float32)] * 4
        + [pltpu.SemaphoreType.DMA((2, LOCAL // KB)), pltpu.SemaphoreType.DMA((OWNERS,))],
        compiler_params=pltpu.CompilerParams(vmem_limit_bytes=16 << 20),
        name="propagate",
    )(speeds, in_hbm(spectrum), *map(in_vmem, (top, bottom, wetness)))


MB = 384
NB = 256
FIRST = 2
FIRST_ROWS = FIRST * LOCAL
REST = RUN - FIRST
PIECES = 6
BLOCKS = RUN * 128 // NB


def source_kernel(
    recv_ref, quad_hbm, diss_ref, coef_ref, points_ref, first_hbm, rest_hbm,
    quad_ref, first_ref, rest_ref, flat, cur, xa, xb, rate, level, flat_first, flat_rest,
    quad_sem, out_sems,
):
    chunk = K
    fetch = pltpu.make_async_copy(quad_hbm, quad_ref, quad_sem)
    fetch.start()

    def give(o):
        return (
            pltpu.make_async_copy(first_ref.at[o], first_hbm.at[o], out_sems.at[0, o]),
            pltpu.make_async_copy(rest_ref.at[o], rest_hbm.at[o], out_sems.at[1, o]),
        )

    def widen(i, carry):
        flat[pl.ds(i * chunk, chunk), :] = recv_ref[pl.ds(i * chunk, chunk), :].astype(jnp.float32)
        return carry

    lax.fori_loop(0, RUN, widen, 0)
    for i in range(K // 128):
        rate[i * 128:(i + 1) * 128, :] = jnp.broadcast_to(diss_ref[i:i + 1, :], (128, 128)).T
    for j in range(RUN):
        base = flat[pl.ds(j, K, stride=RUN), :]
        cols = slice(j * 128, (j + 1) * 128)
        cur[:, cols] = base
        xa[:, cols] = base.astype(jnp.bfloat16)
        level[:, cols] = jnp.sum(base, axis=0, keepdims=True)

    coef = coef_ref[...]
    stress = [
        jnp.dot(coef, xa[:, n * NB:(n + 1) * NB], preferred_element_type=jnp.float32)
        for n in range(BLOCKS)
    ]

    fetch.wait()

    def step(old, new):
        for n in range(BLOCKS):
            cols = slice(n * NB, (n + 1) * NB)
            mean = level[:, cols] * (1.0 / K)
            sums = jnp.zeros((1, NB), jnp.float32)
            for m in range(K // MB):
                rows = slice(m * MB, (m + 1) * MB)
                product = jnp.dot(
                    quad_ref[rows, :], old[:, cols], preferred_element_type=jnp.float32
                )
                each = jnp.concatenate([rate[rows, :]] * (NB // 128), axis=1)
                now = cur[rows, cols]
                now = now + step_source * now * (product - each * mean)
                cur[rows, cols] = now
                new[rows, cols] = now.astype(jnp.bfloat16)
                sums = sums + jnp.sum(now, axis=0, keepdims=True)
            level[:, cols] = sums

    def two_steps(i, carry):
        step(xa, xb)
        step(xb, xa)
        return carry

    lax.fori_loop(0, SRC_STEPS // 2, two_steps, 0)
    for j in range(RUN):
        base = flat[pl.ds(j, K, stride=RUN), :]
        cols = slice(j * 128, (j + 1) * 128)
        gain = (cur[:, cols] - base).astype(jnp.bfloat16)
        xb[:, cols] = gain
        if j < FIRST:
            flat_first[pl.ds(j, K, stride=FIRST), :] = gain.astype(jnp.float32)
        else:
            flat_rest[pl.ds(j - FIRST, K, stride=REST), :] = gain.astype(jnp.float32)
    parts = []
    for n in range(BLOCKS):
        both = stress[n] + jnp.dot(
            coef, xb[:, n * NB:(n + 1) * NB], preferred_element_type=jnp.float32
        )
        rows = [both[c:c + 1] + both[3 + c:4 + c] + both[6 + c:7 + c] for c in range(3)]
        parts.append(jnp.concatenate(rows, axis=0) * (1.0 / K))
    pieces = []
    for c in range(3):
        rows = [parts[j * 128 // NB][c:c + 1, j * 128 % NB:j * 128 % NB + 128] for j in range(RUN)]
        whole = jnp.concatenate(rows + [jnp.zeros((8 - RUN, 128), jnp.float32)], axis=0)
        high = whole.astype(jnp.bfloat16).astype(jnp.float32)
        pieces += [high, whole - high]
    shared = jnp.concatenate(pieces, axis=0).astype(jnp.bfloat16)

    def narrow(o, carry):
        gain = flat_first[pl.ds(o * FIRST_ROWS, FIRST_ROWS), :].astype(jnp.bfloat16)
        first_ref[o, 0:FIRST_ROWS, :] = gain
        first_ref[o, FIRST_ROWS:FIRST_ROWS + 8 * PIECES, :] = shared
        rows = LOCAL * REST
        rest_ref[o] = flat_rest[pl.ds(o * rows, rows), :].astype(jnp.bfloat16)
        for copy in give(o):
            copy.start()
        return carry

    def settle(o, carry):
        for copy in give(o):
            copy.wait()
        return carry

    lax.fori_loop(0, OWNERS, narrow, 0)
    lax.fori_loop(0, OWNERS, settle, 0)


def sources(received, quad_matrix, rates, coef, points_list):
    points = RUN * 128
    vmem = pl.BlockSpec(memory_space=pltpu.VMEM)
    hbm = pl.BlockSpec(memory_space=pltpu.HBM)
    return pl.pallas_call(
        source_kernel,
        in_specs=[vmem, hbm, vmem, vmem, hbm],
        out_specs=[hbm] * 2,
        out_shape=[
            pltpu.HBM((OWNERS, FIRST_ROWS + 8 * PIECES, 128), jnp.bfloat16),
            pltpu.HBM((OWNERS, LOCAL * REST, 128), jnp.bfloat16),
        ],
        scratch_shapes=[
            pltpu.VMEM((K, K), jnp.bfloat16),
            pltpu.VMEM((OWNERS, FIRST_ROWS + 8 * PIECES, 128), jnp.bfloat16),
            pltpu.VMEM((OWNERS, LOCAL * REST, 128), jnp.bfloat16),
            pltpu.VMEM((K * RUN, 128), jnp.float32),
            pltpu.VMEM((K, points), jnp.float32),
            pltpu.VMEM((K, points), jnp.bfloat16),
            pltpu.VMEM((K, points), jnp.bfloat16),
            pltpu.VMEM((K, 128), jnp.float32),
            pltpu.VMEM((1, points), jnp.float32),
            pltpu.VMEM((K * FIRST, 128), jnp.float32),
            pltpu.VMEM((K * REST, 128), jnp.float32),
            pltpu.SemaphoreType.DMA(()),
            pltpu.SemaphoreType.DMA((2, OWNERS)),
        ],
        compiler_params=pltpu.CompilerParams(vmem_limit_bytes=30 << 20),
        name="sources",
    )(in_vmem(received), in_hbm(quad_matrix), in_vmem(rates), in_vmem(coef), in_hbm(points_list))


def pick_kernel(first_ref, points_ref, out_ref):
    pieces = []
    for i in range(PIECES):
        at = FIRST_ROWS + 8 * i
        rows = first_ref[:, at:at + 8, :].astype(jnp.float32).reshape(OWNERS * 8, 128)
        pieces.append(rows.T.astype(jnp.bfloat16))
    table = jnp.concatenate(pieces, axis=0)
    slot = lax.broadcasted_iota(jnp.int32, (OWNERS * 8, 128), 0)
    within = lax.broadcasted_iota(jnp.int32, (128, 128), 0)
    weights = (0.5, 0.3, 0.2)
    for t in range(TILES):
        hots, lows = [], []
        for m in range(3):
            p = points_ref[m * TILES + t:m * TILES + t + 1, :]
            row = p >> 8
            col = p & 255
            hi = (((col >> 7) * GROUP + (row & (GROUP - 1))) << 3) + (row >> 4)
            hots.append(jnp.where(slot == hi, 1.0, 0.0).astype(jnp.bfloat16))
            lows.append(col & 127)
        hot = jnp.concatenate(hots, axis=1)
        found = jnp.dot(table, hot, preferred_element_type=jnp.float32)
        for c in range(3):
            both = found[2 * c * 128:(2 * c + 1) * 128] + found[(2 * c + 1) * 128:(2 * c + 2) * 128]
            acc = jnp.zeros((128, 128), jnp.float32)
            for m in range(3):
                acc = acc + jnp.where(
                    within == lows[m], both[:, m * 128:(m + 1) * 128] * weights[m], 0.0
                )
            out_ref[c, t:t + 1, :] = jnp.sum(acc, axis=0, keepdims=True)


def pick(first, points):
    vmem = pl.BlockSpec(memory_space=pltpu.VMEM)
    return pl.pallas_call(
        pick_kernel,
        in_specs=[vmem] * 2,
        out_specs=vmem,
        out_shape=pltpu.VMEM((3, TILES, 128), jnp.float32),
        compiler_params=pltpu.CompilerParams(vmem_limit_bytes=10 << 20),
        name="pick",
    )(in_vmem(first), in_vmem(points))


def finish_kernel(
    first_ref, rest_ref, prop0_hbm, prop1_hbm, out_hbm,
    prop0, prop1, spread_first, spread_rest, out, sems, keep_sems,
):
    def keep(i):
        part = pl.ds(i * KB * ROWS, KB * ROWS)
        return [
            pltpu.make_async_copy(hbm.at[part], prop.at[part], keep_sems.at[h, i])
            for h, (prop, hbm) in enumerate(((prop0, prop0_hbm), (prop1, prop1_hbm)))
        ]

    def load(i, carry):
        for copy in keep(i):
            copy.start()
        return carry

    lax.fori_loop(0, LOCAL // KB, load, 0)

    def spread(g, carry):
        for h in range(2):
            o = h * GROUP + g
            spread_first[h, pl.ds(g, FIRST_ROWS, stride=GROUP), :] = first_ref[
                o, 0:FIRST_ROWS, :
            ].astype(jnp.float32)
            spread_rest[h, pl.ds(g, LOCAL * REST, stride=GROUP), :] = rest_ref[o].astype(
                jnp.float32
            )
        return carry

    lax.fori_loop(0, GROUP, spread, 0)
    cut = FIRST * GROUP

    def copy(i):
        part = pl.ds(i * KB, KB)
        return pltpu.make_async_copy(out.at[part], out_hbm.at[part], sems.at[i])

    def add(i, carry):
        for copy_in in keep(i):
            copy_in.wait()
        for kk in range(KB):
            k = i * KB + kk
            for h, prop in enumerate((prop0, prop1)):
                cols = slice(h * 128, (h + 1) * 128)
                out[k, 0:cut, cols] = (
                    prop[pl.ds(k * ROWS, cut), :] + spread_first[h, pl.ds(k * cut, cut), :]
                )
                tail = ROWS - cut
                out[k, cut:ROWS, cols] = (
                    prop[pl.ds(k * ROWS + cut, tail), :] + spread_rest[h, pl.ds(k * tail, tail), :]
                )
        copy(i).start()
        return carry

    lax.fori_loop(0, LOCAL // KB, add, 0)

    def settle(i, carry):
        copy(i).wait()
        return carry

    lax.fori_loop(0, LOCAL // KB, settle, 0)


def finish(first, rest, prop0, prop1):
    vmem = pl.BlockSpec(memory_space=pltpu.VMEM)
    hbm = pl.BlockSpec(memory_space=pltpu.HBM)
    shape = (LOCAL, ROWS, 256)
    return pl.pallas_call(
        finish_kernel,
        in_specs=[vmem, vmem, hbm, hbm],
        out_specs=hbm,
        out_shape=pltpu.HBM(shape, jnp.float32),
        scratch_shapes=[
            pltpu.VMEM((LOCAL * ROWS, 128), jnp.float32),
            pltpu.VMEM((LOCAL * ROWS, 128), jnp.float32),
            pltpu.VMEM((2, LOCAL * FIRST * GROUP, 128), jnp.float32),
            pltpu.VMEM((2, LOCAL * REST * GROUP, 128), jnp.float32),
            pltpu.VMEM(shape, jnp.float32),
            pltpu.SemaphoreType.DMA((LOCAL // KB,)),
            pltpu.SemaphoreType.DMA((2, LOCAL // KB)),
        ],
        compiler_params=pltpu.CompilerParams(vmem_limit_bytes=16 << 20),
        name="finish",
    )(in_vmem(first), in_vmem(rest), in_hbm(prop0), in_hbm(prop1))


def from_neighbours(low, high, axis):
    count = lax.axis_size(axis)
    ends = count - 1
    before = lax.ppermute(high, axis, [(i, (i + 1) % count) for i in range(ends)])
    after = lax.ppermute(low, axis, [((i + 1) % count, i) for i in range(ends)])
    return before, after


def diff_rows(extended):
    return 0.5 * (extended[2:, 1:-1] - extended[:-2, 1:-1])


def diff_cols(extended):
    return 0.5 * (extended[1:-1, 2:] - extended[1:-1, :-2])


def shallow_water(wide_state, wide_stress, tile_cols, tile_rows):
    groups = lax.axis_size("comp")
    wide_cols = wide_state.shape[2]
    global_col = (
        lax.axis_index("comp") * tile_cols - MARGIN + jnp.arange(wide_cols, dtype=jnp.int32)
    )
    within = (global_col >= 0) & (global_col < tile_cols * groups)
    inside = within.astype(jnp.float32)[None, :]
    rimmed = jnp.pad(jnp.where(within, wide_stress, 0.0), ((0, 0), (1, 1), (1, 1)))
    force_down = -(diff_rows(rimmed[0]) + diff_cols(rimmed[1]))
    force_across = -(diff_rows(rimmed[1]) + diff_cols(rimmed[2]))
    height, flow_down, flow_across = wide_state
    for _ in range(SW_STEPS):
        down_ext = jnp.pad(flow_down, 1)
        across_ext = jnp.pad(flow_across, 1)
        height = (height - wave_speed * (diff_rows(down_ext) + diff_cols(across_ext))) * inside
        height_ext = jnp.pad(height, 1)
        flow_down = (
            (1.0 - friction) * flow_down
            - wave_speed * diff_rows(height_ext)
            + forcing_gain * force_down
        ) * inside
        flow_across = (
            (1.0 - friction) * flow_across
            - wave_speed * diff_cols(height_ext)
            + forcing_gain * force_across
        ) * inside
    stacked = jnp.stack([height, flow_down, flow_across])
    row_start = lax.axis_index("band") * tile_rows
    own_rows = lax.dynamic_slice_in_dim(stacked, row_start, tile_rows, 1)
    return own_rows[:, :, MARGIN:MARGIN + tile_cols]


def window(spectrum, wet_mask, quad_matrix, dissipation, circulation, source_points):
    offset = lax.axis_index("comp") * LOCAL
    speed_east, speed_north, _ = component_tables(offset, LOCAL)
    speeds = jnp.stack([speed_east, speed_north])
    wetness = wet_mask.astype(jnp.float32)[None]
    low = jnp.concatenate([spectrum[:, :HALO], wetness[:, :HALO]], axis=0)
    high = jnp.concatenate([spectrum[:, -HALO:], wetness[:, -HALO:]], axis=0)
    top, bottom = from_neighbours(low, high, "band")
    prop0, prop1, sent = propagate(speeds, spectrum, top, bottom, wetness[0])
    received = lax.all_to_all(sent, "comp", 0, 0, tiled=True)

    tile_rows = circulation.shape[1]
    tile_cols = circulation.shape[2]
    both = jnp.concatenate([circulation, source_points.astype(jnp.float32)], axis=0)
    before, after = from_neighbours(both[:, :, :MARGIN], both[:, :, -MARGIN:], "comp")
    wide = jnp.concatenate([before, both, after], axis=2)
    left_points = before[3:].astype(jnp.int32).reshape(3, 1, 128)
    right_points = after[3:].astype(jnp.int32).reshape(3, 1, 128)
    points = jnp.concatenate([source_points, left_points, right_points], axis=1)
    points = points.reshape(3 * TILES, 128)

    full_coef = component_tables(0, K)[2]
    coef_high = full_coef.astype(jnp.bfloat16).astype(jnp.float32)
    coef_mid = (full_coef - coef_high).astype(jnp.bfloat16).astype(jnp.float32)
    coef_low = full_coef - coef_high - coef_mid
    spare = jnp.zeros((7, K), jnp.float32)
    coef = jnp.concatenate([coef_high, coef_mid, coef_low, spare]).astype(jnp.bfloat16)
    first, rest = sources(
        received.reshape(K * RUN, 128), quad_matrix, dissipation.reshape(K // 128, 128), coef, points
    )
    first = lax.all_to_all(first, "comp", 0, 0, tiled=True)
    rest = lax.all_to_all(rest, "comp", 0, 0, tiled=True)
    cells = pick(first, points)
    own = cells[:, :tile_rows]
    left = cells[:, tile_rows].reshape(3, tile_rows, MARGIN)
    right = cells[:, tile_rows + 1].reshape(3, tile_rows, MARGIN)
    wide_cells = jnp.concatenate([left, own, right], axis=2)
    everything = lax.all_gather(
        jnp.concatenate([wide[:3], wide_cells], axis=0), "band", axis=1, tiled=True
    )
    circulation_out = shallow_water(everything[:3], everything[3:], tile_cols, tile_rows)
    spectrum_out = finish(first, rest, prop0, prop1)
    return spectrum_out, circulation_out


def solution(mesh):
    in_specs = (
        P("comp", "band", None),
        P("band", None),
        P(),
        P(),
        P(None, "band", "comp"),
        P(None, "band", "comp"),
    )
    out_specs = (P("comp", "band", None), P(None, "band", "comp"))
    return jax.shard_map(window, mesh=mesh, in_specs=in_specs, out_specs=out_specs, check_vma=False)
```

```python
import math

import jax
import jax.numpy as jnp
from jax import lax
from jax.experimental import pallas as pl
from jax.experimental.pallas import tpu as pltpu
from jax.sharding import PartitionSpec as P


NF = 36
ND = 32
K = NF * ND
SUBSTEPS = 4
SRC_STEPS = 4
SW_STEPS = 8

step_source = 0.1
wave_speed = 0.35
friction = 0.05
forcing_gain = 0.15

LOCAL = 36
ROWS = 96
OWNERS = 32
GROUP = 16
RUN = 6
HALO = 4
KB = 4
PAIR = KB
MARGIN = 2 * SW_STEPS
TILES = 10


def component_tables(offset, local_count):
    indices = offset + jnp.arange(local_count, dtype=jnp.int32)
    frequency = (indices // ND).astype(jnp.float32)
    heading = (indices % ND).astype(jnp.float32)
    heading_angle = 2.0 * math.pi * (heading + 0.5) / ND
    fraction = (frequency + 0.5) / NF
    group_speed = 0.25 + 0.4 * fraction
    wave_ratio = 0.5 + 0.5 * fraction
    cosine = jnp.cos(heading_angle)
    sine_part = jnp.sin(heading_angle)
    speed_east = group_speed * cosine
    speed_north = group_speed * sine_part
    stress_coef = jnp.stack(
        [
            wave_ratio * (1.0 + cosine * cosine) - 0.5,
            wave_ratio * sine_part * cosine,
            wave_ratio * (1.0 + sine_part * sine_part) - 0.5,
        ]
    )
    return speed_east, speed_north, stress_coef


def in_hbm(array):
    return pltpu.with_memory_space_constraint(array, pltpu.HBM)


def in_vmem(array):
    return pltpu.with_memory_space_constraint(array, pltpu.VMEM)


def propagate_kernel(
    speeds, spec_hbm, top_ref, bot_ref, wet_ref, prop0_hbm, prop1_hbm, sent_hbm,
    spec_ref, load_sems, prop0, prop1, sent_ref, wet, left_a, right_a, left_b, right_b, keep_sems, sent_sems,
):
    ext = ROWS + 2 * HALO

    def keep(i):
        part = pl.ds(i * KB * ROWS, KB * ROWS)
        return [
            pltpu.make_async_copy(prop.at[part], hbm.at[part], keep_sems.at[h, i])
            for h, (prop, hbm) in enumerate(((prop0, prop0_hbm), (prop1, prop1_hbm)))
        ]

    def give(i):
        rows = pl.ds(i * KB * RUN, KB * RUN)
        return pltpu.make_async_copy(sent_ref.at[i], sent_hbm.at[:, rows, :], sent_sems.at[i])

    def regroup(i):
        for h, prop in enumerate((prop0, prop1)):
            for g in range(GROUP):
                picked = prop[pl.ds(i * KB * ROWS + g, KB * RUN, stride=GROUP), :]
                sent_ref[i, h * GROUP + g] = picked.astype(jnp.bfloat16)

    def load(i):
        part = pl.ds(i * KB, KB)
        return pltpu.make_async_copy(spec_hbm.at[part], spec_ref.at[part], load_sems.at[i])

    def start_load(i, carry):
        load(i).start()
        return carry

    lax.fori_loop(0, LOCAL // KB, start_load, 0)
    wet[0:ROWS, :] = wet_ref[...]
    wet[ROWS:ROWS + HALO, :] = bot_ref[LOCAL]
    wet[ROWS + HALO:ext, :] = top_ref[LOCAL]
    lane = lax.broadcasted_iota(jnp.int32, (ext, 128), 1)
    fields = [[(left_a.at[q], right_a.at[q]), (left_b.at[q], right_b.at[q])] for q in range(PAIR)]

    def advance(first, north):
        edge = 0 if north else 127
        turn = 1 if north else 127
        ahead, a, b, c, side = [], [], [], [], []
        for q in range(PAIR):
            ax = speeds[0, first + q]
            ahead.append(jnp.where(ax >= 0.0, 7, 9))
            a.append(jnp.abs(ax))
            b.append(jnp.abs(speeds[1, first + q]))
            c.append(1.0 - a[q] - b[q])
            side.append(jnp.where(lane == edge, 0.0, b[q]))
        for s in range(SUBSTEPS):
            for q in range(PAIR):
                left_ref, right_ref = fields[q][s % 2]
                left, right = left_ref[8:8 + ext, :], right_ref[8:8 + ext, :]
                ul = left_ref[pl.ds(ahead[q], ext), :]
                ur = right_ref[pl.ds(ahead[q], ext), :]
                rl = pltpu.roll(left, turn, 1)
                rr = pltpu.roll(right, turn, 1)
                if north:
                    across_l = side[q] * rl
                    across_r = b[q] * jnp.where(lane == 0, rl, rr)
                else:
                    across_l = b[q] * jnp.where(lane == 127, rr, rl)
                    across_r = side[q] * rr
                left = wet[:, :128] * (c[q] * left + a[q] * ul + across_l)
                right = wet[:, 128:] * (c[q] * right + a[q] * ur + across_r)
                if s + 1 < SUBSTEPS:
                    for ref, value in zip(fields[q][(s + 1) % 2], (left, right)):
                        ref[8:8 + ext, :] = value
                        ref[7:8, :] = value[ext - 1:]
                        ref[8 + ext:9 + ext, :] = value[0:1]
                else:
                    prop0[pl.ds((first + q) * ROWS, ROWS), :] = left[:ROWS]
                    prop1[pl.ds((first + q) * ROWS, ROWS), :] = right[:ROWS]

    def some(i, carry):
        first = i * PAIR
        for q in range(PAIR):
            k = first + q
            for h, ref in enumerate(fields[q][0]):
                cols = slice(h * 128, (h + 1) * 128)
                top = top_ref[k, :, cols]
                ref[8:8 + ROWS, :] = spec_ref[k, :, cols]
                ref[8 + ROWS:8 + ROWS + HALO, :] = bot_ref[k, :, cols]
                ref[8 + ROWS + HALO:8 + ext, :] = top
                ref[7:8, :] = top[HALO - 1:]
                ref[8 + ext:9 + ext, :] = spec_ref[k, 0:1, cols]
        ay = speeds[1, first]

        @pl.when(ay >= 0.0)
        def _():
            advance(first, True)

        @pl.when(ay < 0.0)
        def _():
            advance(first, False)

        return carry

    def block(i, carry):
        load(i).wait()
        some(i, 0)
        regroup(i)
        give(i).start()
        for copy in keep(i):
            copy.start()
        return carry

    count = LOCAL // KB
    lax.fori_loop(0, count, block, 0)

    def settle(i, carry):
        for copy in keep(i):
            copy.wait()
        give(i).wait()
        return carry

    lax.fori_loop(0, count, settle, 0)


def propagate(speeds, spectrum, top, bottom, wetness):
    cols = spectrum.shape[2]
    ext = ROWS + 2 * HALO
    vmem = pl.BlockSpec(memory_space=pltpu.VMEM)
    hbm = pl.BlockSpec(memory_space=pltpu.HBM)
    return pl.pallas_call(
        propagate_kernel,
        in_specs=[pl.BlockSpec(memory_space=pltpu.SMEM), hbm] + [vmem] * 3,
        out_specs=[hbm] * 3,
        out_shape=[
            pltpu.HBM((LOCAL * ROWS, 128), jnp.float32),
            pltpu.HBM((LOCAL * ROWS, 128), jnp.float32),
            pltpu.HBM((OWNERS, LOCAL * RUN, 128), jnp.bfloat16),
        ],
        scratch_shapes=[
            pltpu.VMEM((LOCAL, ROWS, cols), jnp.float32),
            pltpu.SemaphoreType.DMA((LOCAL // KB,)),
            pltpu.VMEM((LOCAL * ROWS, 128), jnp.float32),
            pltpu.VMEM((LOCAL * ROWS, 128), jnp.float32),
            pltpu.VMEM((LOCAL // KB, OWNERS, KB * RUN, 128), jnp.bfloat16),
            pltpu.VMEM((ext, cols), jnp.float32),
        ]
        + [pltpu.VMEM((PAIR, ext + 16, 128), jnp.float32)] * 4
        + [pltpu.SemaphoreType.DMA((2, LOCAL // KB)), pltpu.SemaphoreType.DMA((LOCAL // KB,))],
        compiler_params=pltpu.CompilerParams(vmem_limit_bytes=16 << 20),
        name="propagate",
    )(speeds, in_hbm(spectrum), *map(in_vmem, (top, bottom, wetness)))


MB = 576
EB = 64
NB = 256
FIRST = 2
FIRST_ROWS = FIRST * LOCAL
REST = RUN - FIRST
PIECES = 6
BLOCKS = RUN * 128 // NB


def source_kernel(
    recv_ref, quad_hbm, diss_ref, coef_ref, points_ref, first_hbm, rest_hbm,
    quad_ref, first_ref, rest_ref, prod_a, prod_b, flat, cur, xa, xb, rate, level, flat_first, flat_rest,
    quad_sem, out_sems,
):
    chunk = K
    fetch = pltpu.make_async_copy(quad_hbm, quad_ref, quad_sem)
    fetch.start()

    def give(o):
        return (
            pltpu.make_async_copy(first_ref.at[o], first_hbm.at[o], out_sems.at[0, o]),
            pltpu.make_async_copy(rest_ref.at[o], rest_hbm.at[o], out_sems.at[1, o]),
        )

    def widen(i, carry):
        flat[pl.ds(i * chunk, chunk), :] = recv_ref[pl.ds(i * chunk, chunk), :].astype(jnp.float32)
        return carry

    lax.fori_loop(0, RUN, widen, 0)
    for i in range(K // 128):
        rate[i * 128:(i + 1) * 128, :] = jnp.broadcast_to(diss_ref[i:i + 1, :], (128, 128)).T
    for j in range(RUN):
        base = flat[pl.ds(j, K, stride=RUN), :]
        cols = slice(j * 128, (j + 1) * 128)
        cur[:, cols] = base
        xa[:, cols] = base.astype(jnp.bfloat16)
        level[:, cols] = jnp.sum(base, axis=0, keepdims=True)

    coef = coef_ref[...]
    stress = [
        jnp.dot(coef, xa[:, n * NB:(n + 1) * NB], preferred_element_type=jnp.float32)
        for n in range(BLOCKS)
    ]

    fetch.wait()

    def multiply(s, n):
        held = (prod_a, prod_b)[(s * BLOCKS + n) % 2]
        old = (xa, xb)[s % 2]
        for m in range(K // MB):
            rows = slice(m * MB, (m + 1) * MB)
            held[rows, :] = jnp.dot(
                quad_ref[rows, :], old[:, n * NB:(n + 1) * NB], preferred_element_type=jnp.float32
            )

    def update(s, n):
        held = (prod_a, prod_b)[(s * BLOCKS + n) % 2]
        new = (xb, xa)[s % 2]
        cols = slice(n * NB, (n + 1) * NB)
        mean = level[:, cols] * (1.0 / K)
        sums = jnp.zeros((8, NB), jnp.float32)
        for m in range(K // EB):
            rows = slice(m * EB, (m + 1) * EB)
            each = jnp.concatenate([rate[rows, :]] * (NB // 128), axis=1)
            now = cur[rows, cols]
            now = now + step_source * now * (held[rows, :] - each * mean)
            cur[rows, cols] = now
            if s + 1 < SRC_STEPS:
                new[rows, cols] = now.astype(jnp.bfloat16)
                sums = sums + jnp.sum(now.reshape(EB // 8, 8, NB), axis=0)
        if s + 1 < SRC_STEPS:
            level[:, cols] = jnp.sum(sums, axis=0, keepdims=True)

    turns = [(s, n) for s in range(SRC_STEPS) for n in range(BLOCKS)]
    for i, turn in enumerate(turns):
        multiply(*turn)
        if i > 0:
            update(*turns[i - 1])
    update(*turns[-1])
    for j in range(RUN):
        base = flat[pl.ds(j, K, stride=RUN), :]
        cols = slice(j * 128, (j + 1) * 128)
        gain = (cur[:, cols] - base).astype(jnp.bfloat16)
        xb[:, cols] = gain
        if j < FIRST:
            flat_first[pl.ds(j, K, stride=FIRST), :] = gain.astype(jnp.float32)
        else:
            flat_rest[pl.ds(j - FIRST, K, stride=REST), :] = gain.astype(jnp.float32)
    parts = []
    for n in range(BLOCKS):
        both = stress[n] + jnp.dot(
            coef, xb[:, n * NB:(n + 1) * NB], preferred_element_type=jnp.float32
        )
        rows = [both[c:c + 1] + both[3 + c:4 + c] + both[6 + c:7 + c] for c in range(3)]
        parts.append(jnp.concatenate(rows, axis=0) * (1.0 / K))
    pieces = []
    for c in range(3):
        rows = [parts[j * 128 // NB][c:c + 1, j * 128 % NB:j * 128 % NB + 128] for j in range(RUN)]
        whole = jnp.concatenate(rows + [jnp.zeros((8 - RUN, 128), jnp.float32)], axis=0)
        high = whole.astype(jnp.bfloat16).astype(jnp.float32)
        pieces += [high, whole - high]
    shared = jnp.concatenate(pieces, axis=0).astype(jnp.bfloat16)

    def narrow(o, carry):
        gain = flat_first[pl.ds(o * FIRST_ROWS, FIRST_ROWS), :].astype(jnp.bfloat16)
        first_ref[o, 0:FIRST_ROWS, :] = gain
        first_ref[o, FIRST_ROWS:FIRST_ROWS + 8 * PIECES, :] = shared
        rows = LOCAL * REST
        rest_ref[o] = flat_rest[pl.ds(o * rows, rows), :].astype(jnp.bfloat16)
        for copy in give(o):
            copy.start()
        return carry

    def settle(o, carry):
        for copy in give(o):
            copy.wait()
        return carry

    lax.fori_loop(0, OWNERS, narrow, 0)
    lax.fori_loop(0, OWNERS, settle, 0)


def sources(received, quad_matrix, rates, coef, points_list):
    points = RUN * 128
    vmem = pl.BlockSpec(memory_space=pltpu.VMEM)
    hbm = pl.BlockSpec(memory_space=pltpu.HBM)
    return pl.pallas_call(
        source_kernel,
        in_specs=[vmem, hbm, vmem, vmem, hbm],
        out_specs=[hbm] * 2,
        out_shape=[
            pltpu.HBM((OWNERS, FIRST_ROWS + 8 * PIECES, 128), jnp.bfloat16),
            pltpu.HBM((OWNERS, LOCAL * REST, 128), jnp.bfloat16),
        ],
        scratch_shapes=[
            pltpu.VMEM((K, K), jnp.bfloat16),
            pltpu.VMEM((OWNERS, FIRST_ROWS + 8 * PIECES, 128), jnp.bfloat16),
            pltpu.VMEM((OWNERS, LOCAL * REST, 128), jnp.bfloat16),
            pltpu.VMEM((K, NB), jnp.float32),
            pltpu.VMEM((K, NB), jnp.float32),
            pltpu.VMEM((K * RUN, 128), jnp.float32),
            pltpu.VMEM((K, points), jnp.float32),
            pltpu.VMEM((K, points), jnp.bfloat16),
            pltpu.VMEM((K, points), jnp.bfloat16),
            pltpu.VMEM((K, 128), jnp.float32),
            pltpu.VMEM((1, points), jnp.float32),
            pltpu.VMEM((K * FIRST, 128), jnp.float32),
            pltpu.VMEM((K * REST, 128), jnp.float32),
            pltpu.SemaphoreType.DMA(()),
            pltpu.SemaphoreType.DMA((2, OWNERS)),
        ],
        compiler_params=pltpu.CompilerParams(vmem_limit_bytes=30 << 20),
        name="sources",
    )(in_vmem(received), in_hbm(quad_matrix), in_vmem(rates), in_vmem(coef), in_hbm(points_list))


def pick_kernel(first_ref, points_ref, out_ref):
    pieces = []
    for i in range(PIECES):
        at = FIRST_ROWS + 8 * i
        rows = first_ref[:, at:at + 8, :].astype(jnp.float32).reshape(OWNERS * 8, 128)
        pieces.append(rows.T.astype(jnp.bfloat16))
    table = jnp.concatenate(pieces, axis=0)
    slot = lax.broadcasted_iota(jnp.int32, (OWNERS * 8, 128), 0)
    within = lax.broadcasted_iota(jnp.int32, (128, 128), 0)
    weights = (0.5, 0.3, 0.2)
    for t in range(TILES):
        hots, lows = [], []
        for m in range(3):
            p = points_ref[m * TILES + t:m * TILES + t + 1, :]
            row = p >> 8
            col = p & 255
            hi = (((col >> 7) * GROUP + (row & (GROUP - 1))) << 3) + (row >> 4)
            hots.append(jnp.where(slot == hi, 1.0, 0.0).astype(jnp.bfloat16))
            lows.append(col & 127)
        hot = jnp.concatenate(hots, axis=1)
        found = jnp.dot(table, hot, preferred_element_type=jnp.float32)
        for c in range(3):
            both = found[2 * c * 128:(2 * c + 1) * 128] + found[(2 * c + 1) * 128:(2 * c + 2) * 128]
            acc = jnp.zeros((128, 128), jnp.float32)
            for m in range(3):
                acc = acc + jnp.where(
                    within == lows[m], both[:, m * 128:(m + 1) * 128] * weights[m], 0.0
                )
            out_ref[c, t:t + 1, :] = jnp.sum(acc, axis=0, keepdims=True)


def pick(first, points):
    vmem = pl.BlockSpec(memory_space=pltpu.VMEM)
    return pl.pallas_call(
        pick_kernel,
        in_specs=[vmem] * 2,
        out_specs=vmem,
        out_shape=pltpu.VMEM((3, TILES, 128), jnp.float32),
        compiler_params=pltpu.CompilerParams(vmem_limit_bytes=10 << 20),
        name="pick",
    )(in_vmem(first), in_vmem(points))


def finish_kernel(
    first_ref, rest_ref, prop0_hbm, prop1_hbm, out_hbm,
    prop0, prop1, spread_first, spread_rest, out, sems, keep_sems,
):
    def keep(i):
        part = pl.ds(i * KB * ROWS, KB * ROWS)
        return [
            pltpu.make_async_copy(hbm.at[part], prop.at[part], keep_sems.at[h, i])
            for h, (prop, hbm) in enumerate(((prop0, prop0_hbm), (prop1, prop1_hbm)))
        ]

    def load(i, carry):
        for copy in keep(i):
            copy.start()
        return carry

    lax.fori_loop(0, LOCAL // KB, load, 0)

    def spread(g, carry):
        for h in range(2):
            o = h * GROUP + g
            spread_first[h, pl.ds(g, FIRST_ROWS, stride=GROUP), :] = first_ref[
                o, 0:FIRST_ROWS, :
            ].astype(jnp.float32)
            spread_rest[h, pl.ds(g, LOCAL * REST, stride=GROUP), :] = rest_ref[o].astype(
                jnp.float32
            )
        return carry

    lax.fori_loop(0, GROUP, spread, 0)
    cut = FIRST * GROUP

    def copy(i):
        part = pl.ds(i * KB, KB)
        return pltpu.make_async_copy(out.at[part], out_hbm.at[part], sems.at[i])

    def add(i, carry):
        for copy_in in keep(i):
            copy_in.wait()
        for kk in range(KB):
            k = i * KB + kk
            for h, prop in enumerate((prop0, prop1)):
                cols = slice(h * 128, (h + 1) * 128)
                out[k, 0:cut, cols] = (
                    prop[pl.ds(k * ROWS, cut), :] + spread_first[h, pl.ds(k * cut, cut), :]
                )
                tail = ROWS - cut
                out[k, cut:ROWS, cols] = (
                    prop[pl.ds(k * ROWS + cut, tail), :] + spread_rest[h, pl.ds(k * tail, tail), :]
                )
        copy(i).start()
        return carry

    lax.fori_loop(0, LOCAL // KB, add, 0)

    def settle(i, carry):
        copy(i).wait()
        return carry

    lax.fori_loop(0, LOCAL // KB, settle, 0)


def finish(first, rest, prop0, prop1):
    vmem = pl.BlockSpec(memory_space=pltpu.VMEM)
    hbm = pl.BlockSpec(memory_space=pltpu.HBM)
    shape = (LOCAL, ROWS, 256)
    return pl.pallas_call(
        finish_kernel,
        in_specs=[vmem, vmem, hbm, hbm],
        out_specs=hbm,
        out_shape=pltpu.HBM(shape, jnp.float32),
        scratch_shapes=[
            pltpu.VMEM((LOCAL * ROWS, 128), jnp.float32),
            pltpu.VMEM((LOCAL * ROWS, 128), jnp.float32),
            pltpu.VMEM((2, LOCAL * FIRST * GROUP, 128), jnp.float32),
            pltpu.VMEM((2, LOCAL * REST * GROUP, 128), jnp.float32),
            pltpu.VMEM(shape, jnp.float32),
            pltpu.SemaphoreType.DMA((LOCAL // KB,)),
            pltpu.SemaphoreType.DMA((2, LOCAL // KB)),
        ],
        compiler_params=pltpu.CompilerParams(vmem_limit_bytes=16 << 20),
        name="finish",
    )(in_vmem(first), in_vmem(rest), in_hbm(prop0), in_hbm(prop1))


def from_neighbours(low, high, axis):
    count = lax.axis_size(axis)
    ends = count - 1
    before = lax.ppermute(high, axis, [(i, (i + 1) % count) for i in range(ends)])
    after = lax.ppermute(low, axis, [((i + 1) % count, i) for i in range(ends)])
    return before, after


def diff_rows(extended):
    return 0.5 * (extended[2:, 1:-1] - extended[:-2, 1:-1])


def diff_cols(extended):
    return 0.5 * (extended[1:-1, 2:] - extended[1:-1, :-2])


def shallow_water(wide_state, wide_stress, tile_cols, tile_rows):
    groups = lax.axis_size("comp")
    wide_cols = wide_state.shape[2]
    global_col = (
        lax.axis_index("comp") * tile_cols - MARGIN + jnp.arange(wide_cols, dtype=jnp.int32)
    )
    within = (global_col >= 0) & (global_col < tile_cols * groups)
    inside = within.astype(jnp.float32)[None, :]
    rimmed = jnp.pad(jnp.where(within, wide_stress, 0.0), ((0, 0), (1, 1), (1, 1)))
    force_down = -(diff_rows(rimmed[0]) + diff_cols(rimmed[1]))
    force_across = -(diff_rows(rimmed[1]) + diff_cols(rimmed[2]))
    height, flow_down, flow_across = wide_state
    for _ in range(SW_STEPS):
        down_ext = jnp.pad(flow_down, 1)
        across_ext = jnp.pad(flow_across, 1)
        height = (height - wave_speed * (diff_rows(down_ext) + diff_cols(across_ext))) * inside
        height_ext = jnp.pad(height, 1)
        flow_down = (
            (1.0 - friction) * flow_down
            - wave_speed * diff_rows(height_ext)
            + forcing_gain * force_down
        ) * inside
        flow_across = (
            (1.0 - friction) * flow_across
            - wave_speed * diff_cols(height_ext)
            + forcing_gain * force_across
        ) * inside
    stacked = jnp.stack([height, flow_down, flow_across])
    row_start = lax.axis_index("band") * tile_rows
    own_rows = lax.dynamic_slice_in_dim(stacked, row_start, tile_rows, 1)
    return own_rows[:, :, MARGIN:MARGIN + tile_cols]


def window(spectrum, wet_mask, quad_matrix, dissipation, circulation, source_points):
    offset = lax.axis_index("comp") * LOCAL
    speed_east, speed_north, _ = component_tables(offset, LOCAL)
    speeds = jnp.stack([speed_east, speed_north])
    wetness = wet_mask.astype(jnp.float32)[None]
    low = jnp.concatenate([spectrum[:, :HALO], wetness[:, :HALO]], axis=0)
    high = jnp.concatenate([spectrum[:, -HALO:], wetness[:, -HALO:]], axis=0)
    top, bottom = from_neighbours(low, high, "band")
    prop0, prop1, sent = propagate(speeds, spectrum, top, bottom, wetness[0])
    received = lax.all_to_all(sent, "comp", 0, 0, tiled=True)

    tile_rows = circulation.shape[1]
    tile_cols = circulation.shape[2]
    both = jnp.concatenate([circulation, source_points.astype(jnp.float32)], axis=0)
    before, after = from_neighbours(both[:, :, :MARGIN], both[:, :, -MARGIN:], "comp")
    wide = jnp.concatenate([before, both, after], axis=2)
    left_points = before[3:].astype(jnp.int32).reshape(3, 1, 128)
    right_points = after[3:].astype(jnp.int32).reshape(3, 1, 128)
    points = jnp.concatenate([source_points, left_points, right_points], axis=1)
    points = points.reshape(3 * TILES, 128)

    full_coef = component_tables(0, K)[2]
    coef_high = full_coef.astype(jnp.bfloat16).astype(jnp.float32)
    coef_mid = (full_coef - coef_high).astype(jnp.bfloat16).astype(jnp.float32)
    coef_low = full_coef - coef_high - coef_mid
    spare = jnp.zeros((7, K), jnp.float32)
    coef = jnp.concatenate([coef_high, coef_mid, coef_low, spare]).astype(jnp.bfloat16)
    first, rest = sources(
        received.reshape(K * RUN, 128), quad_matrix, dissipation.reshape(K // 128, 128), coef, points
    )
    first = lax.all_to_all(first, "comp", 0, 0, tiled=True)
    rest = lax.all_to_all(rest, "comp", 0, 0, tiled=True)
    cells = pick(first, points)
    own = cells[:, :tile_rows]
    left = cells[:, tile_rows].reshape(3, tile_rows, MARGIN)
    right = cells[:, tile_rows + 1].reshape(3, tile_rows, MARGIN)
    wide_cells = jnp.concatenate([left, own, right], axis=2)
    everything = lax.all_gather(
        jnp.concatenate([wide[:3], wide_cells], axis=0), "band", axis=1, tiled=True
    )
    circulation_out = shallow_water(everything[:3], everything[3:], tile_cols, tile_rows)
    spectrum_out = finish(first, rest, prop0, prop1)
    return spectrum_out, circulation_out


def solution(mesh):
    in_specs = (
        P("comp", "band", None),
        P("band", None),
        P(),
        P(),
        P(None, "band", "comp"),
        P(None, "band", "comp"),
    )
    out_specs = (P("comp", "band", None), P(None, "band", "comp"))
    return jax.shard_map(window, mesh=mesh, in_specs=in_specs, out_specs=out_specs, check_vma=False)
```

```python
import math

import jax
import jax.numpy as jnp
from jax import lax
from jax.experimental import pallas as pl
from jax.experimental.pallas import tpu as pltpu
from jax.sharding import PartitionSpec as P


NF = 36
ND = 32
K = NF * ND
SUBSTEPS = 4
SRC_STEPS = 4
SW_STEPS = 8

step_source = 0.1
wave_speed = 0.35
friction = 0.05
forcing_gain = 0.15

LOCAL = 36
ROWS = 96
OWNERS = 32
GROUP = 16
RUN = 6
HALO = 4
KB = 4
PAIR = KB
MARGIN = 2 * SW_STEPS
TILES = 10


def component_tables(offset, local_count):
    indices = offset + jnp.arange(local_count, dtype=jnp.int32)
    frequency = (indices // ND).astype(jnp.float32)
    heading = (indices % ND).astype(jnp.float32)
    heading_angle = 2.0 * math.pi * (heading + 0.5) / ND
    fraction = (frequency + 0.5) / NF
    group_speed = 0.25 + 0.4 * fraction
    wave_ratio = 0.5 + 0.5 * fraction
    cosine = jnp.cos(heading_angle)
    sine_part = jnp.sin(heading_angle)
    speed_east = group_speed * cosine
    speed_north = group_speed * sine_part
    stress_coef = jnp.stack(
        [
            wave_ratio * (1.0 + cosine * cosine) - 0.5,
            wave_ratio * sine_part * cosine,
            wave_ratio * (1.0 + sine_part * sine_part) - 0.5,
        ]
    )
    return speed_east, speed_north, stress_coef


def in_hbm(array):
    return pltpu.with_memory_space_constraint(array, pltpu.HBM)


def in_vmem(array):
    return pltpu.with_memory_space_constraint(array, pltpu.VMEM)


def propagate_kernel(
    speeds, spec_hbm, top_ref, bot_ref, wet_ref, prop0_hbm, prop1_hbm, sent_hbm,
    spec_ref, load_sems, prop0, prop1, sent_ref, wet, left_a, right_a, left_b, right_b, keep_sems, sent_sems,
):
    ext = ROWS + 2 * HALO

    def keep(i):
        part = pl.ds(i * KB * ROWS, KB * ROWS)
        return [
            pltpu.make_async_copy(prop.at[part], hbm.at[part], keep_sems.at[h, i])
            for h, (prop, hbm) in enumerate(((prop0, prop0_hbm), (prop1, prop1_hbm)))
        ]

    def give(i):
        rows = pl.ds(i * KB * RUN, KB * RUN)
        return pltpu.make_async_copy(sent_ref.at[i], sent_hbm.at[:, rows, :], sent_sems.at[i])

    def regroup(i):
        for h, prop in enumerate((prop0, prop1)):
            for g in range(GROUP):
                picked = prop[pl.ds(i * KB * ROWS + g, KB * RUN, stride=GROUP), :]
                sent_ref[i, h * GROUP + g] = picked.astype(jnp.bfloat16)

    def load(i):
        part = pl.ds(i * KB, KB)
        return pltpu.make_async_copy(spec_hbm.at[part], spec_ref.at[part], load_sems.at[i])

    def start_load(i, carry):
        load(i).start()
        return carry

    lax.fori_loop(0, LOCAL // KB, start_load, 0)
    wet[0:ROWS, :] = wet_ref[...]
    wet[ROWS:ROWS + HALO, :] = bot_ref[LOCAL]
    wet[ROWS + HALO:ext, :] = top_ref[LOCAL]
    lane = lax.broadcasted_iota(jnp.int32, (ext, 128), 1)
    fields = [[(left_a.at[q], right_a.at[q]), (left_b.at[q], right_b.at[q])] for q in range(PAIR)]

    def advance(first, north):
        edge = 0 if north else 127
        turn = 1 if north else 127
        ahead, a, b, c, side = [], [], [], [], []
        for q in range(PAIR):
            ax = speeds[0, first + q]
            ahead.append(jnp.where(ax >= 0.0, 7, 9))
            a.append(jnp.abs(ax))
            b.append(jnp.abs(speeds[1, first + q]))
            c.append(1.0 - a[q] - b[q])
            side.append(jnp.where(lane == edge, 0.0, b[q]))
        for s in range(SUBSTEPS):
            for q in range(PAIR):
                left_ref, right_ref = fields[q][s % 2]
                left, right = left_ref[8:8 + ext, :], right_ref[8:8 + ext, :]
                ul = left_ref[pl.ds(ahead[q], ext), :]
                ur = right_ref[pl.ds(ahead[q], ext), :]
                rl = pltpu.roll(left, turn, 1)
                rr = pltpu.roll(right, turn, 1)
                if north:
                    across_l = side[q] * rl
                    across_r = b[q] * jnp.where(lane == 0, rl, rr)
                else:
                    across_l = b[q] * jnp.where(lane == 127, rr, rl)
                    across_r = side[q] * rr
                left = wet[:, :128] * (c[q] * left + a[q] * ul + across_l)
                right = wet[:, 128:] * (c[q] * right + a[q] * ur + across_r)
                if s + 1 < SUBSTEPS:
                    for ref, value in zip(fields[q][(s + 1) % 2], (left, right)):
                        ref[8:8 + ext, :] = value
                        ref[7:8, :] = value[ext - 1:]
                        ref[8 + ext:9 + ext, :] = value[0:1]
                else:
                    prop0[pl.ds((first + q) * ROWS, ROWS), :] = left[:ROWS]
                    prop1[pl.ds((first + q) * ROWS, ROWS), :] = right[:ROWS]

    def some(i, carry):
        first = i * PAIR
        for q in range(PAIR):
            k = first + q
            for h, ref in enumerate(fields[q][0]):
                cols = slice(h * 128, (h + 1) * 128)
                top = top_ref[k, :, cols]
                ref[8:8 + ROWS, :] = spec_ref[k, :, cols]
                ref[8 + ROWS:8 + ROWS + HALO, :] = bot_ref[k, :, cols]
                ref[8 + ROWS + HALO:8 + ext, :] = top
                ref[7:8, :] = top[HALO - 1:]
                ref[8 + ext:9 + ext, :] = spec_ref[k, 0:1, cols]
        ay = speeds[1, first]

        @pl.when(ay >= 0.0)
        def _():
            advance(first, True)

        @pl.when(ay < 0.0)
        def _():
            advance(first, False)

        return carry

    def block(i, carry):
        load(i).wait()
        some(i, 0)
        regroup(i)
        give(i).start()
        for copy in keep(i):
            copy.start()
        return carry

    count = LOCAL // KB
    lax.fori_loop(0, count, block, 0)

    def settle(i, carry):
        for copy in keep(i):
            copy.wait()
        give(i).wait()
        return carry

    lax.fori_loop(0, count, settle, 0)


def propagate(speeds, spectrum, top, bottom, wetness):
    cols = spectrum.shape[2]
    ext = ROWS + 2 * HALO
    vmem = pl.BlockSpec(memory_space=pltpu.VMEM)
    hbm = pl.BlockSpec(memory_space=pltpu.HBM)
    return pl.pallas_call(
        propagate_kernel,
        in_specs=[pl.BlockSpec(memory_space=pltpu.SMEM), hbm] + [vmem] * 3,
        out_specs=[hbm] * 3,
        out_shape=[
            pltpu.HBM((LOCAL * ROWS, 128), jnp.float32),
            pltpu.HBM((LOCAL * ROWS, 128), jnp.float32),
            pltpu.HBM((OWNERS, LOCAL * RUN, 128), jnp.bfloat16),
        ],
        scratch_shapes=[
            pltpu.VMEM((LOCAL, ROWS, cols), jnp.float32),
            pltpu.SemaphoreType.DMA((LOCAL // KB,)),
            pltpu.VMEM((LOCAL * ROWS, 128), jnp.float32),
            pltpu.VMEM((LOCAL * ROWS, 128), jnp.float32),
            pltpu.VMEM((LOCAL // KB, OWNERS, KB * RUN, 128), jnp.bfloat16),
            pltpu.VMEM((ext, cols), jnp.float32),
        ]
        + [pltpu.VMEM((PAIR, ext + 16, 128), jnp.float32)] * 4
        + [pltpu.SemaphoreType.DMA((2, LOCAL // KB)), pltpu.SemaphoreType.DMA((LOCAL // KB,))],
        compiler_params=pltpu.CompilerParams(vmem_limit_bytes=16 << 20),
        name="propagate",
    )(speeds, in_hbm(spectrum), *map(in_vmem, (top, bottom, wetness)))


MB = 576
EB = 64
NB = 256
OWN_ROWS = RUN * LOCAL
PIECES = 6
BLOCKS = RUN * 128 // NB
BACK_ROWS = OWN_ROWS + 8 * PIECES


def source_kernel(
    recv_ref, quad_hbm, diss_ref, coef_ref, points_ref, back_hbm,
    quad_ref, back_ref, prod_a, prod_b, flat, cur, xa, xb, rate, level, quad_sems, out_sem,
):
    halves = K // MB

    def fetch(m):
        part = pl.ds(m * MB, MB)
        return pltpu.make_async_copy(quad_hbm.at[part], quad_ref.at[part], quad_sems.at[m])

    for m in range(halves):
        fetch(m).start()

    def widen(i, carry):
        flat[pl.ds(i * K, K), :] = recv_ref[pl.ds(i * K, K), :].astype(jnp.float32)
        return carry

    lax.fori_loop(0, RUN, widen, 0)
    for i in range(K // 128):
        rate[i * 128:(i + 1) * 128, :] = jnp.broadcast_to(diss_ref[i:i + 1, :], (128, 128)).T
    coef = coef_ref[...]
    each_block = NB // 128
    stress = []
    rows_of = [[], [], []]

    def prepare(n):
        for j in range(n * each_block, (n + 1) * each_block):
            base = flat[pl.ds(j, K, stride=RUN), :]
            cols = slice(j * 128, (j + 1) * 128)
            cur[:, cols] = base
            xa[:, cols] = base.astype(jnp.bfloat16)
            level[:, cols] = jnp.sum(base, axis=0, keepdims=True)
        stress.append(
            jnp.dot(coef, xa[:, n * NB:(n + 1) * NB], preferred_element_type=jnp.float32)
        )

    def multiply(s, n):
        held = (prod_a, prod_b)[(s * BLOCKS + n) % 2]
        old = (xa, xb)[s % 2]
        for m in range(halves):
            rows = slice(m * MB, (m + 1) * MB)
            held[rows, :] = jnp.dot(
                quad_ref[rows, :], old[:, n * NB:(n + 1) * NB], preferred_element_type=jnp.float32
            )

    def update(s, n):
        held = (prod_a, prod_b)[(s * BLOCKS + n) % 2]
        new = (xb, xa)[s % 2]
        cols = slice(n * NB, (n + 1) * NB)
        mean = level[:, cols] * (1.0 / K)
        sums = jnp.zeros((8, NB), jnp.float32)
        for m in range(K // EB):
            rows = slice(m * EB, (m + 1) * EB)
            each = jnp.concatenate([rate[rows, :]] * each_block, axis=1)
            now = cur[rows, cols]
            now = now + step_source * now * (held[rows, :] - each * mean)
            cur[rows, cols] = now
            if s + 1 < SRC_STEPS:
                new[rows, cols] = now.astype(jnp.bfloat16)
                sums = sums + jnp.sum(now.reshape(EB // 8, 8, NB), axis=0)
        if s + 1 < SRC_STEPS:
            level[:, cols] = jnp.sum(sums, axis=0, keepdims=True)

    def conclude(n):
        for j in range(n * each_block, (n + 1) * each_block):
            base = flat[pl.ds(j, K, stride=RUN), :]
            cols = slice(j * 128, (j + 1) * 128)
            gain = (cur[:, cols] - base).astype(jnp.bfloat16)
            xa[:, cols] = gain
            flat[pl.ds(j, K, stride=RUN), :] = gain.astype(jnp.float32)
        both = stress[n] + jnp.dot(
            coef, xa[:, n * NB:(n + 1) * NB], preferred_element_type=jnp.float32
        )
        for c in range(3):
            row = (both[c:c + 1] + both[3 + c:4 + c] + both[6 + c:7 + c]) * (1.0 / K)
            rows_of[c] += [row[:, i * 128:(i + 1) * 128] for i in range(each_block)]

    for m in range(halves):
        fetch(m).wait()
    prepare(0)
    turns = [(s, n) for s in range(SRC_STEPS) for n in range(BLOCKS)]
    for i, (s, n) in enumerate(turns):
        multiply(s, n)
        if s == 0 and n + 1 < BLOCKS:
            prepare(n + 1)
        if i > 0:
            update(*turns[i - 1])
        if s == SRC_STEPS - 1 and n > 0:
            conclude(n - 1)
    update(*turns[-1])
    conclude(BLOCKS - 1)
    pieces = []
    for c in range(3):
        whole = jnp.concatenate(rows_of[c] + [jnp.zeros((8 - RUN, 128), jnp.float32)], axis=0)
        high = whole.astype(jnp.bfloat16).astype(jnp.float32)
        pieces += [high, whole - high]
    shared = jnp.concatenate(pieces, axis=0).astype(jnp.bfloat16)

    def narrow(o, carry):
        back_ref[o, 0:OWN_ROWS, :] = flat[pl.ds(o * OWN_ROWS, OWN_ROWS), :].astype(jnp.bfloat16)
        back_ref[o, OWN_ROWS:BACK_ROWS, :] = shared
        pltpu.make_async_copy(back_ref.at[o], back_hbm.at[o], out_sem).start()
        return carry

    lax.fori_loop(0, OWNERS, narrow, 0)
    pltpu.make_async_copy(back_ref, back_hbm, out_sem).wait()


def sources(received, quad_matrix, rates, coef, points_list):
    points = RUN * 128
    vmem = pl.BlockSpec(memory_space=pltpu.VMEM)
    hbm = pl.BlockSpec(memory_space=pltpu.HBM)
    return pl.pallas_call(
        source_kernel,
        in_specs=[vmem, hbm, vmem, vmem, hbm],
        out_specs=hbm,
        out_shape=pltpu.HBM((OWNERS, BACK_ROWS, 128), jnp.bfloat16),
        scratch_shapes=[
            pltpu.VMEM((K, K), jnp.bfloat16),
            pltpu.VMEM((OWNERS, BACK_ROWS, 128), jnp.bfloat16),
            pltpu.VMEM((K, NB), jnp.float32),
            pltpu.VMEM((K, NB), jnp.float32),
            pltpu.VMEM((K * RUN, 128), jnp.float32),
            pltpu.VMEM((K, points), jnp.float32),
            pltpu.VMEM((K, points), jnp.bfloat16),
            pltpu.VMEM((K, points), jnp.bfloat16),
            pltpu.VMEM((K, 128), jnp.float32),
            pltpu.VMEM((1, points), jnp.float32),
            pltpu.SemaphoreType.DMA((K // MB,)),
            pltpu.SemaphoreType.DMA(()),
        ],
        compiler_params=pltpu.CompilerParams(vmem_limit_bytes=30 << 20),
        name="sources",
    )(in_vmem(received), in_hbm(quad_matrix), in_vmem(rates), in_vmem(coef), in_hbm(points_list))


def pick_kernel(back_ref, points_ref, out_ref):
    pieces = []
    for i in range(PIECES):
        at = OWN_ROWS + 8 * i
        rows = back_ref[:, at:at + 8, :].astype(jnp.float32).reshape(OWNERS * 8, 128)
        pieces.append(rows.T.astype(jnp.bfloat16))
    table = jnp.concatenate(pieces, axis=0)
    slot = lax.broadcasted_iota(jnp.int32, (OWNERS * 8, 128), 0)
    within = lax.broadcasted_iota(jnp.int32, (128, 128), 0)
    weights = (0.5, 0.3, 0.2)
    for t in range(TILES):
        hots, lows = [], []
        for m in range(3):
            p = points_ref[m * TILES + t:m * TILES + t + 1, :]
            row = p >> 8
            col = p & 255
            hi = (((col >> 7) * GROUP + (row & (GROUP - 1))) << 3) + (row >> 4)
            hots.append(jnp.where(slot == hi, 1.0, 0.0).astype(jnp.bfloat16))
            lows.append(col & 127)
        hot = jnp.concatenate(hots, axis=1)
        found = jnp.dot(table, hot, preferred_element_type=jnp.float32)
        for c in range(3):
            both = found[2 * c * 128:(2 * c + 1) * 128] + found[(2 * c + 1) * 128:(2 * c + 2) * 128]
            acc = jnp.zeros((128, 128), jnp.float32)
            for m in range(3):
                acc = acc + jnp.where(
                    within == lows[m], both[:, m * 128:(m + 1) * 128] * weights[m], 0.0
                )
            out_ref[c, t:t + 1, :] = jnp.sum(acc, axis=0, keepdims=True)


def pick(back, points):
    vmem = pl.BlockSpec(memory_space=pltpu.VMEM)
    return pl.pallas_call(
        pick_kernel,
        in_specs=[vmem] * 2,
        out_specs=vmem,
        out_shape=pltpu.VMEM((3, TILES, 128), jnp.float32),
        compiler_params=pltpu.CompilerParams(vmem_limit_bytes=10 << 20),
        name="pick",
    )(in_vmem(back), in_vmem(points))


def finish_kernel(
    back_ref, prop0_hbm, prop1_hbm, out_hbm, prop0, prop1, wide, out, sems, keep_sems,
):
    def keep(i):
        part = pl.ds(i * KB * ROWS, KB * ROWS)
        return [
            pltpu.make_async_copy(hbm.at[part], prop.at[part], keep_sems.at[h, i])
            for h, (prop, hbm) in enumerate(((prop0, prop0_hbm), (prop1, prop1_hbm)))
        ]

    def load(i, carry):
        for copy in keep(i):
            copy.start()
        return carry

    lax.fori_loop(0, LOCAL // KB, load, 0)

    def spread(g, carry):
        for h in range(2):
            gain = back_ref[h * GROUP + g, 0:OWN_ROWS, :].astype(jnp.float32)
            wide[h, pl.ds(g, OWN_ROWS, stride=GROUP), :] = gain
        return carry

    lax.fori_loop(0, GROUP, spread, 0)

    def copy(i):
        part = pl.ds(i * KB, KB)
        return pltpu.make_async_copy(out.at[part], out_hbm.at[part], sems.at[i])

    def add(i, carry):
        for copy_in in keep(i):
            copy_in.wait()
        for kk in range(KB):
            k = i * KB + kk
            for h, prop in enumerate((prop0, prop1)):
                rows = pl.ds(k * ROWS, ROWS)
                out[k, :, h * 128:(h + 1) * 128] = prop[rows, :] + wide[h, rows, :]
        copy(i).start()
        return carry

    lax.fori_loop(0, LOCAL // KB, add, 0)

    def settle(i, carry):
        copy(i).wait()
        return carry

    lax.fori_loop(0, LOCAL // KB, settle, 0)


def finish(back, prop0, prop1):
    vmem = pl.BlockSpec(memory_space=pltpu.VMEM)
    hbm = pl.BlockSpec(memory_space=pltpu.HBM)
    shape = (LOCAL, ROWS, 256)
    return pl.pallas_call(
        finish_kernel,
        in_specs=[vmem, hbm, hbm],
        out_specs=hbm,
        out_shape=pltpu.HBM(shape, jnp.float32),
        scratch_shapes=[
            pltpu.VMEM((LOCAL * ROWS, 128), jnp.float32),
            pltpu.VMEM((LOCAL * ROWS, 128), jnp.float32),
            pltpu.VMEM((2, LOCAL * ROWS, 128), jnp.float32),
            pltpu.VMEM(shape, jnp.float32),
            pltpu.SemaphoreType.DMA((LOCAL // KB,)),
            pltpu.SemaphoreType.DMA((2, LOCAL // KB)),
        ],
        compiler_params=pltpu.CompilerParams(vmem_limit_bytes=16 << 20),
        name="finish",
    )(in_vmem(back), in_hbm(prop0), in_hbm(prop1))


def from_neighbours(low, high, axis):
    count = lax.axis_size(axis)
    ends = count - 1
    before = lax.ppermute(high, axis, [(i, (i + 1) % count) for i in range(ends)])
    after = lax.ppermute(low, axis, [((i + 1) % count, i) for i in range(ends)])
    return before, after


WIDE = 256


def water_kernel(place, own_ref, one_ref, two_ref, three_ref, out_ref, whole, result):
    bands = 4
    tile = own_ref.shape[1]
    width = own_ref.shape[2]
    own_cols = width - 2 * MARGIN
    band = place[0]
    whole[...] = jnp.zeros_like(whole)
    for d, ref in enumerate((own_ref, one_ref, two_ref, three_ref)):
        row = pl.multiple_of((band ^ d) * tile, tile)
        whole[:, pl.ds(row, tile), 0:width] = ref[...]
    shape = (bands * tile, WIDE)
    lane = lax.broadcasted_iota(jnp.int32, shape, 1)
    line = lax.broadcasted_iota(jnp.int32, shape, 0)
    col = place[1] * own_cols - MARGIN + lane
    inside = (col >= 0) & (col < place[2]) & (lane < width)
    first = line == 0
    last = line == shape[0] - 1

    def dx(f):
        after = jnp.where(last, 0.0, pltpu.roll(f, shape[0] - 1, 0))
        before = jnp.where(first, 0.0, pltpu.roll(f, 1, 0))
        return 0.5 * (after - before)

    def dy(f):
        return 0.5 * (pltpu.roll(f, WIDE - 1, 1) - pltpu.roll(f, 1, 1))

    sxx, sxy, syy = (jnp.where(inside, whole[3 + c], 0.0) for c in range(3))
    force_down = -forcing_gain * (dx(sxx) + dy(sxy))
    force_across = -forcing_gain * (dx(sxy) + dy(syy))
    height, down, across = (whole[c] for c in range(3))
    for _ in range(SW_STEPS):
        height = jnp.where(inside, height - wave_speed * (dx(down) + dy(across)), 0.0)
        down = jnp.where(
            inside, (1.0 - friction) * down - wave_speed * dx(height) + force_down, 0.0
        )
        across = jnp.where(
            inside, (1.0 - friction) * across - wave_speed * dy(height) + force_across, 0.0
        )
    for c, value in enumerate((height, down, across)):
        result[c] = pltpu.roll(value, WIDE - MARGIN, 1)[:, :own_cols]
        out_ref[c] = result[c, pl.ds(pl.multiple_of(band * tile, tile), tile), :]


def shallow_water(place, tiles):
    vmem = pl.BlockSpec(memory_space=pltpu.VMEM)
    fields, rows, width = tiles[0].shape
    own_cols = width - 2 * MARGIN
    return pl.pallas_call(
        water_kernel,
        in_specs=[pl.BlockSpec(memory_space=pltpu.SMEM)] + [vmem] * 4,
        out_specs=vmem,
        out_shape=jax.ShapeDtypeStruct((3, rows, own_cols), jnp.float32),
        scratch_shapes=[
            pltpu.VMEM((fields, 4 * rows, WIDE), jnp.float32),
            pltpu.VMEM((3, 4 * rows, own_cols), jnp.float32),
        ],
        compiler_params=pltpu.CompilerParams(vmem_limit_bytes=4 << 20),
        name="water",
    )(place, *map(in_vmem, tiles))


def window(spectrum, wet_mask, quad_matrix, dissipation, circulation, source_points):
    offset = lax.axis_index("comp") * LOCAL
    speed_east, speed_north, _ = component_tables(offset, LOCAL)
    speeds = jnp.stack([speed_east, speed_north])
    wetness = wet_mask.astype(jnp.float32)[None]
    low = jnp.concatenate([spectrum[:, :HALO], wetness[:, :HALO]], axis=0)
    high = jnp.concatenate([spectrum[:, -HALO:], wetness[:, -HALO:]], axis=0)
    top, bottom = from_neighbours(low, high, "band")
    prop0, prop1, sent = propagate(speeds, spectrum, top, bottom, wetness[0])
    received = lax.all_to_all(sent, "comp", 0, 0, tiled=True)

    tile_rows = circulation.shape[1]
    tile_cols = circulation.shape[2]
    both = jnp.concatenate([circulation, source_points.astype(jnp.float32)], axis=0)
    before, after = from_neighbours(both[:, :, :MARGIN], both[:, :, -MARGIN:], "comp")
    wide = jnp.concatenate([before, both, after], axis=2)
    left_points = before[3:].astype(jnp.int32).reshape(3, 1, 128)
    right_points = after[3:].astype(jnp.int32).reshape(3, 1, 128)
    points = jnp.concatenate([source_points, left_points, right_points], axis=1)
    points = points.reshape(3 * TILES, 128)

    full_coef = component_tables(0, K)[2]
    coef_high = full_coef.astype(jnp.bfloat16).astype(jnp.float32)
    coef_mid = (full_coef - coef_high).astype(jnp.bfloat16).astype(jnp.float32)
    coef_low = full_coef - coef_high - coef_mid
    spare = jnp.zeros((7, K), jnp.float32)
    coef = jnp.concatenate([coef_high, coef_mid, coef_low, spare]).astype(jnp.bfloat16)
    back = sources(
        received.reshape(K * RUN, 128), quad_matrix, dissipation.reshape(K // 128, 128), coef, points
    )
    back = lax.all_to_all(back, "comp", 0, 0, tiled=True)
    cells = pick(back, points)
    own = cells[:, :tile_rows]
    left = cells[:, tile_rows].reshape(3, tile_rows, MARGIN)
    right = cells[:, tile_rows + 1].reshape(3, tile_rows, MARGIN)
    wide_cells = jnp.concatenate([left, own, right], axis=2)
    tile = jnp.concatenate([wide[:3], wide_cells], axis=0)
    bands = lax.axis_size("band")
    tiles = [tile]
    for d in range(1, bands):
        tiles.append(lax.ppermute(tile, "band", [(i, i ^ d) for i in range(bands)]))
    spectrum_out = finish(back, prop0, prop1)
    place = jnp.stack(
        [lax.axis_index("band"), lax.axis_index("comp"), tile_cols * lax.axis_size("comp")]
    )
    circulation_out = shallow_water(place.astype(jnp.int32), tiles)
    return spectrum_out, circulation_out


def solution(mesh):
    in_specs = (
        P("comp", "band", None),
        P("band", None),
        P(),
        P(),
        P(None, "band", "comp"),
        P(None, "band", "comp"),
    )
    out_specs = (P("comp", "band", None), P(None, "band", "comp"))
    return jax.shard_map(window, mesh=mesh, in_specs=in_specs, out_specs=out_specs, check_vma=False)
```

```python
import math

import jax
import jax.numpy as jnp
from jax import lax
from jax.experimental import pallas as pl
from jax.experimental.pallas import tpu as pltpu
from jax.sharding import PartitionSpec as P


NF = 36
ND = 32
K = NF * ND
SUBSTEPS = 4
SRC_STEPS = 4
SW_STEPS = 8

step_source = 0.1
wave_speed = 0.35
friction = 0.05
forcing_gain = 0.15

LOCAL = 36
ROWS = 96
OWNERS = 32
GROUP = 16
RUN = 6
HALO = 4
KB = 4
PAIR = KB
MARGIN = 2 * SW_STEPS
TILES = 10


def component_tables(offset, local_count):
    indices = offset + jnp.arange(local_count, dtype=jnp.int32)
    frequency = (indices // ND).astype(jnp.float32)
    heading = (indices % ND).astype(jnp.float32)
    heading_angle = 2.0 * math.pi * (heading + 0.5) / ND
    fraction = (frequency + 0.5) / NF
    group_speed = 0.25 + 0.4 * fraction
    wave_ratio = 0.5 + 0.5 * fraction
    cosine = jnp.cos(heading_angle)
    sine_part = jnp.sin(heading_angle)
    speed_east = group_speed * cosine
    speed_north = group_speed * sine_part
    stress_coef = jnp.stack(
        [
            wave_ratio * (1.0 + cosine * cosine) - 0.5,
            wave_ratio * sine_part * cosine,
            wave_ratio * (1.0 + sine_part * sine_part) - 0.5,
        ]
    )
    return speed_east, speed_north, stress_coef


def in_hbm(array):
    return pltpu.with_memory_space_constraint(array, pltpu.HBM)


def in_vmem(array):
    return pltpu.with_memory_space_constraint(array, pltpu.VMEM)


def propagate_kernel(
    speeds, spec_hbm, top_ref, bot_ref, wet_ref, prop0_hbm, prop1_hbm, sent_hbm,
    spec_ref, load_sems, prop0, prop1, sent_ref, wet, left_a, right_a, left_b, right_b, keep_sems, sent_sems,
):
    ext = ROWS + 2 * HALO

    def keep(i):
        part = pl.ds(i * KB * ROWS, KB * ROWS)
        return [
            pltpu.make_async_copy(prop.at[part], hbm.at[part], keep_sems.at[h, i])
            for h, (prop, hbm) in enumerate(((prop0, prop0_hbm), (prop1, prop1_hbm)))
        ]

    def give(i):
        rows = pl.ds(i * KB * RUN, KB * RUN)
        return pltpu.make_async_copy(sent_ref.at[i], sent_hbm.at[:, rows, :], sent_sems.at[i])

    def regroup(i):
        for h, prop in enumerate((prop0, prop1)):
            for g in range(GROUP):
                picked = prop[pl.ds(i * KB * ROWS + g, KB * RUN, stride=GROUP), :]
                sent_ref[i, h * GROUP + g] = picked.astype(jnp.bfloat16)

    def load(i):
        part = pl.ds(i * KB, KB)
        return pltpu.make_async_copy(spec_hbm.at[part], spec_ref.at[part], load_sems.at[i])

    def start_load(i, carry):
        load(i).start()
        return carry

    lax.fori_loop(0, LOCAL // KB, start_load, 0)
    wet[0:ROWS, :] = wet_ref[...]
    wet[ROWS:ROWS + HALO, :] = bot_ref[LOCAL]
    wet[ROWS + HALO:ext, :] = top_ref[LOCAL]
    lane = lax.broadcasted_iota(jnp.int32, (ext, 128), 1)
    fields = [[(left_a.at[q], right_a.at[q]), (left_b.at[q], right_b.at[q])] for q in range(PAIR)]

    def advance(first, north):
        edge = 0 if north else 127
        turn = 1 if north else 127
        ahead, a, b, c, side = [], [], [], [], []
        for q in range(PAIR):
            ax = speeds[0, first + q]
            ahead.append(jnp.where(ax >= 0.0, 7, 9))
            a.append(jnp.abs(ax))
            b.append(jnp.abs(speeds[1, first + q]))
            c.append(1.0 - a[q] - b[q])
            side.append(jnp.where(lane == edge, 0.0, b[q]))
        for s in range(SUBSTEPS):
            for q in range(PAIR):
                left_ref, right_ref = fields[q][s % 2]
                left, right = left_ref[8:8 + ext, :], right_ref[8:8 + ext, :]
                ul = left_ref[pl.ds(ahead[q], ext), :]
                ur = right_ref[pl.ds(ahead[q], ext), :]
                rl = pltpu.roll(left, turn, 1)
                rr = pltpu.roll(right, turn, 1)
                if north:
                    across_l = side[q] * rl
                    across_r = b[q] * jnp.where(lane == 0, rl, rr)
                else:
                    across_l = b[q] * jnp.where(lane == 127, rr, rl)
                    across_r = side[q] * rr
                left = wet[:, :128] * (c[q] * left + a[q] * ul + across_l)
                right = wet[:, 128:] * (c[q] * right + a[q] * ur + across_r)
                if s + 1 < SUBSTEPS:
                    for ref, value in zip(fields[q][(s + 1) % 2], (left, right)):
                        ref[8:8 + ext, :] = value
                        ref[7:8, :] = value[ext - 1:]
                        ref[8 + ext:9 + ext, :] = value[0:1]
                else:
                    prop0[pl.ds((first + q) * ROWS, ROWS), :] = left[:ROWS]
                    prop1[pl.ds((first + q) * ROWS, ROWS), :] = right[:ROWS]

    def some(i, carry):
        first = i * PAIR
        for q in range(PAIR):
            k = first + q
            for h, ref in enumerate(fields[q][0]):
                cols = slice(h * 128, (h + 1) * 128)
                top = top_ref[k, :, cols]
                ref[8:8 + ROWS, :] = spec_ref[k, :, cols]
                ref[8 + ROWS:8 + ROWS + HALO, :] = bot_ref[k, :, cols]
                ref[8 + ROWS + HALO:8 + ext, :] = top
                ref[7:8, :] = top[HALO - 1:]
                ref[8 + ext:9 + ext, :] = spec_ref[k, 0:1, cols]
        ay = speeds[1, first]

        @pl.when(ay >= 0.0)
        def _():
            advance(first, True)

        @pl.when(ay < 0.0)
        def _():
            advance(first, False)

        return carry

    def block(i, carry):
        load(i).wait()
        some(i, 0)
        regroup(i)
        give(i).start()
        for copy in keep(i):
            copy.start()
        return carry

    count = LOCAL // KB
    lax.fori_loop(0, count, block, 0)

    def settle(i, carry):
        for copy in keep(i):
            copy.wait()
        give(i).wait()
        return carry

    lax.fori_loop(0, count, settle, 0)


def propagate(speeds, spectrum, top, bottom, wetness):
    cols = spectrum.shape[2]
    ext = ROWS + 2 * HALO
    vmem = pl.BlockSpec(memory_space=pltpu.VMEM)
    hbm = pl.BlockSpec(memory_space=pltpu.HBM)
    return pl.pallas_call(
        propagate_kernel,
        in_specs=[pl.BlockSpec(memory_space=pltpu.SMEM), hbm] + [vmem] * 3,
        out_specs=[hbm] * 3,
        out_shape=[
            pltpu.HBM((LOCAL * ROWS, 128), jnp.float32),
            pltpu.HBM((LOCAL * ROWS, 128), jnp.float32),
            pltpu.HBM((OWNERS, LOCAL * RUN, 128), jnp.bfloat16),
        ],
        scratch_shapes=[
            pltpu.VMEM((LOCAL, ROWS, cols), jnp.float32),
            pltpu.SemaphoreType.DMA((LOCAL // KB,)),
            pltpu.VMEM((LOCAL * ROWS, 128), jnp.float32),
            pltpu.VMEM((LOCAL * ROWS, 128), jnp.float32),
            pltpu.VMEM((LOCAL // KB, OWNERS, KB * RUN, 128), jnp.bfloat16),
            pltpu.VMEM((ext, cols), jnp.float32),
        ]
        + [pltpu.VMEM((PAIR, ext + 16, 128), jnp.float32)] * 4
        + [pltpu.SemaphoreType.DMA((2, LOCAL // KB)), pltpu.SemaphoreType.DMA((LOCAL // KB,))],
        compiler_params=pltpu.CompilerParams(vmem_limit_bytes=16 << 20),
        name="propagate",
    )(speeds, in_hbm(spectrum), *map(in_vmem, (top, bottom, wetness)))


MB = 576
EB = 64
NB = 256
OWN_ROWS = RUN * LOCAL
PIECES = 3
BLOCKS = RUN * 128 // NB
BACK_ROWS = OWN_ROWS + 8 * PIECES


def source_kernel(
    recv_ref, quad_hbm, diss_ref, coef_ref, points_ref, back_hbm,
    quad_ref, back_ref, prod_a, prod_b, flat, cur, xa, xb, rate, level, quad_sems, out_sem,
):
    halves = K // MB
    points = RUN * 128

    def fetch(m):
        part = pl.ds(m * MB, MB)
        return pltpu.make_async_copy(quad_hbm.at[part], quad_ref.at[part], quad_sems.at[m])

    for m in range(halves):
        fetch(m).start()

    def widen(i, carry):
        flat[pl.ds(i * K, K), :] = recv_ref[pl.ds(i * K, K), :].astype(jnp.float32)
        return carry

    lax.fori_loop(0, RUN, widen, 0)
    for i in range(K // 128):
        rate[i * 128:(i + 1) * 128, :] = jnp.broadcast_to(diss_ref[i:i + 1, :], (128, 128)).T
    coef = coef_ref[...]
    each_block = NB // 128
    stress = []
    rows_of = [[], [], []]

    def prepare(n):
        for j in range(n * each_block, (n + 1) * each_block):
            base = flat[pl.ds(j, K, stride=RUN), :]
            cols = slice(j * 128, (j + 1) * 128)
            cur[:, cols] = base
            xa[:, cols] = base.astype(jnp.bfloat16)
            level[:, cols] = jnp.sum(base, axis=0, keepdims=True)

    def multiply(s, n):
        held = (prod_a, prod_b)[(s * BLOCKS + n) % 2]
        old = (xa, xb)[s % 2]
        for m in range(halves):
            rows = slice(m * MB, (m + 1) * MB)
            held[rows, :] = jnp.dot(
                quad_ref[rows, :], old[:, n * NB:(n + 1) * NB], preferred_element_type=jnp.float32
            )

    def update(s, n):
        held = (prod_a, prod_b)[(s * BLOCKS + n) % 2]
        new = (xb, xa)[s % 2]
        cols = slice(n * NB, (n + 1) * NB)
        mean = level[:, cols] * (1.0 / K)
        sums = jnp.zeros((8, NB), jnp.float32)
        for m in range(K // EB):
            rows = slice(m * EB, (m + 1) * EB)
            each = jnp.concatenate([rate[rows, :]] * each_block, axis=1)
            now = cur[rows, cols]
            now = now + step_source * now * (held[rows, :] - each * mean)
            cur[rows, cols] = now
            if s + 1 < SRC_STEPS:
                new[rows, cols] = now.astype(jnp.bfloat16)
                sums = sums + jnp.sum(now.reshape(EB // 8, 8, NB), axis=0)
        if s + 1 < SRC_STEPS:
            level[:, cols] = jnp.sum(sums, axis=0, keepdims=True)

    def conclude(n):
        for j in range(n * each_block, (n + 1) * each_block):
            base = flat[pl.ds(j, K, stride=RUN), :]
            cols = slice(j * 128, (j + 1) * 128)
            gain = (cur[:, cols] - base).astype(jnp.bfloat16)
            xb[:, cols] = gain
            flat[pl.ds(j, K, stride=RUN), :] = gain.astype(jnp.float32)

    def weigh(n):
        both = stress[n] + jnp.dot(
            coef, xb[:, n * NB:(n + 1) * NB], preferred_element_type=jnp.float32
        )
        for c in range(3):
            row = (both[c:c + 1] + both[3 + c:4 + c] + both[6 + c:7 + c]) * (1.0 / K)
            rows_of[c] += [row[:, i * 128:(i + 1) * 128] for i in range(each_block)]

    for n in range(BLOCKS):
        prepare(n)
    for n in range(BLOCKS):
        stress.append(
            jnp.dot(coef, xa[:, n * NB:(n + 1) * NB], preferred_element_type=jnp.float32)
        )
    for m in range(halves):
        fetch(m).wait()
    turns = [(s, n) for s in range(SRC_STEPS) for n in range(BLOCKS)]
    for i, (s, n) in enumerate(turns):
        multiply(s, n)
        if i > 0:
            update(*turns[i - 1])
    update(*turns[-1])
    for n in range(BLOCKS):
        conclude(n)
    for n in range(BLOCKS):
        weigh(n)
    pieces = []
    for c in range(3):
        whole = jnp.concatenate(rows_of[c], axis=0)
        mean = jnp.sum(jnp.sum(whole, axis=0, keepdims=True), axis=1, keepdims=True)
        mean = jnp.broadcast_to(mean * (1.0 / points), (1, 128))
        high = mean.astype(jnp.bfloat16).astype(jnp.float32)
        low = (mean - high).astype(jnp.bfloat16).astype(jnp.float32)
        pieces += [whole - (high + low), high, low]
    shared = jnp.concatenate(pieces, axis=0).astype(jnp.bfloat16)

    def narrow(o, carry):
        back_ref[o, 0:OWN_ROWS, :] = flat[pl.ds(o * OWN_ROWS, OWN_ROWS), :].astype(jnp.bfloat16)
        back_ref[o, OWN_ROWS:BACK_ROWS, :] = shared
        pltpu.make_async_copy(back_ref.at[o], back_hbm.at[o], out_sem).start()
        return carry

    lax.fori_loop(0, OWNERS, narrow, 0)
    pltpu.make_async_copy(back_ref, back_hbm, out_sem).wait()


def sources(received, quad_matrix, rates, coef, points_list):
    points = RUN * 128
    vmem = pl.BlockSpec(memory_space=pltpu.VMEM)
    hbm = pl.BlockSpec(memory_space=pltpu.HBM)
    return pl.pallas_call(
        source_kernel,
        in_specs=[vmem, hbm, vmem, vmem, hbm],
        out_specs=hbm,
        out_shape=pltpu.HBM((OWNERS, BACK_ROWS, 128), jnp.bfloat16),
        scratch_shapes=[
            pltpu.VMEM((K, K), jnp.bfloat16),
            pltpu.VMEM((OWNERS, BACK_ROWS, 128), jnp.bfloat16),
            pltpu.VMEM((K, NB), jnp.float32),
            pltpu.VMEM((K, NB), jnp.float32),
            pltpu.VMEM((K * RUN, 128), jnp.float32),
            pltpu.VMEM((K, points), jnp.float32),
            pltpu.VMEM((K, points), jnp.bfloat16),
            pltpu.VMEM((K, points), jnp.bfloat16),
            pltpu.VMEM((K, 128), jnp.float32),
            pltpu.VMEM((1, points), jnp.float32),
            pltpu.SemaphoreType.DMA((K // MB,)),
            pltpu.SemaphoreType.DMA(()),
        ],
        compiler_params=pltpu.CompilerParams(vmem_limit_bytes=30 << 20),
        name="sources",
    )(in_vmem(received), in_hbm(quad_matrix), in_vmem(rates), in_vmem(coef), in_hbm(points_list))


def pick_kernel(back_ref, points_ref, out_ref):
    pieces = []
    for i in range(PIECES):
        at = OWN_ROWS + 8 * i
        rows = back_ref[:, at:at + 8, :].astype(jnp.float32).reshape(OWNERS * 8, 128)
        pieces.append(rows.T.astype(jnp.bfloat16))
    table = jnp.concatenate(pieces, axis=0)
    slot = lax.broadcasted_iota(jnp.int32, (OWNERS * 8, 128), 0)
    within = lax.broadcasted_iota(jnp.int32, (128, 128), 0)
    weights = (0.5, 0.3, 0.2)
    for t in range(TILES):
        hots, lows = [], []
        for m in range(3):
            p = points_ref[m * TILES + t:m * TILES + t + 1, :]
            row = p >> 8
            col = p & 255
            hi = (((col >> 7) * GROUP + (row & (GROUP - 1))) << 3) + (row >> 4)
            taken = (slot == hi) | ((slot | 1) == (hi | 7))
            hots.append(jnp.where(taken, 1.0, 0.0).astype(jnp.bfloat16))
            lows.append(col & 127)
        hot = jnp.concatenate(hots, axis=1)
        found = jnp.dot(table, hot, preferred_element_type=jnp.float32)
        for c in range(3):
            both = found[c * 128:(c + 1) * 128]
            acc = jnp.zeros((128, 128), jnp.float32)
            for m in range(3):
                acc = acc + jnp.where(
                    within == lows[m], both[:, m * 128:(m + 1) * 128] * weights[m], 0.0
                )
            out_ref[c, t:t + 1, :] = jnp.sum(acc, axis=0, keepdims=True)


def pick(back, points):
    vmem = pl.BlockSpec(memory_space=pltpu.VMEM)
    return pl.pallas_call(
        pick_kernel,
        in_specs=[vmem] * 2,
        out_specs=vmem,
        out_shape=pltpu.VMEM((3, TILES, 128), jnp.float32),
        compiler_params=pltpu.CompilerParams(vmem_limit_bytes=10 << 20),
        name="pick",
    )(in_vmem(back), in_vmem(points))


def finish_kernel(
    back_ref, prop0_hbm, prop1_hbm, out_hbm, prop0, prop1, wide, out, sems, keep_sems,
):
    def keep(i):
        part = pl.ds(i * KB * ROWS, KB * ROWS)
        return [
            pltpu.make_async_copy(hbm.at[part], prop.at[part], keep_sems.at[h, i])
            for h, (prop, hbm) in enumerate(((prop0, prop0_hbm), (prop1, prop1_hbm)))
        ]

    def load(i, carry):
        for copy in keep(i):
            copy.start()
        return carry

    lax.fori_loop(0, LOCAL // KB, load, 0)

    def spread(i):
        rows = pl.ds(pl.multiple_of(i * KB * RUN, 8), KB * RUN)
        for h in range(2):
            for g in range(GROUP):
                gain = back_ref[h * GROUP + g, rows, :].astype(jnp.float32)
                wide[h, pl.ds(g, KB * RUN, stride=GROUP), :] = gain

    def copy(i):
        part = pl.ds(i * KB, KB)
        return pltpu.make_async_copy(out.at[part], out_hbm.at[part], sems.at[i])

    def add(i, carry):
        for copy_in in keep(i):
            copy_in.wait()
        spread(i)
        for kk in range(KB):
            k = i * KB + kk
            for h, prop in enumerate((prop0, prop1)):
                rows = pl.ds(k * ROWS, ROWS)
                out[k, :, h * 128:(h + 1) * 128] = (
                    prop[rows, :] + wide[h, kk * ROWS:(kk + 1) * ROWS, :]
                )
        copy(i).start()
        return carry

    lax.fori_loop(0, LOCAL // KB, add, 0)

    def settle(i, carry):
        copy(i).wait()
        return carry

    lax.fori_loop(0, LOCAL // KB, settle, 0)


def finish(back, prop0, prop1):
    vmem = pl.BlockSpec(memory_space=pltpu.VMEM)
    hbm = pl.BlockSpec(memory_space=pltpu.HBM)
    shape = (LOCAL, ROWS, 256)
    return pl.pallas_call(
        finish_kernel,
        in_specs=[vmem, hbm, hbm],
        out_specs=hbm,
        out_shape=pltpu.HBM(shape, jnp.float32),
        scratch_shapes=[
            pltpu.VMEM((LOCAL * ROWS, 128), jnp.float32),
            pltpu.VMEM((LOCAL * ROWS, 128), jnp.float32),
            pltpu.VMEM((2, KB * ROWS, 128), jnp.float32),
            pltpu.VMEM(shape, jnp.float32),
            pltpu.SemaphoreType.DMA((LOCAL // KB,)),
            pltpu.SemaphoreType.DMA((2, LOCAL // KB)),
        ],
        compiler_params=pltpu.CompilerParams(vmem_limit_bytes=16 << 20),
        name="finish",
    )(in_vmem(back), in_hbm(prop0), in_hbm(prop1))


def from_neighbours(low, high, axis):
    count = lax.axis_size(axis)
    ends = count - 1
    before = lax.ppermute(high, axis, [(i, (i + 1) % count) for i in range(ends)])
    after = lax.ppermute(low, axis, [((i + 1) % count, i) for i in range(ends)])
    return before, after


WIDE = 256


def water_kernel(place, own_ref, one_ref, two_ref, three_ref, out_ref, whole, result):
    bands = 4
    tile = own_ref.shape[1]
    width = own_ref.shape[2]
    own_cols = width - 2 * MARGIN
    band = place[0]
    whole[...] = jnp.zeros_like(whole)
    for d, ref in enumerate((own_ref, one_ref, two_ref, three_ref)):
        row = pl.multiple_of((band ^ d) * tile, tile)
        whole[:, pl.ds(row, tile), 0:width] = ref[...]
    shape = (bands * tile, WIDE)
    lane = lax.broadcasted_iota(jnp.int32, shape, 1)
    line = lax.broadcasted_iota(jnp.int32, shape, 0)
    col = place[1] * own_cols - MARGIN + lane
    inside = (col >= 0) & (col < place[2]) & (lane < width)
    first = line == 0
    last = line == shape[0] - 1

    def dx(f):
        after = jnp.where(last, 0.0, pltpu.roll(f, shape[0] - 1, 0))
        before = jnp.where(first, 0.0, pltpu.roll(f, 1, 0))
        return 0.5 * (after - before)

    def dy(f):
        return 0.5 * (pltpu.roll(f, WIDE - 1, 1) - pltpu.roll(f, 1, 1))

    sxx, sxy, syy = (jnp.where(inside, whole[3 + c], 0.0) for c in range(3))
    force_down = -forcing_gain * (dx(sxx) + dy(sxy))
    force_across = -forcing_gain * (dx(sxy) + dy(syy))
    height, down, across = (whole[c] for c in range(3))
    for _ in range(SW_STEPS):
        height = jnp.where(inside, height - wave_speed * (dx(down) + dy(across)), 0.0)
        down = jnp.where(
            inside, (1.0 - friction) * down - wave_speed * dx(height) + force_down, 0.0
        )
        across = jnp.where(
            inside, (1.0 - friction) * across - wave_speed * dy(height) + force_across, 0.0
        )
    for c, value in enumerate((height, down, across)):
        result[c] = pltpu.roll(value, WIDE - MARGIN, 1)[:, :own_cols]
        out_ref[c] = result[c, pl.ds(pl.multiple_of(band * tile, tile), tile), :]


def shallow_water(place, tiles):
    vmem = pl.BlockSpec(memory_space=pltpu.VMEM)
    fields, rows, width = tiles[0].shape
    own_cols = width - 2 * MARGIN
    return pl.pallas_call(
        water_kernel,
        in_specs=[pl.BlockSpec(memory_space=pltpu.SMEM)] + [vmem] * 4,
        out_specs=vmem,
        out_shape=jax.ShapeDtypeStruct((3, rows, own_cols), jnp.float32),
        scratch_shapes=[
            pltpu.VMEM((fields, 4 * rows, WIDE), jnp.float32),
            pltpu.VMEM((3, 4 * rows, own_cols), jnp.float32),
        ],
        compiler_params=pltpu.CompilerParams(vmem_limit_bytes=4 << 20),
        name="water",
    )(place, *map(in_vmem, tiles))


def window(spectrum, wet_mask, quad_matrix, dissipation, circulation, source_points):
    offset = lax.axis_index("comp") * LOCAL
    speed_east, speed_north, _ = component_tables(offset, LOCAL)
    speeds = jnp.stack([speed_east, speed_north])
    wetness = wet_mask.astype(jnp.float32)[None]
    low = jnp.concatenate([spectrum[:, :HALO], wetness[:, :HALO]], axis=0)
    high = jnp.concatenate([spectrum[:, -HALO:], wetness[:, -HALO:]], axis=0)
    top, bottom = from_neighbours(low, high, "band")
    prop0, prop1, sent = propagate(speeds, spectrum, top, bottom, wetness[0])
    received = lax.all_to_all(sent, "comp", 0, 0, tiled=True)

    tile_rows = circulation.shape[1]
    tile_cols = circulation.shape[2]
    both = jnp.concatenate([circulation, source_points.astype(jnp.float32)], axis=0)
    before, after = from_neighbours(both[:, :, :MARGIN], both[:, :, -MARGIN:], "comp")
    wide = jnp.concatenate([before, both, after], axis=2)
    left_points = before[3:].astype(jnp.int32).reshape(3, 1, 128)
    right_points = after[3:].astype(jnp.int32).reshape(3, 1, 128)
    points = jnp.concatenate([source_points, left_points, right_points], axis=1)
    points = points.reshape(3 * TILES, 128)

    full_coef = component_tables(0, K)[2]
    coef_high = full_coef.astype(jnp.bfloat16).astype(jnp.float32)
    coef_mid = (full_coef - coef_high).astype(jnp.bfloat16).astype(jnp.float32)
    coef_low = full_coef - coef_high - coef_mid
    spare = jnp.zeros((7, K), jnp.float32)
    coef = jnp.concatenate([coef_high, coef_mid, coef_low, spare]).astype(jnp.bfloat16)
    back = sources(
        received.reshape(K * RUN, 128), quad_matrix, dissipation.reshape(K // 128, 128), coef, points
    )
    back = lax.all_to_all(back, "comp", 0, 0, tiled=True)
    cells = pick(back, points)
    own = cells[:, :tile_rows]
    left = cells[:, tile_rows].reshape(3, tile_rows, MARGIN)
    right = cells[:, tile_rows + 1].reshape(3, tile_rows, MARGIN)
    wide_cells = jnp.concatenate([left, own, right], axis=2)
    tile = jnp.concatenate([wide[:3], wide_cells], axis=0)
    bands = lax.axis_size("band")
    tiles = [tile]
    for d in range(1, bands):
        tiles.append(lax.ppermute(tile, "band", [(i, i ^ d) for i in range(bands)]))
    spectrum_out = finish(back, prop0, prop1)
    place = jnp.stack(
        [lax.axis_index("band"), lax.axis_index("comp"), tile_cols * lax.axis_size("comp")]
    )
    circulation_out = shallow_water(place.astype(jnp.int32), tiles)
    return spectrum_out, circulation_out


def solution(mesh):
    in_specs = (
        P("comp", "band", None),
        P("band", None),
        P(),
        P(),
        P(None, "band", "comp"),
        P(None, "band", "comp"),
    )
    out_specs = (P("comp", "band", None), P(None, "band", "comp"))
    return jax.shard_map(window, mesh=mesh, in_specs=in_specs, out_specs=out_specs, check_vma=False)
```

```python
import math

import jax
import jax.numpy as jnp
from jax import lax
from jax.experimental import pallas as pl
from jax.experimental.pallas import tpu as pltpu
from jax.sharding import PartitionSpec as P


NF = 36
ND = 32
K = NF * ND
SUBSTEPS = 4
SRC_STEPS = 4
SW_STEPS = 8

step_source = 0.1
wave_speed = 0.35
friction = 0.05
forcing_gain = 0.15

LOCAL = 36
ROWS = 96
OWNERS = 32
GROUP = 16
RUN = 6
HALO = 4
KB = 4
PAIR = KB
MARGIN = 2 * SW_STEPS
TILES = 10


def component_tables(offset, local_count):
    indices = offset + jnp.arange(local_count, dtype=jnp.int32)
    frequency = (indices // ND).astype(jnp.float32)
    heading = (indices % ND).astype(jnp.float32)
    heading_angle = 2.0 * math.pi * (heading + 0.5) / ND
    fraction = (frequency + 0.5) / NF
    group_speed = 0.25 + 0.4 * fraction
    wave_ratio = 0.5 + 0.5 * fraction
    cosine = jnp.cos(heading_angle)
    sine_part = jnp.sin(heading_angle)
    speed_east = group_speed * cosine
    speed_north = group_speed * sine_part
    stress_coef = jnp.stack(
        [
            wave_ratio * (1.0 + cosine * cosine) - 0.5,
            wave_ratio * sine_part * cosine,
            wave_ratio * (1.0 + sine_part * sine_part) - 0.5,
        ]
    )
    return speed_east, speed_north, stress_coef


def in_hbm(array):
    return pltpu.with_memory_space_constraint(array, pltpu.HBM)


def in_vmem(array):
    return pltpu.with_memory_space_constraint(array, pltpu.VMEM)


def rim_kernel(spec_hbm, wet_hbm, low_ref, high_ref, wet_ref, head, tail, mask, sems):
    copies = (
        pltpu.make_async_copy(spec_hbm.at[:, 0:8, :], head, sems.at[0]),
        pltpu.make_async_copy(spec_hbm.at[:, ROWS - 8:ROWS, :], tail, sems.at[1]),
        pltpu.make_async_copy(wet_hbm, mask, sems.at[2]),
    )
    for copy in copies:
        copy.start()
    copies[2].wait()
    wet = mask[...].astype(jnp.float32)
    wet_ref[...] = wet
    low_ref[LOCAL] = wet[0:HALO]
    high_ref[LOCAL] = wet[ROWS - HALO:ROWS]
    copies[0].wait()
    low_ref[0:LOCAL] = head[:, 0:HALO, :]
    copies[1].wait()
    high_ref[0:LOCAL] = tail[:, 8 - HALO:8, :]


def rims(spectrum, wet_mask):
    cols = spectrum.shape[2]
    vmem = pl.BlockSpec(memory_space=pltpu.VMEM)
    hbm = pl.BlockSpec(memory_space=pltpu.HBM)
    return pl.pallas_call(
        rim_kernel,
        in_specs=[hbm] * 2,
        out_specs=[vmem] * 3,
        out_shape=[
            pltpu.VMEM((LOCAL + 1, HALO, cols), jnp.float32),
            pltpu.VMEM((LOCAL + 1, HALO, cols), jnp.float32),
            pltpu.VMEM((ROWS, cols), jnp.float32),
        ],
        scratch_shapes=[
            pltpu.VMEM((LOCAL, 8, cols), jnp.float32),
            pltpu.VMEM((LOCAL, 8, cols), jnp.float32),
            pltpu.VMEM((ROWS, cols), jnp.int32),
            pltpu.SemaphoreType.DMA((3,)),
        ],
        compiler_params=pltpu.CompilerParams(vmem_limit_bytes=4 << 20),
        name="rims",
    )(in_hbm(spectrum), in_hbm(wet_mask))


def propagate_kernel(
    speeds, spec_hbm, top_ref, bot_ref, wet_ref, prop0_hbm, prop1_hbm, sent_hbm,
    spec_ref, load_sems, prop0, prop1, sent_ref, wet, left_a, right_a, left_b, right_b, keep_sems, sent_sems,
):
    ext = ROWS + 2 * HALO

    def keep(i):
        part = pl.ds(i * KB * ROWS, KB * ROWS)
        return [
            pltpu.make_async_copy(prop.at[part], hbm.at[part], keep_sems.at[h, i])
            for h, (prop, hbm) in enumerate(((prop0, prop0_hbm), (prop1, prop1_hbm)))
        ]

    def give(i):
        rows = pl.ds(i * KB * RUN, KB * RUN)
        return pltpu.make_async_copy(sent_ref.at[i], sent_hbm.at[:, rows, :], sent_sems.at[i])

    def regroup(i):
        for h, prop in enumerate((prop0, prop1)):
            for g in range(GROUP):
                picked = prop[pl.ds(i * KB * ROWS + g, KB * RUN, stride=GROUP), :]
                sent_ref[i, h * GROUP + g] = picked.astype(jnp.bfloat16)

    def load(i):
        part = pl.ds(i * KB, KB)
        return pltpu.make_async_copy(spec_hbm.at[part], spec_ref.at[part], load_sems.at[i])

    def start_load(i, carry):
        load(i).start()
        return carry

    lax.fori_loop(0, LOCAL // KB, start_load, 0)
    wet[0:ROWS, :] = wet_ref[...]
    wet[ROWS:ROWS + HALO, :] = bot_ref[LOCAL]
    wet[ROWS + HALO:ext, :] = top_ref[LOCAL]
    lane = lax.broadcasted_iota(jnp.int32, (ext, 128), 1)
    fields = [[(left_a.at[q], right_a.at[q]), (left_b.at[q], right_b.at[q])] for q in range(PAIR)]

    def advance(first, north):
        edge = 0 if north else 127
        turn = 1 if north else 127
        ahead, a, b, c, side = [], [], [], [], []
        for q in range(PAIR):
            ax = speeds[0, first + q]
            ahead.append(jnp.where(ax >= 0.0, 7, 9))
            a.append(jnp.abs(ax))
            b.append(jnp.abs(speeds[1, first + q]))
            c.append(1.0 - a[q] - b[q])
            side.append(jnp.where(lane == edge, 0.0, b[q]))
        for s in range(SUBSTEPS):
            for q in range(PAIR):
                count = ext if s + 1 < SUBSTEPS else ROWS
                left_ref, right_ref = fields[q][s % 2]
                left, right = left_ref[8:8 + count, :], right_ref[8:8 + count, :]
                ul = left_ref[pl.ds(ahead[q], count), :]
                ur = right_ref[pl.ds(ahead[q], count), :]
                rl = pltpu.roll(left, turn, 1)
                rr = pltpu.roll(right, turn, 1)
                if north:
                    across_l = side[q][:count] * rl
                    across_r = b[q] * jnp.where(lane[:count] == 0, rl, rr)
                else:
                    across_l = b[q] * jnp.where(lane[:count] == 127, rr, rl)
                    across_r = side[q][:count] * rr
                left = wet[:count, :128] * (c[q] * left + a[q] * ul + across_l)
                right = wet[:count, 128:] * (c[q] * right + a[q] * ur + across_r)
                if s + 1 < SUBSTEPS:
                    for ref, value in zip(fields[q][(s + 1) % 2], (left, right)):
                        ref[8:8 + ext, :] = value
                        ref[7:8, :] = value[ext - 1:]
                        ref[8 + ext:9 + ext, :] = value[0:1]
                else:
                    prop0[pl.ds((first + q) * ROWS, ROWS), :] = left
                    prop1[pl.ds((first + q) * ROWS, ROWS), :] = right

    def some(i, carry):
        first = i * PAIR
        for q in range(PAIR):
            k = first + q
            for h, ref in enumerate(fields[q][0]):
                cols = slice(h * 128, (h + 1) * 128)
                top = top_ref[k, :, cols]
                ref[8:8 + ROWS, :] = spec_ref[k, :, cols]
                ref[8 + ROWS:8 + ROWS + HALO, :] = bot_ref[k, :, cols]
                ref[8 + ROWS + HALO:8 + ext, :] = top
                ref[7:8, :] = top[HALO - 1:]
                ref[8 + ext:9 + ext, :] = spec_ref[k, 0:1, cols]
        ay = speeds[1, first]

        @pl.when(ay >= 0.0)
        def _():
            advance(first, True)

        @pl.when(ay < 0.0)
        def _():
            advance(first, False)

        return carry

    def block(i, carry):
        load(i).wait()
        some(i, 0)
        regroup(i)
        give(i).start()
        for copy in keep(i):
            copy.start()
        return carry

    count = LOCAL // KB
    lax.fori_loop(0, count, block, 0)

    def settle(i, carry):
        for copy in keep(i):
            copy.wait()
        give(i).wait()
        return carry

    lax.fori_loop(0, count, settle, 0)


def propagate(speeds, spectrum, top, bottom, wetness):
    cols = spectrum.shape[2]
    ext = ROWS + 2 * HALO
    vmem = pl.BlockSpec(memory_space=pltpu.VMEM)
    hbm = pl.BlockSpec(memory_space=pltpu.HBM)
    return pl.pallas_call(
        propagate_kernel,
        in_specs=[pl.BlockSpec(memory_space=pltpu.SMEM), hbm] + [vmem] * 3,
        out_specs=[hbm] * 3,
        out_shape=[
            pltpu.HBM((LOCAL * ROWS, 128), jnp.float32),
            pltpu.HBM((LOCAL * ROWS, 128), jnp.float32),
            pltpu.HBM((OWNERS, LOCAL * RUN, 128), jnp.bfloat16),
        ],
        scratch_shapes=[
            pltpu.VMEM((LOCAL, ROWS, cols), jnp.float32),
            pltpu.SemaphoreType.DMA((LOCAL // KB,)),
            pltpu.VMEM((LOCAL * ROWS, 128), jnp.float32),
            pltpu.VMEM((LOCAL * ROWS, 128), jnp.float32),
            pltpu.VMEM((LOCAL // KB, OWNERS, KB * RUN, 128), jnp.bfloat16),
            pltpu.VMEM((ext, cols), jnp.float32),
        ]
        + [pltpu.VMEM((PAIR, ext + 16, 128), jnp.float32)] * 4
        + [pltpu.SemaphoreType.DMA((2, LOCAL // KB)), pltpu.SemaphoreType.DMA((LOCAL // KB,))],
        compiler_params=pltpu.CompilerParams(vmem_limit_bytes=16 << 20),
        name="propagate",
    )(pltpu.with_memory_space_constraint(speeds, pltpu.SMEM), in_hbm(spectrum), *map(in_vmem, (top, bottom, wetness)))


MB = 576
EB = 64
NB = 256
OWN_ROWS = RUN * LOCAL
PIECES = 3
BLOCKS = RUN * 128 // NB
BACK_ROWS = OWN_ROWS + 8 * PIECES


def source_kernel(
    recv_ref, quad_hbm, diss_ref, coef_ref, points_ref, back_hbm,
    quad_ref, back_ref, prod_a, prod_b, flat, cur, xa, xb, rate, level, quad_sems, out_sem,
):
    halves = K // MB
    points = RUN * 128

    def fetch(m):
        part = pl.ds(m * MB, MB)
        return pltpu.make_async_copy(quad_hbm.at[part], quad_ref.at[part], quad_sems.at[m])

    for m in range(halves):
        fetch(m).start()

    def widen(i, carry):
        flat[pl.ds(i * K, K), :] = recv_ref[pl.ds(i * K, K), :].astype(jnp.float32)
        return carry

    lax.fori_loop(0, RUN, widen, 0)
    for i in range(K // 128):
        rate[i * 128:(i + 1) * 128, :] = jnp.broadcast_to(diss_ref[i:i + 1, :], (128, 128)).T
    coef = coef_ref[...]
    each_block = NB // 128
    stress = []
    rows_of = [[], [], []]

    def prepare(n):
        for j in range(n * each_block, (n + 1) * each_block):
            base = flat[pl.ds(j, K, stride=RUN), :]
            cols = slice(j * 128, (j + 1) * 128)
            cur[:, cols] = base
            xa[:, cols] = base.astype(jnp.bfloat16)
            level[:, cols] = jnp.sum(base, axis=0, keepdims=True)

    def multiply(s, n):
        held = (prod_a, prod_b)[(s * BLOCKS + n) % 2]
        old = (xa, xb)[s % 2]
        for m in range(halves):
            rows = slice(m * MB, (m + 1) * MB)
            held[rows, :] = jnp.dot(
                quad_ref[rows, :], old[:, n * NB:(n + 1) * NB], preferred_element_type=jnp.float32
            )

    def update(s, n):
        held = (prod_a, prod_b)[(s * BLOCKS + n) % 2]
        new = (xb, xa)[s % 2]
        cols = slice(n * NB, (n + 1) * NB)
        mean = level[:, cols] * (1.0 / K)
        sums = jnp.zeros((8, NB), jnp.float32)
        for m in range(K // EB):
            rows = slice(m * EB, (m + 1) * EB)
            each = jnp.concatenate([rate[rows, :]] * each_block, axis=1)
            now = cur[rows, cols]
            now = now + step_source * now * (held[rows, :] - each * mean)
            cur[rows, cols] = now
            if s + 1 < SRC_STEPS:
                new[rows, cols] = now.astype(jnp.bfloat16)
                sums = sums + jnp.sum(now.reshape(EB // 8, 8, NB), axis=0)
        if s + 1 < SRC_STEPS:
            level[:, cols] = jnp.sum(sums, axis=0, keepdims=True)

    def conclude(n):
        for j in range(n * each_block, (n + 1) * each_block):
            base = flat[pl.ds(j, K, stride=RUN), :]
            cols = slice(j * 128, (j + 1) * 128)
            gain = (cur[:, cols] - base).astype(jnp.bfloat16)
            xb[:, cols] = gain
            flat[pl.ds(j, K, stride=RUN), :] = gain.astype(jnp.float32)

    def weigh(n):
        both = stress[n] + jnp.dot(
            coef, xb[:, n * NB:(n + 1) * NB], preferred_element_type=jnp.float32
        )
        for c in range(3):
            row = (both[c:c + 1] + both[3 + c:4 + c] + both[6 + c:7 + c]) * (1.0 / K)
            rows_of[c] += [row[:, i * 128:(i + 1) * 128] for i in range(each_block)]

    for n in range(BLOCKS):
        prepare(n)
    for n in range(BLOCKS):
        stress.append(
            jnp.dot(coef, xa[:, n * NB:(n + 1) * NB], preferred_element_type=jnp.float32)
        )
    for m in range(halves):
        fetch(m).wait()
    turns = [(s, n) for s in range(SRC_STEPS) for n in range(BLOCKS)]
    for i, (s, n) in enumerate(turns):
        multiply(s, n)
        if i > 0:
            update(*turns[i - 1])
    update(*turns[-1])
    for n in range(BLOCKS):
        conclude(n)
    for n in range(BLOCKS):
        weigh(n)
    pieces = []
    for c in range(3):
        whole = jnp.concatenate(rows_of[c], axis=0)
        mean = jnp.sum(jnp.sum(whole, axis=0, keepdims=True), axis=1, keepdims=True)
        mean = jnp.broadcast_to(mean * (1.0 / points), (1, 128))
        high = mean.astype(jnp.bfloat16).astype(jnp.float32)
        low = (mean - high).astype(jnp.bfloat16).astype(jnp.float32)
        pieces += [whole - (high + low), high, low]
    shared = jnp.concatenate(pieces, axis=0).astype(jnp.bfloat16)

    def narrow(o, carry):
        back_ref[o, 0:OWN_ROWS, :] = flat[pl.ds(o * OWN_ROWS, OWN_ROWS), :].astype(jnp.bfloat16)
        back_ref[o, OWN_ROWS:BACK_ROWS, :] = shared
        pltpu.make_async_copy(back_ref.at[o], back_hbm.at[o], out_sem).start()
        return carry

    lax.fori_loop(0, OWNERS, narrow, 0)
    pltpu.make_async_copy(back_ref, back_hbm, out_sem).wait()


def sources(received, quad_matrix, rates, coef, points_list):
    points = RUN * 128
    vmem = pl.BlockSpec(memory_space=pltpu.VMEM)
    hbm = pl.BlockSpec(memory_space=pltpu.HBM)
    return pl.pallas_call(
        source_kernel,
        in_specs=[vmem, hbm, vmem, vmem, hbm],
        out_specs=hbm,
        out_shape=pltpu.HBM((OWNERS, BACK_ROWS, 128), jnp.bfloat16),
        scratch_shapes=[
            pltpu.VMEM((K, K), jnp.bfloat16),
            pltpu.VMEM((OWNERS, BACK_ROWS, 128), jnp.bfloat16),
            pltpu.VMEM((K, NB), jnp.float32),
            pltpu.VMEM((K, NB), jnp.float32),
            pltpu.VMEM((K * RUN, 128), jnp.float32),
            pltpu.VMEM((K, points), jnp.float32),
            pltpu.VMEM((K, points), jnp.bfloat16),
            pltpu.VMEM((K, points), jnp.bfloat16),
            pltpu.VMEM((K, 128), jnp.float32),
            pltpu.VMEM((1, points), jnp.float32),
            pltpu.SemaphoreType.DMA((K // MB,)),
            pltpu.SemaphoreType.DMA(()),
        ],
        compiler_params=pltpu.CompilerParams(vmem_limit_bytes=30 << 20),
        name="sources",
    )(in_vmem(received), in_hbm(quad_matrix), in_vmem(rates), in_vmem(coef), in_hbm(points_list))


def pick_kernel(back_ref, points_ref, out_ref):
    pieces = []
    for i in range(PIECES):
        at = OWN_ROWS + 8 * i
        rows = back_ref[:, at:at + 8, :].astype(jnp.float32).reshape(OWNERS * 8, 128)
        pieces.append(rows.T.astype(jnp.bfloat16))
    table = jnp.concatenate(pieces, axis=0)
    kind = lax.broadcasted_iota(jnp.int32, (8, 128), 0)
    slot = lax.broadcasted_iota(jnp.int32, (OWNERS, 8, 128), 0) * 8 + kind
    within = lax.broadcasted_iota(jnp.int32, (128, 128), 0)
    weights = (0.5, 0.3, 0.2)
    for t in range(TILES):
        hots, lows = [], []
        for m in range(3):
            p = points_ref[m * TILES + t:m * TILES + t + 1, :]
            row = p >> 8
            col = p & 255
            hi = (((col >> 7) * GROUP + (row & (GROUP - 1))) << 3) + (row >> 4)
            wanted = jnp.where(kind < RUN, hi, (hi & -8) + kind)
            taken = jnp.where(slot == wanted, 1.0, 0.0).reshape(OWNERS * 8, 128)
            hots.append(taken.astype(jnp.bfloat16))
            lows.append(col & 127)
        hot = jnp.concatenate(hots, axis=1)
        found = jnp.dot(table, hot, preferred_element_type=jnp.float32)
        for c in range(3):
            both = found[c * 128:(c + 1) * 128]
            acc = jnp.zeros((8, 128), jnp.float32)
            for m in range(3):
                kept = jnp.where(within == lows[m], both[:, m * 128:(m + 1) * 128], 0.0)
                acc = acc + weights[m] * jnp.sum(kept.reshape(16, 8, 128), axis=0)
            out_ref[c, t:t + 1, :] = jnp.sum(acc, axis=0, keepdims=True)


def pick(back, points):
    vmem = pl.BlockSpec(memory_space=pltpu.VMEM)
    return pl.pallas_call(
        pick_kernel,
        in_specs=[vmem] * 2,
        out_specs=vmem,
        out_shape=pltpu.VMEM((3, TILES, 128), jnp.float32),
        compiler_params=pltpu.CompilerParams(vmem_limit_bytes=10 << 20),
        name="pick",
    )(in_vmem(back), in_vmem(points))


def finish_kernel(
    back_ref, prop0_hbm, prop1_hbm, out_hbm, prop0, prop1, wide, out, sems, keep_sems,
):
    def keep(i):
        part = pl.ds(i * KB * ROWS, KB * ROWS)
        return [
            pltpu.make_async_copy(hbm.at[part], prop.at[part], keep_sems.at[h, i])
            for h, (prop, hbm) in enumerate(((prop0, prop0_hbm), (prop1, prop1_hbm)))
        ]

    def load(i, carry):
        for copy in keep(i):
            copy.start()
        return carry

    lax.fori_loop(0, LOCAL // KB, load, 0)

    def spread(i):
        rows = pl.ds(pl.multiple_of(i * KB * RUN, 8), KB * RUN)
        for h in range(2):
            for g in range(GROUP):
                gain = back_ref[h * GROUP + g, rows, :].astype(jnp.float32)
                wide[h, pl.ds(g, KB * RUN, stride=GROUP), :] = gain

    def copy(i):
        part = pl.ds(i * KB, KB)
        return pltpu.make_async_copy(out.at[part], out_hbm.at[part], sems.at[i])

    def add(i, carry):
        spread(i)
        for copy_in in keep(i):
            copy_in.wait()
        for kk in range(KB):
            k = i * KB + kk
            for h, prop in enumerate((prop0, prop1)):
                rows = pl.ds(k * ROWS, ROWS)
                out[k, :, h * 128:(h + 1) * 128] = (
                    prop[rows, :] + wide[h, kk * ROWS:(kk + 1) * ROWS, :]
                )
        copy(i).start()
        return carry

    lax.fori_loop(0, LOCAL // KB, add, 0)

    def settle(i, carry):
        copy(i).wait()
        return carry

    lax.fori_loop(0, LOCAL // KB, settle, 0)


def finish(back, prop0, prop1):
    vmem = pl.BlockSpec(memory_space=pltpu.VMEM)
    hbm = pl.BlockSpec(memory_space=pltpu.HBM)
    shape = (LOCAL, ROWS, 256)
    return pl.pallas_call(
        finish_kernel,
        in_specs=[vmem, hbm, hbm],
        out_specs=hbm,
        out_shape=pltpu.HBM(shape, jnp.float32),
        scratch_shapes=[
            pltpu.VMEM((LOCAL * ROWS, 128), jnp.float32),
            pltpu.VMEM((LOCAL * ROWS, 128), jnp.float32),
            pltpu.VMEM((2, KB * ROWS, 128), jnp.float32),
            pltpu.VMEM(shape, jnp.float32),
            pltpu.SemaphoreType.DMA((LOCAL // KB,)),
            pltpu.SemaphoreType.DMA((2, LOCAL // KB)),
        ],
        compiler_params=pltpu.CompilerParams(vmem_limit_bytes=16 << 20),
        name="finish",
    )(in_vmem(back), in_hbm(prop0), in_hbm(prop1))


def from_neighbours(low, high, axis):
    count = lax.axis_size(axis)
    ends = count - 1
    before = lax.ppermute(high, axis, [(i, (i + 1) % count) for i in range(ends)])
    after = lax.ppermute(low, axis, [((i + 1) % count, i) for i in range(ends)])
    return before, after


WIDE = 256


def water_kernel(own_ref, one_ref, two_ref, three_ref, out_ref, whole, result):
    bands = 4
    tile = own_ref.shape[1]
    width = own_ref.shape[2]
    own_cols = width - 2 * MARGIN
    band = lax.axis_index("band")
    comp = lax.axis_index("comp")
    whole[...] = jnp.zeros_like(whole)
    for d, ref in enumerate((own_ref, one_ref, two_ref, three_ref)):
        row = pl.multiple_of((band ^ d) * tile, tile)
        whole[:, pl.ds(row, tile), 0:width] = ref[...]
    shape = (bands * tile, WIDE)
    lane = lax.broadcasted_iota(jnp.int32, shape, 1)
    line = lax.broadcasted_iota(jnp.int32, shape, 0)
    col = comp * own_cols - MARGIN + lane
    inside = (col >= 0) & (col < lax.axis_size("comp") * own_cols) & (lane < width)
    first = line == 0
    last = line == shape[0] - 1

    def dx(f):
        after = jnp.where(last, 0.0, pltpu.roll(f, shape[0] - 1, 0))
        before = jnp.where(first, 0.0, pltpu.roll(f, 1, 0))
        return 0.5 * (after - before)

    def dy(f):
        return 0.5 * (pltpu.roll(f, WIDE - 1, 1) - pltpu.roll(f, 1, 1))

    sxx, sxy, syy = (jnp.where(inside, whole[3 + c], 0.0) for c in range(3))
    force_down = -forcing_gain * (dx(sxx) + dy(sxy))
    force_across = -forcing_gain * (dx(sxy) + dy(syy))
    height, down, across = (whole[c] for c in range(3))
    for _ in range(SW_STEPS):
        height = jnp.where(inside, height - wave_speed * (dx(down) + dy(across)), 0.0)
        down = jnp.where(
            inside, (1.0 - friction) * down - wave_speed * dx(height) + force_down, 0.0
        )
        across = jnp.where(
            inside, (1.0 - friction) * across - wave_speed * dy(height) + force_across, 0.0
        )
    for c, value in enumerate((height, down, across)):
        result[c] = pltpu.roll(value, WIDE - MARGIN, 1)[:, :own_cols]
        out_ref[c] = result[c, pl.ds(pl.multiple_of(band * tile, tile), tile), :]


def shallow_water(tiles):
    vmem = pl.BlockSpec(memory_space=pltpu.VMEM)
    fields, rows, width = tiles[0].shape
    own_cols = width - 2 * MARGIN
    return pl.pallas_call(
        water_kernel,
        in_specs=[vmem] * 4,
        out_specs=vmem,
        out_shape=jax.ShapeDtypeStruct((3, rows, own_cols), jnp.float32),
        scratch_shapes=[
            pltpu.VMEM((fields, 4 * rows, WIDE), jnp.float32),
            pltpu.VMEM((3, 4 * rows, own_cols), jnp.float32),
        ],
        compiler_params=pltpu.CompilerParams(vmem_limit_bytes=4 << 20),
        name="water",
    )(*map(in_vmem, tiles))


def window(spectrum, wet_mask, quad_matrix, dissipation, circulation, source_points):
    offset = lax.axis_index("comp") * LOCAL
    speed_east, speed_north, _ = component_tables(offset, LOCAL)
    speeds = jnp.stack([speed_east, speed_north])
    low, high, wetness = rims(spectrum, wet_mask)
    top, bottom = from_neighbours(low, high, "band")
    prop0, prop1, sent = propagate(speeds, spectrum, top, bottom, wetness)
    received = lax.all_to_all(sent, "comp", 0, 0, tiled=True)

    tile_rows = circulation.shape[1]
    both = jnp.concatenate([circulation, source_points.astype(jnp.float32)], axis=0)
    before, after = from_neighbours(both[:, :, :MARGIN], both[:, :, -MARGIN:], "comp")
    wide = jnp.concatenate([before, both, after], axis=2)
    left_points = before[3:].astype(jnp.int32).reshape(3, 1, 128)
    right_points = after[3:].astype(jnp.int32).reshape(3, 1, 128)
    points = jnp.concatenate([source_points, left_points, right_points], axis=1)
    points = points.reshape(3 * TILES, 128)

    full_coef = component_tables(0, K)[2]
    coef_high = full_coef.astype(jnp.bfloat16).astype(jnp.float32)
    coef_mid = (full_coef - coef_high).astype(jnp.bfloat16).astype(jnp.float32)
    coef_low = full_coef - coef_high - coef_mid
    spare = jnp.zeros((7, K), jnp.float32)
    coef = jnp.concatenate([coef_high, coef_mid, coef_low, spare]).astype(jnp.bfloat16)
    back = sources(
        received.reshape(K * RUN, 128), quad_matrix, dissipation.reshape(K // 128, 128), coef, points
    )
    back = lax.all_to_all(back, "comp", 0, 0, tiled=True)
    cells = pick(back, points)
    own = cells[:, :tile_rows]
    left = cells[:, tile_rows].reshape(3, tile_rows, MARGIN)
    right = cells[:, tile_rows + 1].reshape(3, tile_rows, MARGIN)
    wide_cells = jnp.concatenate([left, own, right], axis=2)
    tile = jnp.concatenate([wide[:3], wide_cells], axis=0)
    bands = lax.axis_size("band")
    tiles = [tile]
    for d in range(1, bands):
        tiles.append(lax.ppermute(tile, "band", [(i, i ^ d) for i in range(bands)]))
    spectrum_out = finish(back, prop0, prop1)
    circulation_out = shallow_water(tiles)
    return spectrum_out, circulation_out


def solution(mesh):
    in_specs = (
        P("comp", "band", None),
        P("band", None),
        P(),
        P(),
        P(None, "band", "comp"),
        P(None, "band", "comp"),
    )
    out_specs = (P("comp", "band", None), P(None, "band", "comp"))
    return jax.shard_map(window, mesh=mesh, in_specs=in_specs, out_specs=out_specs, check_vma=False)
```

```python
import math

import jax
import jax.numpy as jnp
from jax import lax
from jax.experimental import pallas as pl
from jax.experimental.pallas import tpu as pltpu
from jax.sharding import PartitionSpec as P


NF = 36
ND = 32
K = NF * ND
SUBSTEPS = 4
SRC_STEPS = 4
SW_STEPS = 8

step_source = 0.1
wave_speed = 0.35
friction = 0.05
forcing_gain = 0.15

LOCAL = 36
ROWS = 96
OWNERS = 32
GROUP = 16
RUN = 6
HALO = 4
KB = 4
PAIR = KB
MARGIN = 2 * SW_STEPS
TILES = 10


def component_tables(offset, local_count):
    indices = offset + jnp.arange(local_count, dtype=jnp.int32)
    frequency = (indices // ND).astype(jnp.float32)
    heading = (indices % ND).astype(jnp.float32)
    heading_angle = 2.0 * math.pi * (heading + 0.5) / ND
    fraction = (frequency + 0.5) / NF
    group_speed = 0.25 + 0.4 * fraction
    wave_ratio = 0.5 + 0.5 * fraction
    cosine = jnp.cos(heading_angle)
    sine_part = jnp.sin(heading_angle)
    speed_east = group_speed * cosine
    speed_north = group_speed * sine_part
    stress_coef = jnp.stack(
        [
            wave_ratio * (1.0 + cosine * cosine) - 0.5,
            wave_ratio * sine_part * cosine,
            wave_ratio * (1.0 + sine_part * sine_part) - 0.5,
        ]
    )
    return speed_east, speed_north, stress_coef


def in_hbm(array):
    return pltpu.with_memory_space_constraint(array, pltpu.HBM)


def in_vmem(array):
    return pltpu.with_memory_space_constraint(array, pltpu.VMEM)


def rim_kernel(spec_hbm, wet_hbm, low_ref, high_ref, wet_ref, head, tail, mask, sems):
    copies = (
        pltpu.make_async_copy(spec_hbm.at[:, 0:8, :], head, sems.at[0]),
        pltpu.make_async_copy(spec_hbm.at[:, ROWS - 8:ROWS, :], tail, sems.at[1]),
        pltpu.make_async_copy(wet_hbm, mask, sems.at[2]),
    )
    for copy in copies:
        copy.start()
    copies[2].wait()
    wet = mask[...].astype(jnp.float32)
    wet_ref[...] = wet
    low_ref[LOCAL] = wet[0:HALO]
    high_ref[LOCAL] = wet[ROWS - HALO:ROWS]
    copies[0].wait()
    low_ref[0:LOCAL] = head[:, 0:HALO, :]
    copies[1].wait()
    high_ref[0:LOCAL] = tail[:, 8 - HALO:8, :]


def rims(spectrum, wet_mask):
    cols = spectrum.shape[2]
    vmem = pl.BlockSpec(memory_space=pltpu.VMEM)
    hbm = pl.BlockSpec(memory_space=pltpu.HBM)
    return pl.pallas_call(
        rim_kernel,
        in_specs=[hbm] * 2,
        out_specs=[vmem] * 3,
        out_shape=[
            pltpu.VMEM((LOCAL + 1, HALO, cols), jnp.float32),
            pltpu.VMEM((LOCAL + 1, HALO, cols), jnp.float32),
            pltpu.VMEM((ROWS, cols), jnp.float32),
        ],
        scratch_shapes=[
            pltpu.VMEM((LOCAL, 8, cols), jnp.float32),
            pltpu.VMEM((LOCAL, 8, cols), jnp.float32),
            pltpu.VMEM((ROWS, cols), jnp.int32),
            pltpu.SemaphoreType.DMA((3,)),
        ],
        compiler_params=pltpu.CompilerParams(vmem_limit_bytes=4 << 20),
        name="rims",
    )(in_hbm(spectrum), in_hbm(wet_mask))


def propagate_kernel(
    speeds, spec_hbm, top_ref, bot_ref, wet_ref, prop0_hbm, prop1_hbm, sent_hbm,
    spec_ref, load_sems, prop0, prop1, sent_ref, wet, left_a, right_a, left_b, right_b, keep_sems, sent_sems,
):
    ext = ROWS + 2 * HALO

    def keep(i):
        part = pl.ds(i * KB * ROWS, KB * ROWS)
        return [
            pltpu.make_async_copy(prop.at[part], hbm.at[part], keep_sems.at[h, i])
            for h, (prop, hbm) in enumerate(((prop0, prop0_hbm), (prop1, prop1_hbm)))
        ]

    def give(i):
        rows = pl.ds(i * KB * RUN, KB * RUN)
        return pltpu.make_async_copy(sent_ref.at[i], sent_hbm.at[:, rows, :], sent_sems.at[i])

    def regroup(i):
        for h, prop in enumerate((prop0, prop1)):
            for g in range(GROUP):
                picked = prop[pl.ds(i * KB * ROWS + g, KB * RUN, stride=GROUP), :]
                sent_ref[i, h * GROUP + g] = picked.astype(jnp.bfloat16)

    def load(i):
        part = pl.ds(i * KB, KB)
        return pltpu.make_async_copy(spec_hbm.at[part], spec_ref.at[part], load_sems.at[i])

    def start_load(i, carry):
        load(i).start()
        return carry

    lax.fori_loop(0, LOCAL // KB, start_load, 0)
    wet[0:ROWS, :] = wet_ref[...]
    wet[ROWS:ROWS + HALO, :] = bot_ref[LOCAL]
    wet[ROWS + HALO:ext, :] = top_ref[LOCAL]
    lane = lax.broadcasted_iota(jnp.int32, (ext, 128), 1)
    fields = [[(left_a.at[q], right_a.at[q]), (left_b.at[q], right_b.at[q])] for q in range(PAIR)]

    def advance(first, north):
        edge = 0 if north else 127
        turn = 1 if north else 127
        ahead, a, b, c, side = [], [], [], [], []
        for q in range(PAIR):
            ax = speeds[0, first + q]
            ahead.append(jnp.where(ax >= 0.0, 7, 9))
            a.append(jnp.abs(ax))
            b.append(jnp.abs(speeds[1, first + q]))
            c.append(1.0 - a[q] - b[q])
            side.append(jnp.where(lane == edge, 0.0, b[q]))
        for s in range(SUBSTEPS):
            for q in range(PAIR):
                count = ext if s + 1 < SUBSTEPS else ROWS
                left_ref, right_ref = fields[q][s % 2]
                left, right = left_ref[8:8 + count, :], right_ref[8:8 + count, :]
                ul = left_ref[pl.ds(ahead[q], count), :]
                ur = right_ref[pl.ds(ahead[q], count), :]
                rl = pltpu.roll(left, turn, 1)
                rr = pltpu.roll(right, turn, 1)
                if north:
                    across_l = side[q][:count] * rl
                    across_r = b[q] * jnp.where(lane[:count] == 0, rl, rr)
                else:
                    across_l = b[q] * jnp.where(lane[:count] == 127, rr, rl)
                    across_r = side[q][:count] * rr
                left = wet[:count, :128] * (c[q] * left + a[q] * ul + across_l)
                right = wet[:count, 128:] * (c[q] * right + a[q] * ur + across_r)
                if s + 1 < SUBSTEPS:
                    for ref, value in zip(fields[q][(s + 1) % 2], (left, right)):
                        ref[8:8 + ext, :] = value
                        ref[7:8, :] = value[ext - 1:]
                        ref[8 + ext:9 + ext, :] = value[0:1]
                else:
                    prop0[pl.ds((first + q) * ROWS, ROWS), :] = left
                    prop1[pl.ds((first + q) * ROWS, ROWS), :] = right

    def some(i, carry):
        first = i * PAIR
        for q in range(PAIR):
            k = first + q
            for h, ref in enumerate(fields[q][0]):
                cols = slice(h * 128, (h + 1) * 128)
                top = top_ref[k, :, cols]
                ref[8:8 + ROWS, :] = spec_ref[k, :, cols]
                ref[8 + ROWS:8 + ROWS + HALO, :] = bot_ref[k, :, cols]
                ref[8 + ROWS + HALO:8 + ext, :] = top
                ref[7:8, :] = top[HALO - 1:]
                ref[8 + ext:9 + ext, :] = spec_ref[k, 0:1, cols]
        ay = speeds[1, first]

        @pl.when(ay >= 0.0)
        def _():
            advance(first, True)

        @pl.when(ay < 0.0)
        def _():
            advance(first, False)

        return carry

    def block(i, carry):
        load(i).wait()
        some(i, 0)
        regroup(i)
        give(i).start()
        for copy in keep(i):
            copy.start()
        return carry

    count = LOCAL // KB
    lax.fori_loop(0, count, block, 0)

    def settle(i, carry):
        for copy in keep(i):
            copy.wait()
        give(i).wait()
        return carry

    lax.fori_loop(0, count, settle, 0)


def propagate(speeds, spectrum, top, bottom, wetness):
    cols = spectrum.shape[2]
    ext = ROWS + 2 * HALO
    vmem = pl.BlockSpec(memory_space=pltpu.VMEM)
    hbm = pl.BlockSpec(memory_space=pltpu.HBM)
    return pl.pallas_call(
        propagate_kernel,
        in_specs=[pl.BlockSpec(memory_space=pltpu.SMEM), hbm] + [vmem] * 3,
        out_specs=[hbm] * 3,
        out_shape=[
            pltpu.HBM((LOCAL * ROWS, 128), jnp.float32),
            pltpu.HBM((LOCAL * ROWS, 128), jnp.float32),
            pltpu.HBM((OWNERS, LOCAL * RUN, 128), jnp.bfloat16),
        ],
        scratch_shapes=[
            pltpu.VMEM((LOCAL, ROWS, cols), jnp.float32),
            pltpu.SemaphoreType.DMA((LOCAL // KB,)),
            pltpu.VMEM((LOCAL * ROWS, 128), jnp.float32),
            pltpu.VMEM((LOCAL * ROWS, 128), jnp.float32),
            pltpu.VMEM((LOCAL // KB, OWNERS, KB * RUN, 128), jnp.bfloat16),
            pltpu.VMEM((ext, cols), jnp.float32),
        ]
        + [pltpu.VMEM((PAIR, ext + 16, 128), jnp.float32)] * 4
        + [pltpu.SemaphoreType.DMA((2, LOCAL // KB)), pltpu.SemaphoreType.DMA((LOCAL // KB,))],
        compiler_params=pltpu.CompilerParams(vmem_limit_bytes=16 << 20),
        name="propagate",
    )(pltpu.with_memory_space_constraint(speeds, pltpu.SMEM), in_hbm(spectrum), *map(in_vmem, (top, bottom, wetness)))


MB = 576
EB = 64
NB = 256
OWN_ROWS = RUN * LOCAL
PIECES = 3
BLOCKS = RUN * 128 // NB
BACK_ROWS = OWN_ROWS + 8 * PIECES


def source_kernel(
    recv_ref, quad_hbm, diss_ref, coef_ref, back_hbm,
    quad_ref, back_ref, prod_a, prod_b, flat, cur, xa, xb, rate, level, quad_sems, out_sem,
):
    halves = K // MB
    points = RUN * 128

    def fetch(m):
        part = pl.ds(m * MB, MB)
        return pltpu.make_async_copy(quad_hbm.at[part], quad_ref.at[part], quad_sems.at[m])

    for m in range(halves):
        fetch(m).start()

    def widen(i, carry):
        flat[pl.ds(i * K, K), :] = recv_ref[pl.ds(i * K, K), :].astype(jnp.float32)
        return carry

    lax.fori_loop(0, RUN, widen, 0)
    for i in range(K // 128):
        rate[i * 128:(i + 1) * 128, :] = jnp.broadcast_to(diss_ref[i:i + 1, :], (128, 128)).T
    coef = coef_ref[...]
    each_block = NB // 128
    stress = []
    rows_of = [[], [], []]

    def prepare(n):
        for j in range(n * each_block, (n + 1) * each_block):
            base = flat[pl.ds(j, K, stride=RUN), :]
            cols = slice(j * 128, (j + 1) * 128)
            cur[:, cols] = base
            xa[:, cols] = base.astype(jnp.bfloat16)
            level[:, cols] = jnp.sum(base, axis=0, keepdims=True)

    def multiply(s, n):
        held = (prod_a, prod_b)[(s * BLOCKS + n) % 2]
        old = (xa, xb)[s % 2]
        for m in range(halves):
            rows = slice(m * MB, (m + 1) * MB)
            held[rows, :] = jnp.dot(
                quad_ref[rows, :], old[:, n * NB:(n + 1) * NB], preferred_element_type=jnp.float32
            )

    def update(s, n):
        held = (prod_a, prod_b)[(s * BLOCKS + n) % 2]
        new = (xb, xa)[s % 2]
        cols = slice(n * NB, (n + 1) * NB)
        mean = level[:, cols] * (1.0 / K)
        sums = jnp.zeros((8, NB), jnp.float32)
        for m in range(K // EB):
            rows = slice(m * EB, (m + 1) * EB)
            each = jnp.concatenate([rate[rows, :]] * each_block, axis=1)
            now = cur[rows, cols]
            now = now + step_source * now * (held[rows, :] - each * mean)
            cur[rows, cols] = now
            if s + 1 < SRC_STEPS:
                new[rows, cols] = now.astype(jnp.bfloat16)
                sums = sums + jnp.sum(now.reshape(EB // 8, 8, NB), axis=0)
        if s + 1 < SRC_STEPS:
            level[:, cols] = jnp.sum(sums, axis=0, keepdims=True)

    def conclude(n):
        for j in range(n * each_block, (n + 1) * each_block):
            base = flat[pl.ds(j, K, stride=RUN), :]
            cols = slice(j * 128, (j + 1) * 128)
            gain = (cur[:, cols] - base).astype(jnp.bfloat16)
            xb[:, cols] = gain
            flat[pl.ds(j, K, stride=RUN), :] = gain.astype(jnp.float32)

    def weigh(n):
        both = stress[n] + jnp.dot(
            coef, xb[:, n * NB:(n + 1) * NB], preferred_element_type=jnp.float32
        )
        for c in range(3):
            row = (both[c:c + 1] + both[3 + c:4 + c] + both[6 + c:7 + c]) * (1.0 / K)
            rows_of[c] += [row[:, i * 128:(i + 1) * 128] for i in range(each_block)]

    for n in range(BLOCKS):
        prepare(n)
    for n in range(BLOCKS):
        stress.append(
            jnp.dot(coef, xa[:, n * NB:(n + 1) * NB], preferred_element_type=jnp.float32)
        )
    for m in range(halves):
        fetch(m).wait()
    turns = [(s, n) for s in range(SRC_STEPS) for n in range(BLOCKS)]
    for i, (s, n) in enumerate(turns):
        multiply(s, n)
        if i > 0:
            update(*turns[i - 1])
    update(*turns[-1])
    for n in range(BLOCKS):
        conclude(n)
    for n in range(BLOCKS):
        weigh(n)
    pieces = []
    for c in range(3):
        whole = jnp.concatenate(rows_of[c], axis=0)
        mean = jnp.sum(jnp.sum(whole, axis=0, keepdims=True), axis=1, keepdims=True)
        mean = jnp.broadcast_to(mean * (1.0 / points), (1, 128))
        high = mean.astype(jnp.bfloat16).astype(jnp.float32)
        low = (mean - high).astype(jnp.bfloat16).astype(jnp.float32)
        pieces += [whole - (high + low), high, low]
    shared = jnp.concatenate(pieces, axis=0).astype(jnp.bfloat16)

    def narrow(o, carry):
        back_ref[o, 0:OWN_ROWS, :] = flat[pl.ds(o * OWN_ROWS, OWN_ROWS), :].astype(jnp.bfloat16)
        back_ref[o, OWN_ROWS:BACK_ROWS, :] = shared
        pltpu.make_async_copy(back_ref.at[o], back_hbm.at[o], out_sem).start()
        return carry

    lax.fori_loop(0, OWNERS, narrow, 0)
    pltpu.make_async_copy(back_ref, back_hbm, out_sem).wait()


def sources(received, quad_matrix, rates, coef):
    points = RUN * 128
    vmem = pl.BlockSpec(memory_space=pltpu.VMEM)
    hbm = pl.BlockSpec(memory_space=pltpu.HBM)
    return pl.pallas_call(
        source_kernel,
        in_specs=[vmem, hbm, vmem, vmem],
        out_specs=hbm,
        out_shape=pltpu.HBM((OWNERS, BACK_ROWS, 128), jnp.bfloat16),
        scratch_shapes=[
            pltpu.VMEM((K, K), jnp.bfloat16),
            pltpu.VMEM((OWNERS, BACK_ROWS, 128), jnp.bfloat16),
            pltpu.VMEM((K, NB), jnp.float32),
            pltpu.VMEM((K, NB), jnp.float32),
            pltpu.VMEM((K * RUN, 128), jnp.float32),
            pltpu.VMEM((K, points), jnp.float32),
            pltpu.VMEM((K, points), jnp.bfloat16),
            pltpu.VMEM((K, points), jnp.bfloat16),
            pltpu.VMEM((K, 128), jnp.float32),
            pltpu.VMEM((1, points), jnp.float32),
            pltpu.SemaphoreType.DMA((K // MB,)),
            pltpu.SemaphoreType.DMA(()),
        ],
        compiler_params=pltpu.CompilerParams(vmem_limit_bytes=30 << 20),
        name="sources",
    )(in_vmem(received), in_hbm(quad_matrix), in_vmem(rates), in_vmem(coef))


def pick_kernel(back_ref, points_ref, out_ref):
    pieces = []
    for i in range(PIECES):
        at = OWN_ROWS + 8 * i
        rows = back_ref[:, at:at + 8, :].astype(jnp.float32).reshape(OWNERS * 8, 128)
        pieces.append(rows.T.astype(jnp.bfloat16))
    table = jnp.concatenate(pieces, axis=0)
    kind = lax.broadcasted_iota(jnp.int32, (8, 128), 0)
    slot = lax.broadcasted_iota(jnp.int32, (OWNERS, 8, 128), 0) * 8 + kind
    within = lax.broadcasted_iota(jnp.int32, (128, 128), 0)
    weights = (0.5, 0.3, 0.2)
    for t in range(TILES):
        hots, lows = [], []
        for m in range(3):
            p = points_ref[m * TILES + t:m * TILES + t + 1, :]
            row = p >> 8
            col = p & 255
            hi = (((col >> 7) * GROUP + (row & (GROUP - 1))) << 3) + (row >> 4)
            wanted = jnp.where(kind < RUN, hi, (hi & -8) + kind)
            taken = jnp.where(slot == wanted, 1.0, 0.0).reshape(OWNERS * 8, 128)
            hots.append(taken.astype(jnp.bfloat16))
            lows.append(col & 127)
        hot = jnp.concatenate(hots, axis=1)
        found = jnp.dot(table, hot, preferred_element_type=jnp.float32)
        for c in range(3):
            both = found[c * 128:(c + 1) * 128]
            acc = jnp.zeros((8, 128), jnp.float32)
            for m in range(3):
                kept = jnp.where(within == lows[m], both[:, m * 128:(m + 1) * 128], 0.0)
                acc = acc + weights[m] * jnp.sum(kept.reshape(16, 8, 128), axis=0)
            out_ref[c, t:t + 1, :] = jnp.sum(acc, axis=0, keepdims=True)


def pick(back, points):
    vmem = pl.BlockSpec(memory_space=pltpu.VMEM)
    return pl.pallas_call(
        pick_kernel,
        in_specs=[vmem] * 2,
        out_specs=vmem,
        out_shape=pltpu.VMEM((3, TILES, 128), jnp.float32),
        compiler_params=pltpu.CompilerParams(vmem_limit_bytes=10 << 20),
        name="pick",
    )(in_vmem(back), in_vmem(points))


def finish_kernel(
    back_ref, prop0_hbm, prop1_hbm, out_hbm, prop0, prop1, wide, out, sems, keep_sems,
):
    def keep(i):
        part = pl.ds(i * KB * ROWS, KB * ROWS)
        return [
            pltpu.make_async_copy(hbm.at[part], prop.at[part], keep_sems.at[h, i])
            for h, (prop, hbm) in enumerate(((prop0, prop0_hbm), (prop1, prop1_hbm)))
        ]

    def load(i, carry):
        for copy in keep(i):
            copy.start()
        return carry

    lax.fori_loop(0, LOCAL // KB, load, 0)

    def spread(i):
        rows = pl.ds(pl.multiple_of(i * KB * RUN, 8), KB * RUN)
        for h in range(2):
            for g in range(GROUP):
                gain = back_ref[h * GROUP + g, rows, :].astype(jnp.float32)
                wide[h, pl.ds(g, KB * RUN, stride=GROUP), :] = gain

    def copy(i):
        part = pl.ds(i * KB, KB)
        return pltpu.make_async_copy(out.at[part], out_hbm.at[part], sems.at[i])

    def add(i, carry):
        spread(i)
        for copy_in in keep(i):
            copy_in.wait()
        for kk in range(KB):
            k = i * KB + kk
            for h, prop in enumerate((prop0, prop1)):
                rows = pl.ds(k * ROWS, ROWS)
                out[k, :, h * 128:(h + 1) * 128] = (
                    prop[rows, :] + wide[h, kk * ROWS:(kk + 1) * ROWS, :]
                )
        copy(i).start()
        return carry

    lax.fori_loop(0, LOCAL // KB, add, 0)

    def settle(i, carry):
        copy(i).wait()
        return carry

    lax.fori_loop(0, LOCAL // KB, settle, 0)


def finish(back, prop0, prop1):
    vmem = pl.BlockSpec(memory_space=pltpu.VMEM)
    hbm = pl.BlockSpec(memory_space=pltpu.HBM)
    shape = (LOCAL, ROWS, 256)
    return pl.pallas_call(
        finish_kernel,
        in_specs=[vmem, hbm, hbm],
        out_specs=hbm,
        out_shape=pltpu.HBM(shape, jnp.float32),
        scratch_shapes=[
            pltpu.VMEM((LOCAL * ROWS, 128), jnp.float32),
            pltpu.VMEM((LOCAL * ROWS, 128), jnp.float32),
            pltpu.VMEM((2, KB * ROWS, 128), jnp.float32),
            pltpu.VMEM(shape, jnp.float32),
            pltpu.SemaphoreType.DMA((LOCAL // KB,)),
            pltpu.SemaphoreType.DMA((2, LOCAL // KB)),
        ],
        compiler_params=pltpu.CompilerParams(vmem_limit_bytes=16 << 20),
        name="finish",
    )(in_vmem(back), in_hbm(prop0), in_hbm(prop1))


def from_neighbours(low, high, axis):
    count = lax.axis_size(axis)
    ends = count - 1
    before = lax.ppermute(high, axis, [(i, (i + 1) % count) for i in range(ends)])
    after = lax.ppermute(low, axis, [((i + 1) % count, i) for i in range(ends)])
    return before, after


WIDE = 256


def water_kernel(own_ref, one_ref, two_ref, three_ref, out_ref, whole, result):
    bands = 4
    tile = own_ref.shape[1]
    width = own_ref.shape[2]
    own_cols = width - 2 * MARGIN
    band = lax.axis_index("band")
    comp = lax.axis_index("comp")
    whole[...] = jnp.zeros_like(whole)
    for d, ref in enumerate((own_ref, one_ref, two_ref, three_ref)):
        row = pl.multiple_of((band ^ d) * tile, tile)
        whole[:, pl.ds(row, tile), 0:width] = ref[...]
    shape = (bands * tile, WIDE)
    lane = lax.broadcasted_iota(jnp.int32, shape, 1)
    line = lax.broadcasted_iota(jnp.int32, shape, 0)
    col = comp * own_cols - MARGIN + lane
    inside = (col >= 0) & (col < lax.axis_size("comp") * own_cols) & (lane < width)
    first = line == 0
    last = line == shape[0] - 1

    def dx(f):
        after = jnp.where(last, 0.0, pltpu.roll(f, shape[0] - 1, 0))
        before = jnp.where(first, 0.0, pltpu.roll(f, 1, 0))
        return 0.5 * (after - before)

    def dy(f):
        return 0.5 * (pltpu.roll(f, WIDE - 1, 1) - pltpu.roll(f, 1, 1))

    sxx, sxy, syy = (jnp.where(inside, whole[3 + c], 0.0) for c in range(3))
    force_down = -forcing_gain * (dx(sxx) + dy(sxy))
    force_across = -forcing_gain * (dx(sxy) + dy(syy))
    height, down, across = (whole[c] for c in range(3))
    for _ in range(SW_STEPS):
        height = jnp.where(inside, height - wave_speed * (dx(down) + dy(across)), 0.0)
        down = jnp.where(
            inside, (1.0 - friction) * down - wave_speed * dx(height) + force_down, 0.0
        )
        across = jnp.where(
            inside, (1.0 - friction) * across - wave_speed * dy(height) + force_across, 0.0
        )
    for c, value in enumerate((height, down, across)):
        result[c] = pltpu.roll(value, WIDE - MARGIN, 1)[:, :own_cols]
        out_ref[c] = result[c, pl.ds(pl.multiple_of(band * tile, tile), tile), :]


def shallow_water(tiles):
    vmem = pl.BlockSpec(memory_space=pltpu.VMEM)
    fields, rows, width = tiles[0].shape
    own_cols = width - 2 * MARGIN
    return pl.pallas_call(
        water_kernel,
        in_specs=[vmem] * 4,
        out_specs=vmem,
        out_shape=jax.ShapeDtypeStruct((3, rows, own_cols), jnp.float32),
        scratch_shapes=[
            pltpu.VMEM((fields, 4 * rows, WIDE), jnp.float32),
            pltpu.VMEM((3, 4 * rows, own_cols), jnp.float32),
        ],
        compiler_params=pltpu.CompilerParams(vmem_limit_bytes=4 << 20),
        name="water",
    )(*map(in_vmem, tiles))


def window(spectrum, wet_mask, quad_matrix, dissipation, circulation, source_points):
    offset = lax.axis_index("comp") * LOCAL
    speed_east, speed_north, _ = component_tables(offset, LOCAL)
    speeds = jnp.stack([speed_east, speed_north])
    low, high, wetness = rims(spectrum, wet_mask)
    top, bottom = from_neighbours(low, high, "band")
    prop0, prop1, sent = propagate(speeds, spectrum, top, bottom, wetness)
    received = lax.all_to_all(sent, "comp", 0, 0, tiled=True)

    tile_rows = circulation.shape[1]
    both = jnp.concatenate([circulation, source_points.astype(jnp.float32)], axis=0)
    before, after = from_neighbours(both[:, :, :MARGIN], both[:, :, -MARGIN:], "comp")
    wide = jnp.concatenate([before, both, after], axis=2)
    left_points = before[3:].astype(jnp.int32).reshape(3, 1, 128)
    right_points = after[3:].astype(jnp.int32).reshape(3, 1, 128)
    points = jnp.concatenate([source_points, left_points, right_points], axis=1)
    points = points.reshape(3 * TILES, 128)

    full_coef = component_tables(0, K)[2]
    coef_high = full_coef.astype(jnp.bfloat16).astype(jnp.float32)
    coef_mid = (full_coef - coef_high).astype(jnp.bfloat16).astype(jnp.float32)
    coef_low = full_coef - coef_high - coef_mid
    spare = jnp.zeros((7, K), jnp.float32)
    coef = jnp.concatenate([coef_high, coef_mid, coef_low, spare]).astype(jnp.bfloat16)
    back = sources(
        received.reshape(K * RUN, 128), quad_matrix, dissipation.reshape(K // 128, 128), coef
    )
    back = lax.all_to_all(back, "comp", 0, 0, tiled=True)
    cells = pick(back, points)
    own = cells[:, :tile_rows]
    left = cells[:, tile_rows].reshape(3, tile_rows, MARGIN)
    right = cells[:, tile_rows + 1].reshape(3, tile_rows, MARGIN)
    wide_cells = jnp.concatenate([left, own, right], axis=2)
    tile = jnp.concatenate([wide[:3], wide_cells], axis=0)
    bands = lax.axis_size("band")
    tiles = [tile]
    for d in range(1, bands):
        tiles.append(lax.ppermute(tile, "band", [(i, i ^ d) for i in range(bands)]))
    spectrum_out = finish(back, prop0, prop1)
    circulation_out = shallow_water(tiles)
    return spectrum_out, circulation_out


def solution(mesh):
    in_specs = (
        P("comp", "band", None),
        P("band", None),
        P(),
        P(),
        P(None, "band", "comp"),
        P(None, "band", "comp"),
    )
    out_specs = (P("comp", "band", None), P(None, "band", "comp"))
    return jax.shard_map(window, mesh=mesh, in_specs=in_specs, out_specs=out_specs, check_vma=False)
```

```python
import math

import jax
import jax.numpy as jnp
from jax import lax
from jax.experimental import pallas as pl
from jax.experimental.pallas import tpu as pltpu
from jax.sharding import PartitionSpec as P


NF = 36
ND = 32
K = NF * ND
SUBSTEPS = 4
SRC_STEPS = 4
SW_STEPS = 8

step_source = 0.1
wave_speed = 0.35
friction = 0.05
forcing_gain = 0.15

LOCAL = 36
ROWS = 96
OWNERS = 32
GROUP = 16
RUN = 6
HALO = 4
KB = 4
PAIR = KB
MARGIN = 2 * SW_STEPS
TILES = 10


def component_tables(offset, local_count):
    indices = offset + jnp.arange(local_count, dtype=jnp.int32)
    frequency = (indices // ND).astype(jnp.float32)
    heading = (indices % ND).astype(jnp.float32)
    heading_angle = 2.0 * math.pi * (heading + 0.5) / ND
    fraction = (frequency + 0.5) / NF
    group_speed = 0.25 + 0.4 * fraction
    wave_ratio = 0.5 + 0.5 * fraction
    cosine = jnp.cos(heading_angle)
    sine_part = jnp.sin(heading_angle)
    speed_east = group_speed * cosine
    speed_north = group_speed * sine_part
    stress_coef = jnp.stack(
        [
            wave_ratio * (1.0 + cosine * cosine) - 0.5,
            wave_ratio * sine_part * cosine,
            wave_ratio * (1.0 + sine_part * sine_part) - 0.5,
        ]
    )
    return speed_east, speed_north, stress_coef


def in_hbm(array):
    return pltpu.with_memory_space_constraint(array, pltpu.HBM)


def in_vmem(array):
    return pltpu.with_memory_space_constraint(array, pltpu.VMEM)


def rim_kernel(spec_hbm, wet_hbm, low_ref, high_ref, wet_ref, begin_ref, head, tail, mask, sems):
    copies = (
        pltpu.make_async_copy(spec_hbm.at[:, 0:8, :], head, sems.at[0]),
        pltpu.make_async_copy(spec_hbm.at[:, ROWS - 8:ROWS, :], tail, sems.at[1]),
        pltpu.make_async_copy(wet_hbm, mask, sems.at[2]),
        pltpu.make_async_copy(spec_hbm.at[0:KB], begin_ref, sems.at[3]),
    )
    for copy in copies:
        copy.start()
    copies[2].wait()
    wet = mask[...].astype(jnp.float32)
    wet_ref[...] = wet
    low_ref[LOCAL] = wet[0:HALO]
    high_ref[LOCAL] = wet[ROWS - HALO:ROWS]
    copies[0].wait()
    low_ref[0:LOCAL] = head[:, 0:HALO, :]
    copies[1].wait()
    high_ref[0:LOCAL] = tail[:, 8 - HALO:8, :]
    copies[3].wait()


def rims(spectrum, wet_mask):
    cols = spectrum.shape[2]
    vmem = pl.BlockSpec(memory_space=pltpu.VMEM)
    hbm = pl.BlockSpec(memory_space=pltpu.HBM)
    return pl.pallas_call(
        rim_kernel,
        in_specs=[hbm] * 2,
        out_specs=[vmem] * 4,
        out_shape=[
            pltpu.VMEM((LOCAL + 1, HALO, cols), jnp.float32),
            pltpu.VMEM((LOCAL + 1, HALO, cols), jnp.float32),
            pltpu.VMEM((ROWS, cols), jnp.float32),
            pltpu.VMEM((KB, ROWS, cols), jnp.float32),
        ],
        scratch_shapes=[
            pltpu.VMEM((LOCAL, 8, cols), jnp.float32),
            pltpu.VMEM((LOCAL, 8, cols), jnp.float32),
            pltpu.VMEM((ROWS, cols), jnp.int32),
            pltpu.SemaphoreType.DMA((4,)),
        ],
        compiler_params=pltpu.CompilerParams(vmem_limit_bytes=4 << 20),
        name="rims",
    )(in_hbm(spectrum), in_hbm(wet_mask))


def propagate_kernel(
    speeds, spec_hbm, top_ref, bot_ref, wet_ref, begin_ref, prop0_hbm, prop1_hbm, sent_hbm,
    spec_ref, load_sems, prop0, prop1, sent_ref, wet, left_a, right_a, left_b, right_b, keep_sems, sent_sems,
):
    ext = ROWS + 2 * HALO

    def keep(i):
        part = pl.ds(i * KB * ROWS, KB * ROWS)
        return [
            pltpu.make_async_copy(prop.at[part], hbm.at[part], keep_sems.at[h, i])
            for h, (prop, hbm) in enumerate(((prop0, prop0_hbm), (prop1, prop1_hbm)))
        ]

    def give(i):
        rows = pl.ds(i * KB * RUN, KB * RUN)
        return pltpu.make_async_copy(sent_ref.at[i], sent_hbm.at[:, rows, :], sent_sems.at[i])

    def regroup(i):
        for h, prop in enumerate((prop0, prop1)):
            for g in range(GROUP):
                picked = prop[pl.ds(i * KB * ROWS + g, KB * RUN, stride=GROUP), :]
                sent_ref[i, h * GROUP + g] = picked.astype(jnp.bfloat16)

    def load(i):
        part = pl.ds(i * KB, KB)
        return pltpu.make_async_copy(spec_hbm.at[part], spec_ref.at[part], load_sems.at[i])

    def start_load(i, carry):
        load(i).start()
        return carry

    lax.fori_loop(1, LOCAL // KB, start_load, 0)
    spec_ref[0:KB] = begin_ref[...]
    wet[0:ROWS, :] = wet_ref[...]
    wet[ROWS:ROWS + HALO, :] = bot_ref[LOCAL]
    wet[ROWS + HALO:ext, :] = top_ref[LOCAL]
    lane = lax.broadcasted_iota(jnp.int32, (ext, 128), 1)
    fields = [[(left_a.at[q], right_a.at[q]), (left_b.at[q], right_b.at[q])] for q in range(PAIR)]

    def advance(first, north):
        edge = 0 if north else 127
        turn = 1 if north else 127
        ahead, a, b, c, side = [], [], [], [], []
        for q in range(PAIR):
            ax = speeds[0, first + q]
            ahead.append(jnp.where(ax >= 0.0, 7, 9))
            a.append(jnp.abs(ax))
            b.append(jnp.abs(speeds[1, first + q]))
            c.append(1.0 - a[q] - b[q])
            side.append(jnp.where(lane == edge, 0.0, b[q]))
        for s in range(SUBSTEPS):
            for q in range(PAIR):
                count = ext if s + 1 < SUBSTEPS else ROWS
                left_ref, right_ref = fields[q][s % 2]
                left, right = left_ref[8:8 + count, :], right_ref[8:8 + count, :]
                ul = left_ref[pl.ds(ahead[q], count), :]
                ur = right_ref[pl.ds(ahead[q], count), :]
                rl = pltpu.roll(left, turn, 1)
                rr = pltpu.roll(right, turn, 1)
                if north:
                    across_l = side[q][:count] * rl
                    across_r = b[q] * jnp.where(lane[:count] == 0, rl, rr)
                else:
                    across_l = b[q] * jnp.where(lane[:count] == 127, rr, rl)
                    across_r = side[q][:count] * rr
                left = wet[:count, :128] * (c[q] * left + a[q] * ul + across_l)
                right = wet[:count, 128:] * (c[q] * right + a[q] * ur + across_r)
                if s + 1 < SUBSTEPS:
                    for ref, value in zip(fields[q][(s + 1) % 2], (left, right)):
                        ref[8:8 + ext, :] = value
                        ref[7:8, :] = value[ext - 1:]
                        ref[8 + ext:9 + ext, :] = value[0:1]
                else:
                    prop0[pl.ds((first + q) * ROWS, ROWS), :] = left
                    prop1[pl.ds((first + q) * ROWS, ROWS), :] = right

    def some(i, carry):
        first = i * PAIR
        for q in range(PAIR):
            k = first + q
            for h, ref in enumerate(fields[q][0]):
                cols = slice(h * 128, (h + 1) * 128)
                top = top_ref[k, :, cols]
                ref[8:8 + ROWS, :] = spec_ref[k, :, cols]
                ref[8 + ROWS:8 + ROWS + HALO, :] = bot_ref[k, :, cols]
                ref[8 + ROWS + HALO:8 + ext, :] = top
                ref[7:8, :] = top[HALO - 1:]
                ref[8 + ext:9 + ext, :] = spec_ref[k, 0:1, cols]
        ay = speeds[1, first]

        @pl.when(ay >= 0.0)
        def _():
            advance(first, True)

        @pl.when(ay < 0.0)
        def _():
            advance(first, False)

        return carry

    def block(i, carry):
        @pl.when(i > 0)
        def _():
            load(i).wait()

        some(i, 0)
        regroup(i)
        give(i).start()
        for copy in keep(i):
            copy.start()
        return carry

    count = LOCAL // KB
    lax.fori_loop(0, count, block, 0)

    def settle(i, carry):
        for copy in keep(i):
            copy.wait()
        give(i).wait()
        return carry

    lax.fori_loop(0, count, settle, 0)


def propagate(speeds, spectrum, top, bottom, wetness, begin):
    cols = spectrum.shape[2]
    ext = ROWS + 2 * HALO
    vmem = pl.BlockSpec(memory_space=pltpu.VMEM)
    hbm = pl.BlockSpec(memory_space=pltpu.HBM)
    return pl.pallas_call(
        propagate_kernel,
        in_specs=[pl.BlockSpec(memory_space=pltpu.SMEM), hbm] + [vmem] * 4,
        out_specs=[hbm] * 3,
        out_shape=[
            pltpu.HBM((LOCAL * ROWS, 128), jnp.float32),
            pltpu.HBM((LOCAL * ROWS, 128), jnp.float32),
            pltpu.HBM((OWNERS, LOCAL * RUN, 128), jnp.bfloat16),
        ],
        scratch_shapes=[
            pltpu.VMEM((LOCAL, ROWS, cols), jnp.float32),
            pltpu.SemaphoreType.DMA((LOCAL // KB,)),
            pltpu.VMEM((LOCAL * ROWS, 128), jnp.float32),
            pltpu.VMEM((LOCAL * ROWS, 128), jnp.float32),
            pltpu.VMEM((LOCAL // KB, OWNERS, KB * RUN, 128), jnp.bfloat16),
            pltpu.VMEM((ext, cols), jnp.float32),
        ]
        + [pltpu.VMEM((PAIR, ext + 16, 128), jnp.float32)] * 4
        + [pltpu.SemaphoreType.DMA((2, LOCAL // KB)), pltpu.SemaphoreType.DMA((LOCAL // KB,))],
        compiler_params=pltpu.CompilerParams(vmem_limit_bytes=16 << 20),
        name="propagate",
    )(pltpu.with_memory_space_constraint(speeds, pltpu.SMEM), in_hbm(spectrum), *map(in_vmem, (top, bottom, wetness, begin)))


MB = 576
EB = 64
NB = 256
OWN_ROWS = RUN * LOCAL
PIECES = 3
BLOCKS = RUN * 128 // NB
BACK_ROWS = OWN_ROWS + 8 * PIECES


def source_kernel(
    recv_ref, quad_hbm, diss_ref, coef_ref, back_hbm,
    quad_ref, back_ref, prod_a, prod_b, flat, cur, xa, xb, rate, level, quad_sems, out_sem,
):
    halves = K // MB
    points = RUN * 128

    def fetch(m):
        part = pl.ds(m * MB, MB)
        return pltpu.make_async_copy(quad_hbm.at[part], quad_ref.at[part], quad_sems.at[m])

    for m in range(halves):
        fetch(m).start()

    def widen(i, carry):
        flat[pl.ds(i * K, K), :] = recv_ref[pl.ds(i * K, K), :].astype(jnp.float32)
        return carry

    lax.fori_loop(0, RUN, widen, 0)
    for i in range(K // 128):
        rate[i * 128:(i + 1) * 128, :] = jnp.broadcast_to(diss_ref[i:i + 1, :], (128, 128)).T
    coef = coef_ref[...]
    each_block = NB // 128
    stress = []
    rows_of = [[], [], []]

    def prepare(n):
        for j in range(n * each_block, (n + 1) * each_block):
            base = flat[pl.ds(j, K, stride=RUN), :]
            cols = slice(j * 128, (j + 1) * 128)
            cur[:, cols] = base
            xa[:, cols] = base.astype(jnp.bfloat16)
            level[:, cols] = jnp.sum(base, axis=0, keepdims=True)

    def multiply(s, n):
        held = (prod_a, prod_b)[(s * BLOCKS + n) % 2]
        old = (xa, xb)[s % 2]
        for m in range(halves):
            rows = slice(m * MB, (m + 1) * MB)
            held[rows, :] = jnp.dot(
                quad_ref[rows, :], old[:, n * NB:(n + 1) * NB], preferred_element_type=jnp.float32
            )

    def update(s, n):
        held = (prod_a, prod_b)[(s * BLOCKS + n) % 2]
        new = (xb, xa)[s % 2]
        cols = slice(n * NB, (n + 1) * NB)
        mean = level[:, cols] * (1.0 / K)
        sums = jnp.zeros((8, NB), jnp.float32)
        for m in range(K // EB):
            rows = slice(m * EB, (m + 1) * EB)
            each = jnp.concatenate([rate[rows, :]] * each_block, axis=1)
            now = cur[rows, cols]
            now = now + step_source * now * (held[rows, :] - each * mean)
            cur[rows, cols] = now
            if s + 1 < SRC_STEPS:
                new[rows, cols] = now.astype(jnp.bfloat16)
                sums = sums + jnp.sum(now.reshape(EB // 8, 8, NB), axis=0)
        if s + 1 < SRC_STEPS:
            level[:, cols] = jnp.sum(sums, axis=0, keepdims=True)

    def conclude(n):
        for j in range(n * each_block, (n + 1) * each_block):
            base = flat[pl.ds(j, K, stride=RUN), :]
            cols = slice(j * 128, (j + 1) * 128)
            gain = (cur[:, cols] - base).astype(jnp.bfloat16)
            xb[:, cols] = gain
            flat[pl.ds(j, K, stride=RUN), :] = gain.astype(jnp.float32)

    def weigh(n):
        both = stress[n] + jnp.dot(
            coef, xb[:, n * NB:(n + 1) * NB], preferred_element_type=jnp.float32
        )
        for c in range(3):
            row = (both[c:c + 1] + both[3 + c:4 + c] + both[6 + c:7 + c]) * (1.0 / K)
            rows_of[c] += [row[:, i * 128:(i + 1) * 128] for i in range(each_block)]

    for n in range(BLOCKS):
        prepare(n)
    for n in range(BLOCKS):
        stress.append(
            jnp.dot(coef, xa[:, n * NB:(n + 1) * NB], preferred_element_type=jnp.float32)
        )
    for m in range(halves):
        fetch(m).wait()
    turns = [(s, n) for s in range(SRC_STEPS) for n in range(BLOCKS)]
    for i, (s, n) in enumerate(turns):
        multiply(s, n)
        if i > 0:
            update(*turns[i - 1])
    update(*turns[-1])
    for n in range(BLOCKS):
        conclude(n)
    for n in range(BLOCKS):
        weigh(n)
    pieces = []
    for c in range(3):
        whole = jnp.concatenate(rows_of[c], axis=0)
        mean = jnp.sum(jnp.sum(whole, axis=0, keepdims=True), axis=1, keepdims=True)
        mean = jnp.broadcast_to(mean * (1.0 / points), (1, 128))
        high = mean.astype(jnp.bfloat16).astype(jnp.float32)
        low = (mean - high).astype(jnp.bfloat16).astype(jnp.float32)
        pieces += [whole - (high + low), high, low]
    shared = jnp.concatenate(pieces, axis=0).astype(jnp.bfloat16)

    def narrow(o, carry):
        back_ref[o, 0:OWN_ROWS, :] = flat[pl.ds(o * OWN_ROWS, OWN_ROWS), :].astype(jnp.bfloat16)
        back_ref[o, OWN_ROWS:BACK_ROWS, :] = shared
        pltpu.make_async_copy(back_ref.at[o], back_hbm.at[o], out_sem).start()
        return carry

    lax.fori_loop(0, OWNERS, narrow, 0)
    pltpu.make_async_copy(back_ref, back_hbm, out_sem).wait()


def sources(received, quad_matrix, rates, coef):
    points = RUN * 128
    vmem = pl.BlockSpec(memory_space=pltpu.VMEM)
    hbm = pl.BlockSpec(memory_space=pltpu.HBM)
    return pl.pallas_call(
        source_kernel,
        in_specs=[vmem, hbm, vmem, vmem],
        out_specs=hbm,
        out_shape=pltpu.HBM((OWNERS, BACK_ROWS, 128), jnp.bfloat16),
        scratch_shapes=[
            pltpu.VMEM((K, K), jnp.bfloat16),
            pltpu.VMEM((OWNERS, BACK_ROWS, 128), jnp.bfloat16),
            pltpu.VMEM((K, NB), jnp.float32),
            pltpu.VMEM((K, NB), jnp.float32),
            pltpu.VMEM((K * RUN, 128), jnp.float32),
            pltpu.VMEM((K, points), jnp.float32),
            pltpu.VMEM((K, points), jnp.bfloat16),
            pltpu.VMEM((K, points), jnp.bfloat16),
            pltpu.VMEM((K, 128), jnp.float32),
            pltpu.VMEM((1, points), jnp.float32),
            pltpu.SemaphoreType.DMA((K // MB,)),
            pltpu.SemaphoreType.DMA(()),
        ],
        compiler_params=pltpu.CompilerParams(vmem_limit_bytes=30 << 20),
        name="sources",
    )(in_vmem(received), in_hbm(quad_matrix), in_vmem(rates), in_vmem(coef))


def pick_kernel(back_ref, points_ref, out_ref):
    pieces = []
    for i in range(PIECES):
        at = OWN_ROWS + 8 * i
        rows = back_ref[:, at:at + 8, :].astype(jnp.float32).reshape(OWNERS * 8, 128)
        pieces.append(rows.T.astype(jnp.bfloat16))
    table = jnp.concatenate(pieces, axis=0)
    kind = lax.broadcasted_iota(jnp.int32, (8, 128), 0)
    slot = lax.broadcasted_iota(jnp.int32, (OWNERS, 8, 128), 0) * 8 + kind
    within = lax.broadcasted_iota(jnp.int32, (128, 128), 0)
    weights = (0.5, 0.3, 0.2)
    for t in range(TILES):
        hots, lows = [], []
        for m in range(3):
            p = points_ref[m * TILES + t:m * TILES + t + 1, :]
            row = p >> 8
            col = p & 255
            hi = (((col >> 7) * GROUP + (row & (GROUP - 1))) << 3) + (row >> 4)
            wanted = jnp.where(kind < RUN, hi, (hi & -8) + kind)
            taken = jnp.where(slot == wanted, 1.0, 0.0).reshape(OWNERS * 8, 128)
            hots.append(taken.astype(jnp.bfloat16))
            lows.append(col & 127)
        hot = jnp.concatenate(hots, axis=1)
        found = jnp.dot(table, hot, preferred_element_type=jnp.float32)
        for c in range(3):
            both = found[c * 128:(c + 1) * 128]
            acc = jnp.zeros((8, 128), jnp.float32)
            for m in range(3):
                kept = jnp.where(within == lows[m], both[:, m * 128:(m + 1) * 128], 0.0)
                acc = acc + weights[m] * jnp.sum(kept.reshape(16, 8, 128), axis=0)
            out_ref[c, t:t + 1, :] = jnp.sum(acc, axis=0, keepdims=True)


def pick(back, points):
    vmem = pl.BlockSpec(memory_space=pltpu.VMEM)
    return pl.pallas_call(
        pick_kernel,
        in_specs=[vmem] * 2,
        out_specs=vmem,
        out_shape=pltpu.VMEM((3, TILES, 128), jnp.float32),
        compiler_params=pltpu.CompilerParams(vmem_limit_bytes=10 << 20),
        name="pick",
    )(in_vmem(back), in_vmem(points))


def finish_kernel(
    back_ref, prop0_hbm, prop1_hbm, out_hbm, prop0, prop1, wide, out, sems, keep_sems,
):
    def keep(i):
        part = pl.ds(i * KB * ROWS, KB * ROWS)
        return [
            pltpu.make_async_copy(hbm.at[part], prop.at[part], keep_sems.at[h, i])
            for h, (prop, hbm) in enumerate(((prop0, prop0_hbm), (prop1, prop1_hbm)))
        ]

    def load(i, carry):
        for copy in keep(i):
            copy.start()
        return carry

    lax.fori_loop(0, LOCAL // KB, load, 0)

    def spread(i):
        rows = pl.ds(pl.multiple_of(i * KB * RUN, 8), KB * RUN)
        for h in range(2):
            for g in range(GROUP):
                gain = back_ref[h * GROUP + g, rows, :].astype(jnp.float32)
                wide[h, pl.ds(g, KB * RUN, stride=GROUP), :] = gain

    def copy(i):
        part = pl.ds(i * KB, KB)
        return pltpu.make_async_copy(out.at[part], out_hbm.at[part], sems.at[i])

    def add(i, carry):
        spread(i)
        for copy_in in keep(i):
            copy_in.wait()
        for kk in range(KB):
            k = i * KB + kk
            for h, prop in enumerate((prop0, prop1)):
                rows = pl.ds(k * ROWS, ROWS)
                out[k, :, h * 128:(h + 1) * 128] = (
                    prop[rows, :] + wide[h, kk * ROWS:(kk + 1) * ROWS, :]
                )
        copy(i).start()
        return carry

    lax.fori_loop(0, LOCAL // KB, add, 0)

    def settle(i, carry):
        copy(i).wait()
        return carry

    lax.fori_loop(0, LOCAL // KB, settle, 0)


def finish(back, prop0, prop1):
    vmem = pl.BlockSpec(memory_space=pltpu.VMEM)
    hbm = pl.BlockSpec(memory_space=pltpu.HBM)
    shape = (LOCAL, ROWS, 256)
    return pl.pallas_call(
        finish_kernel,
        in_specs=[vmem, hbm, hbm],
        out_specs=hbm,
        out_shape=pltpu.HBM(shape, jnp.float32),
        scratch_shapes=[
            pltpu.VMEM((LOCAL * ROWS, 128), jnp.float32),
            pltpu.VMEM((LOCAL * ROWS, 128), jnp.float32),
            pltpu.VMEM((2, KB * ROWS, 128), jnp.float32),
            pltpu.VMEM(shape, jnp.float32),
            pltpu.SemaphoreType.DMA((LOCAL // KB,)),
            pltpu.SemaphoreType.DMA((2, LOCAL // KB)),
        ],
        compiler_params=pltpu.CompilerParams(vmem_limit_bytes=16 << 20),
        name="finish",
    )(in_vmem(back), in_hbm(prop0), in_hbm(prop1))


def from_neighbours(low, high, axis):
    count = lax.axis_size(axis)
    ends = count - 1
    before = lax.ppermute(high, axis, [(i, (i + 1) % count) for i in range(ends)])
    after = lax.ppermute(low, axis, [((i + 1) % count, i) for i in range(ends)])
    return before, after


WIDE = 256


def water_kernel(own_ref, one_ref, two_ref, three_ref, out_ref, whole, result):
    bands = 4
    tile = own_ref.shape[1]
    width = own_ref.shape[2]
    own_cols = width - 2 * MARGIN
    band = lax.axis_index("band")
    comp = lax.axis_index("comp")
    whole[...] = jnp.zeros_like(whole)
    for d, ref in enumerate((own_ref, one_ref, two_ref, three_ref)):
        row = pl.multiple_of((band ^ d) * tile, tile)
        whole[:, pl.ds(row, tile), 0:width] = ref[...]
    shape = (bands * tile, WIDE)
    lane = lax.broadcasted_iota(jnp.int32, shape, 1)
    line = lax.broadcasted_iota(jnp.int32, shape, 0)
    col = comp * own_cols - MARGIN + lane
    inside = (col >= 0) & (col < lax.axis_size("comp") * own_cols) & (lane < width)
    first = line == 0
    last = line == shape[0] - 1

    def dx(f):
        after = jnp.where(last, 0.0, pltpu.roll(f, shape[0] - 1, 0))
        before = jnp.where(first, 0.0, pltpu.roll(f, 1, 0))
        return 0.5 * (after - before)

    def dy(f):
        return 0.5 * (pltpu.roll(f, WIDE - 1, 1) - pltpu.roll(f, 1, 1))

    sxx, sxy, syy = (jnp.where(inside, whole[3 + c], 0.0) for c in range(3))
    force_down = -forcing_gain * (dx(sxx) + dy(sxy))
    force_across = -forcing_gain * (dx(sxy) + dy(syy))
    height, down, across = (whole[c] for c in range(3))
    for _ in range(SW_STEPS):
        height = jnp.where(inside, height - wave_speed * (dx(down) + dy(across)), 0.0)
        down = jnp.where(
            inside, (1.0 - friction) * down - wave_speed * dx(height) + force_down, 0.0
        )
        across = jnp.where(
            inside, (1.0 - friction) * across - wave_speed * dy(height) + force_across, 0.0
        )
    for c, value in enumerate((height, down, across)):
        result[c] = pltpu.roll(value, WIDE - MARGIN, 1)[:, :own_cols]
        out_ref[c] = result[c, pl.ds(pl.multiple_of(band * tile, tile), tile), :]


def shallow_water(tiles):
    vmem = pl.BlockSpec(memory_space=pltpu.VMEM)
    fields, rows, width = tiles[0].shape
    own_cols = width - 2 * MARGIN
    return pl.pallas_call(
        water_kernel,
        in_specs=[vmem] * 4,
        out_specs=vmem,
        out_shape=jax.ShapeDtypeStruct((3, rows, own_cols), jnp.float32),
        scratch_shapes=[
            pltpu.VMEM((fields, 4 * rows, WIDE), jnp.float32),
            pltpu.VMEM((3, 4 * rows, own_cols), jnp.float32),
        ],
        compiler_params=pltpu.CompilerParams(vmem_limit_bytes=4 << 20),
        name="water",
    )(*map(in_vmem, tiles))


def window(spectrum, wet_mask, quad_matrix, dissipation, circulation, source_points):
    offset = lax.axis_index("comp") * LOCAL
    speed_east, speed_north, _ = component_tables(offset, LOCAL)
    speeds = jnp.stack([speed_east, speed_north])
    low, high, wetness, begin = rims(spectrum, wet_mask)
    top, bottom = from_neighbours(low, high, "band")
    prop0, prop1, sent = propagate(speeds, spectrum, top, bottom, wetness, begin)
    received = lax.all_to_all(sent, "comp", 0, 0, tiled=True)

    tile_rows = circulation.shape[1]
    both = jnp.concatenate([circulation, source_points.astype(jnp.float32)], axis=0)
    before, after = from_neighbours(both[:, :, :MARGIN], both[:, :, -MARGIN:], "comp")
    wide = jnp.concatenate([before, both, after], axis=2)
    left_points = before[3:].astype(jnp.int32).reshape(3, 1, 128)
    right_points = after[3:].astype(jnp.int32).reshape(3, 1, 128)
    points = jnp.concatenate([source_points, left_points, right_points], axis=1)
    points = points.reshape(3 * TILES, 128)

    full_coef = component_tables(0, K)[2]
    coef_high = full_coef.astype(jnp.bfloat16).astype(jnp.float32)
    coef_mid = (full_coef - coef_high).astype(jnp.bfloat16).astype(jnp.float32)
    coef_low = full_coef - coef_high - coef_mid
    spare = jnp.zeros((7, K), jnp.float32)
    coef = jnp.concatenate([coef_high, coef_mid, coef_low, spare]).astype(jnp.bfloat16)
    back = sources(
        received.reshape(K * RUN, 128), quad_matrix, dissipation.reshape(K // 128, 128), coef
    )
    back = lax.all_to_all(back, "comp", 0, 0, tiled=True)
    cells = pick(back, points)
    own = cells[:, :tile_rows]
    left = cells[:, tile_rows].reshape(3, tile_rows, MARGIN)
    right = cells[:, tile_rows + 1].reshape(3, tile_rows, MARGIN)
    wide_cells = jnp.concatenate([left, own, right], axis=2)
    tile = jnp.concatenate([wide[:3], wide_cells], axis=0)
    bands = lax.axis_size("band")
    tiles = [tile]
    for d in range(1, bands):
        tiles.append(lax.ppermute(tile, "band", [(i, i ^ d) for i in range(bands)]))
    spectrum_out = finish(back, prop0, prop1)
    circulation_out = shallow_water(tiles)
    return spectrum_out, circulation_out


def solution(mesh):
    in_specs = (
        P("comp", "band", None),
        P("band", None),
        P(),
        P(),
        P(None, "band", "comp"),
        P(None, "band", "comp"),
    )
    out_specs = (P("comp", "band", None), P(None, "band", "comp"))
    return jax.shard_map(window, mesh=mesh, in_specs=in_specs, out_specs=out_specs, check_vma=False)
```

```python
import math

import jax
import jax.numpy as jnp
from jax import lax
from jax.experimental import pallas as pl
from jax.experimental.pallas import tpu as pltpu
from jax.sharding import PartitionSpec as P


NF = 36
ND = 32
K = NF * ND
SUBSTEPS = 4
SRC_STEPS = 4
SW_STEPS = 8

step_source = 0.1
wave_speed = 0.35
friction = 0.05
forcing_gain = 0.15

LOCAL = 36
ROWS = 96
OWNERS = 32
GROUP = 16
RUN = 6
HALO = 4
KB = 4
PAIR = KB
EARLY = 3
MARGIN = 2 * SW_STEPS
TILES = 10


def component_tables(offset, local_count):
    indices = offset + jnp.arange(local_count, dtype=jnp.int32)
    frequency = (indices // ND).astype(jnp.float32)
    heading = (indices % ND).astype(jnp.float32)
    heading_angle = 2.0 * math.pi * (heading + 0.5) / ND
    fraction = (frequency + 0.5) / NF
    group_speed = 0.25 + 0.4 * fraction
    wave_ratio = 0.5 + 0.5 * fraction
    cosine = jnp.cos(heading_angle)
    sine_part = jnp.sin(heading_angle)
    speed_east = group_speed * cosine
    speed_north = group_speed * sine_part
    stress_coef = jnp.stack(
        [
            wave_ratio * (1.0 + cosine * cosine) - 0.5,
            wave_ratio * sine_part * cosine,
            wave_ratio * (1.0 + sine_part * sine_part) - 0.5,
        ]
    )
    return speed_east, speed_north, stress_coef


def in_hbm(array):
    return pltpu.with_memory_space_constraint(array, pltpu.HBM)


def in_vmem(array):
    return pltpu.with_memory_space_constraint(array, pltpu.VMEM)


def rim_kernel(spec_hbm, wet_hbm, low_ref, high_ref, wet_ref, begin_ref, head, tail, mask, sems):
    copies = (
        pltpu.make_async_copy(spec_hbm.at[:, 0:8, :], head, sems.at[0]),
        pltpu.make_async_copy(spec_hbm.at[:, ROWS - 8:ROWS, :], tail, sems.at[1]),
        pltpu.make_async_copy(wet_hbm, mask, sems.at[2]),
        pltpu.make_async_copy(spec_hbm.at[0:KB], begin_ref, sems.at[3]),
    )
    for copy in copies:
        copy.start()
    copies[2].wait()
    wet = mask[...].astype(jnp.float32)
    wet_ref[...] = wet
    low_ref[LOCAL] = wet[0:HALO]
    high_ref[LOCAL] = wet[ROWS - HALO:ROWS]
    copies[0].wait()
    low_ref[0:LOCAL] = head[:, 0:HALO, :]
    copies[1].wait()
    high_ref[0:LOCAL] = tail[:, 8 - HALO:8, :]
    copies[3].wait()


def rims(spectrum, wet_mask):
    cols = spectrum.shape[2]
    vmem = pl.BlockSpec(memory_space=pltpu.VMEM)
    hbm = pl.BlockSpec(memory_space=pltpu.HBM)
    return pl.pallas_call(
        rim_kernel,
        in_specs=[hbm] * 2,
        out_specs=[vmem] * 4,
        out_shape=[
            pltpu.VMEM((LOCAL + 1, HALO, cols), jnp.float32),
            pltpu.VMEM((LOCAL + 1, HALO, cols), jnp.float32),
            pltpu.VMEM((ROWS, cols), jnp.float32),
            pltpu.VMEM((KB, ROWS, cols), jnp.float32),
        ],
        scratch_shapes=[
            pltpu.VMEM((LOCAL, 8, cols), jnp.float32),
            pltpu.VMEM((LOCAL, 8, cols), jnp.float32),
            pltpu.VMEM((ROWS, cols), jnp.int32),
            pltpu.SemaphoreType.DMA((4,)),
        ],
        compiler_params=pltpu.CompilerParams(vmem_limit_bytes=4 << 20),
        name="rims",
    )(in_hbm(spectrum), in_hbm(wet_mask))


def propagate_kernel(
    speeds, spec_hbm, top_ref, bot_ref, wet_ref, begin_ref, prop0_hbm, prop1_hbm, sent_hbm,
    spec_ref, load_sems, prop0, prop1, sent_ref, wet, left_a, right_a, left_b, right_b, keep_sems, sent_sems,
):
    ext = ROWS + 2 * HALO

    def keep(i):
        part = pl.ds(i * KB * ROWS, KB * ROWS)
        return [
            pltpu.make_async_copy(prop.at[part], hbm.at[part], keep_sems.at[h, i])
            for h, (prop, hbm) in enumerate(((prop0, prop0_hbm), (prop1, prop1_hbm)))
        ]

    def give(i):
        rows = pl.ds(i * KB * RUN, KB * RUN)
        return pltpu.make_async_copy(sent_ref.at[i], sent_hbm.at[:, rows, :], sent_sems.at[i])

    def regroup(i):
        for h, prop in enumerate((prop0, prop1)):
            for g in range(GROUP):
                picked = prop[pl.ds(i * KB * ROWS + g, KB * RUN, stride=GROUP), :]
                sent_ref[i, h * GROUP + g] = picked.astype(jnp.bfloat16)

    def load(i):
        part = pl.ds(i * KB, KB)
        return pltpu.make_async_copy(spec_hbm.at[part], spec_ref.at[part], load_sems.at[i])

    def start_load(i, carry):
        load(i).start()
        return carry

    lax.fori_loop(1, LOCAL // KB, start_load, 0)
    spec_ref[0:KB] = begin_ref[...]
    wet[0:ROWS, :] = wet_ref[...]
    wet[ROWS:ROWS + HALO, :] = bot_ref[LOCAL]
    wet[ROWS + HALO:ext, :] = top_ref[LOCAL]
    lane = lax.broadcasted_iota(jnp.int32, (ext, 128), 1)
    fields = [[(left_a.at[q], right_a.at[q]), (left_b.at[q], right_b.at[q])] for q in range(PAIR)]

    def advance(first, north):
        edge = 0 if north else 127
        turn = 1 if north else 127
        ahead, a, b, c, side = [], [], [], [], []
        for q in range(PAIR):
            ax = speeds[0, first + q]
            ahead.append(jnp.where(ax >= 0.0, 7, 9))
            a.append(jnp.abs(ax))
            b.append(jnp.abs(speeds[1, first + q]))
            c.append(1.0 - a[q] - b[q])
            side.append(jnp.where(lane == edge, 0.0, b[q]))
        for s in range(SUBSTEPS):
            for q in range(PAIR):
                count = ext if s + 1 < SUBSTEPS else ROWS
                left_ref, right_ref = fields[q][s % 2]
                left, right = left_ref[8:8 + count, :], right_ref[8:8 + count, :]
                ul = left_ref[pl.ds(ahead[q], count), :]
                ur = right_ref[pl.ds(ahead[q], count), :]
                rl = pltpu.roll(left, turn, 1)
                rr = pltpu.roll(right, turn, 1)
                if north:
                    across_l = side[q][:count] * rl
                    across_r = b[q] * jnp.where(lane[:count] == 0, rl, rr)
                else:
                    across_l = b[q] * jnp.where(lane[:count] == 127, rr, rl)
                    across_r = side[q][:count] * rr
                left = wet[:count, :128] * (c[q] * left + a[q] * ul + across_l)
                right = wet[:count, 128:] * (c[q] * right + a[q] * ur + across_r)
                if s + 1 < SUBSTEPS:
                    for ref, value in zip(fields[q][(s + 1) % 2], (left, right)):
                        ref[8:8 + ext, :] = value
                        ref[7:8, :] = value[ext - 1:]
                        ref[8 + ext:9 + ext, :] = value[0:1]
                else:
                    prop0[pl.ds((first + q) * ROWS, ROWS), :] = left
                    prop1[pl.ds((first + q) * ROWS, ROWS), :] = right

    def some(i, carry):
        first = i * PAIR
        for q in range(PAIR):
            k = first + q
            for h, ref in enumerate(fields[q][0]):
                cols = slice(h * 128, (h + 1) * 128)
                top = top_ref[k, :, cols]
                ref[8:8 + ROWS, :] = spec_ref[k, :, cols]
                ref[8 + ROWS:8 + ROWS + HALO, :] = bot_ref[k, :, cols]
                ref[8 + ROWS + HALO:8 + ext, :] = top
                ref[7:8, :] = top[HALO - 1:]
                ref[8 + ext:9 + ext, :] = spec_ref[k, 0:1, cols]
        ay = speeds[1, first]

        @pl.when(ay >= 0.0)
        def _():
            advance(first, True)

        @pl.when(ay < 0.0)
        def _():
            advance(first, False)

        return carry

    def block(i, carry):
        @pl.when(i > 0)
        def _():
            load(i).wait()

        some(i, 0)
        regroup(i)
        give(i).start()
        for copy in keep(i):
            copy.start()
        return carry

    count = LOCAL // KB
    lax.fori_loop(0, count, block, 0)

    def settle(i, carry):
        for copy in keep(i):
            copy.wait()
        give(i).wait()
        return carry

    lax.fori_loop(0, count, settle, 0)


def propagate(speeds, spectrum, top, bottom, wetness, begin):
    cols = spectrum.shape[2]
    ext = ROWS + 2 * HALO
    vmem = pl.BlockSpec(memory_space=pltpu.VMEM)
    hbm = pl.BlockSpec(memory_space=pltpu.HBM)
    return pl.pallas_call(
        propagate_kernel,
        in_specs=[pl.BlockSpec(memory_space=pltpu.SMEM), hbm] + [vmem] * 4,
        out_specs=[hbm] * 3,
        out_shape=[
            pltpu.HBM((LOCAL * ROWS, 128), jnp.float32),
            pltpu.HBM((LOCAL * ROWS, 128), jnp.float32),
            pltpu.HBM((OWNERS, LOCAL * RUN, 128), jnp.bfloat16),
        ],
        scratch_shapes=[
            pltpu.VMEM((LOCAL, ROWS, cols), jnp.float32),
            pltpu.SemaphoreType.DMA((LOCAL // KB,)),
            pltpu.VMEM((LOCAL * ROWS, 128), jnp.float32),
            pltpu.VMEM((LOCAL * ROWS, 128), jnp.float32),
            pltpu.VMEM((LOCAL // KB, OWNERS, KB * RUN, 128), jnp.bfloat16),
            pltpu.VMEM((ext, cols), jnp.float32),
        ]
        + [pltpu.VMEM((PAIR, ext + 16, 128), jnp.float32)] * 4
        + [pltpu.SemaphoreType.DMA((2, LOCAL // KB)), pltpu.SemaphoreType.DMA((LOCAL // KB,))],
        compiler_params=pltpu.CompilerParams(vmem_limit_bytes=16 << 20),
        name="propagate",
    )(pltpu.with_memory_space_constraint(speeds, pltpu.SMEM), in_hbm(spectrum), *map(in_vmem, (top, bottom, wetness, begin)))


MB = 576
EB = 64
NB = 256
OWN_ROWS = RUN * LOCAL
PIECES = 3
BLOCKS = RUN * 128 // NB
BACK_ROWS = OWN_ROWS + 8 * PIECES


def source_kernel(
    recv_ref, quad_hbm, diss_ref, coef_ref, back_hbm,
    quad_ref, back_ref, prod_a, prod_b, flat, cur, xa, xb, rate, level, quad_sems, out_sem,
):
    halves = K // MB
    points = RUN * 128

    def fetch(m):
        part = pl.ds(m * MB, MB)
        return pltpu.make_async_copy(quad_hbm.at[part], quad_ref.at[part], quad_sems.at[m])

    for m in range(halves):
        fetch(m).start()

    def widen(i, carry):
        flat[pl.ds(i * K, K), :] = recv_ref[pl.ds(i * K, K), :].astype(jnp.float32)
        return carry

    lax.fori_loop(0, RUN, widen, 0)
    for i in range(K // 128):
        rate[i * 128:(i + 1) * 128, :] = jnp.broadcast_to(diss_ref[i:i + 1, :], (128, 128)).T
    coef = coef_ref[...]
    each_block = NB // 128
    stress = []
    rows_of = [[], [], []]

    def prepare(n):
        for j in range(n * each_block, (n + 1) * each_block):
            base = flat[pl.ds(j, K, stride=RUN), :]
            cols = slice(j * 128, (j + 1) * 128)
            cur[:, cols] = base
            xa[:, cols] = base.astype(jnp.bfloat16)
            level[:, cols] = jnp.sum(base, axis=0, keepdims=True)

    def multiply(s, n):
        held = (prod_a, prod_b)[(s * BLOCKS + n) % 2]
        old = (xa, xb)[s % 2]
        for m in range(halves):
            rows = slice(m * MB, (m + 1) * MB)
            held[rows, :] = jnp.dot(
                quad_ref[rows, :], old[:, n * NB:(n + 1) * NB], preferred_element_type=jnp.float32
            )

    def update(s, n):
        held = (prod_a, prod_b)[(s * BLOCKS + n) % 2]
        new = (xb, xa)[s % 2]
        cols = slice(n * NB, (n + 1) * NB)
        mean = level[:, cols] * (1.0 / K)
        sums = jnp.zeros((8, NB), jnp.float32)
        for m in range(K // EB):
            rows = slice(m * EB, (m + 1) * EB)
            each = jnp.concatenate([rate[rows, :]] * each_block, axis=1)
            now = cur[rows, cols]
            now = now + step_source * now * (held[rows, :] - each * mean)
            cur[rows, cols] = now
            if s + 1 < SRC_STEPS:
                new[rows, cols] = now.astype(jnp.bfloat16)
                sums = sums + jnp.sum(now.reshape(EB // 8, 8, NB), axis=0)
        if s + 1 < SRC_STEPS:
            level[:, cols] = jnp.sum(sums, axis=0, keepdims=True)

    def conclude(n):
        for j in range(n * each_block, (n + 1) * each_block):
            base = flat[pl.ds(j, K, stride=RUN), :]
            cols = slice(j * 128, (j + 1) * 128)
            gain = (cur[:, cols] - base).astype(jnp.bfloat16)
            xb[:, cols] = gain
            flat[pl.ds(j, K, stride=RUN), :] = gain.astype(jnp.float32)

    def weigh(n):
        both = stress[n] + jnp.dot(
            coef, xb[:, n * NB:(n + 1) * NB], preferred_element_type=jnp.float32
        )
        for c in range(3):
            row = (both[c:c + 1] + both[3 + c:4 + c] + both[6 + c:7 + c]) * (1.0 / K)
            rows_of[c] += [row[:, i * 128:(i + 1) * 128] for i in range(each_block)]

    for n in range(BLOCKS):
        prepare(n)
    for n in range(BLOCKS):
        stress.append(
            jnp.dot(coef, xa[:, n * NB:(n + 1) * NB], preferred_element_type=jnp.float32)
        )
    for m in range(halves):
        fetch(m).wait()
    turns = [(s, n) for s in range(SRC_STEPS) for n in range(BLOCKS)]
    for i, (s, n) in enumerate(turns):
        multiply(s, n)
        if i > 0:
            update(*turns[i - 1])
    update(*turns[-1])
    for n in range(BLOCKS):
        conclude(n)
    for n in range(BLOCKS):
        weigh(n)
    pieces = []
    for c in range(3):
        whole = jnp.concatenate(rows_of[c], axis=0)
        mean = jnp.sum(jnp.sum(whole, axis=0, keepdims=True), axis=1, keepdims=True)
        mean = jnp.broadcast_to(mean * (1.0 / points), (1, 128))
        high = mean.astype(jnp.bfloat16).astype(jnp.float32)
        low = (mean - high).astype(jnp.bfloat16).astype(jnp.float32)
        pieces += [whole - (high + low), high, low]
    shared = jnp.concatenate(pieces, axis=0).astype(jnp.bfloat16)

    def narrow(o, carry):
        back_ref[o, 0:OWN_ROWS, :] = flat[pl.ds(o * OWN_ROWS, OWN_ROWS), :].astype(jnp.bfloat16)
        back_ref[o, OWN_ROWS:BACK_ROWS, :] = shared
        pltpu.make_async_copy(back_ref.at[o], back_hbm.at[o], out_sem).start()
        return carry

    lax.fori_loop(0, OWNERS, narrow, 0)
    pltpu.make_async_copy(back_ref, back_hbm, out_sem).wait()


def sources(received, quad_matrix, rates, coef):
    points = RUN * 128
    vmem = pl.BlockSpec(memory_space=pltpu.VMEM)
    hbm = pl.BlockSpec(memory_space=pltpu.HBM)
    return pl.pallas_call(
        source_kernel,
        in_specs=[vmem, hbm, vmem, vmem],
        out_specs=hbm,
        out_shape=pltpu.HBM((OWNERS, BACK_ROWS, 128), jnp.bfloat16),
        scratch_shapes=[
            pltpu.VMEM((K, K), jnp.bfloat16),
            pltpu.VMEM((OWNERS, BACK_ROWS, 128), jnp.bfloat16),
            pltpu.VMEM((K, NB), jnp.float32),
            pltpu.VMEM((K, NB), jnp.float32),
            pltpu.VMEM((K * RUN, 128), jnp.float32),
            pltpu.VMEM((K, points), jnp.float32),
            pltpu.VMEM((K, points), jnp.bfloat16),
            pltpu.VMEM((K, points), jnp.bfloat16),
            pltpu.VMEM((K, 128), jnp.float32),
            pltpu.VMEM((1, points), jnp.float32),
            pltpu.SemaphoreType.DMA((K // MB,)),
            pltpu.SemaphoreType.DMA(()),
        ],
        compiler_params=pltpu.CompilerParams(vmem_limit_bytes=30 << 20),
        name="sources",
    )(in_vmem(received), in_hbm(quad_matrix), in_vmem(rates), in_vmem(coef))


def pick_kernel(
    back_ref, points_ref, prop0_hbm, prop1_hbm, out_ref, early0, early1, sems
):
    rows = pl.ds(0, EARLY * KB * ROWS)
    copies = (
        pltpu.make_async_copy(prop0_hbm.at[rows], early0, sems.at[0]),
        pltpu.make_async_copy(prop1_hbm.at[rows], early1, sems.at[1]),
    )
    for copy in copies:
        copy.start()
    pieces = []
    for i in range(PIECES):
        at = OWN_ROWS + 8 * i
        rows = back_ref[:, at:at + 8, :].astype(jnp.float32).reshape(OWNERS * 8, 128)
        pieces.append(rows.T.astype(jnp.bfloat16))
    table = jnp.concatenate(pieces, axis=0)
    kind = lax.broadcasted_iota(jnp.int32, (8, 128), 0)
    slot = lax.broadcasted_iota(jnp.int32, (OWNERS, 8, 128), 0) * 8 + kind
    within = lax.broadcasted_iota(jnp.int32, (128, 128), 0)
    weights = (0.5, 0.3, 0.2)
    for t in range(TILES):
        hots, lows = [], []
        for m in range(3):
            p = points_ref[m * TILES + t:m * TILES + t + 1, :]
            row = p >> 8
            col = p & 255
            hi = (((col >> 7) * GROUP + (row & (GROUP - 1))) << 3) + (row >> 4)
            wanted = jnp.where(kind < RUN, hi, (hi & -8) + kind)
            taken = jnp.where(slot == wanted, 1.0, 0.0).reshape(OWNERS * 8, 128)
            hots.append(taken.astype(jnp.bfloat16))
            lows.append(col & 127)
        hot = jnp.concatenate(hots, axis=1)
        found = jnp.dot(table, hot, preferred_element_type=jnp.float32)
        for c in range(3):
            both = found[c * 128:(c + 1) * 128]
            acc = jnp.zeros((8, 128), jnp.float32)
            for m in range(3):
                kept = jnp.where(within == lows[m], both[:, m * 128:(m + 1) * 128], 0.0)
                acc = acc + weights[m] * jnp.sum(kept.reshape(16, 8, 128), axis=0)
            out_ref[c, t:t + 1, :] = jnp.sum(acc, axis=0, keepdims=True)
    for copy in copies:
        copy.wait()


def pick(back, points, prop0, prop1):
    vmem = pl.BlockSpec(memory_space=pltpu.VMEM)
    hbm = pl.BlockSpec(memory_space=pltpu.HBM)
    early = pltpu.VMEM((EARLY * KB * ROWS, 128), jnp.float32)
    return pl.pallas_call(
        pick_kernel,
        in_specs=[vmem, vmem, hbm, hbm],
        out_specs=[vmem] * 3,
        out_shape=[pltpu.VMEM((3, TILES, 128), jnp.float32), early, early],
        scratch_shapes=[pltpu.SemaphoreType.DMA((2,))],
        compiler_params=pltpu.CompilerParams(vmem_limit_bytes=10 << 20),
        name="pick",
    )(in_vmem(back), in_vmem(points), in_hbm(prop0), in_hbm(prop1))


def finish_kernel(
    back_ref, early0, early1, prop0_hbm, prop1_hbm, out_hbm,
    prop0, prop1, wide, out, sems, keep_sems,
):
    def keep(i):
        part = pl.ds(i * KB * ROWS, KB * ROWS)
        return [
            pltpu.make_async_copy(hbm.at[part], prop.at[part], keep_sems.at[h, i])
            for h, (prop, hbm) in enumerate(((prop0, prop0_hbm), (prop1, prop1_hbm)))
        ]

    def load(i, carry):
        for copy in keep(i):
            copy.start()
        return carry

    lax.fori_loop(EARLY, LOCAL // KB, load, 0)

    def spread(i):
        rows = pl.ds(pl.multiple_of(i * KB * RUN, 8), KB * RUN)
        for h in range(2):
            for g in range(GROUP):
                gain = back_ref[h * GROUP + g, rows, :].astype(jnp.float32)
                wide[h, pl.ds(g, KB * RUN, stride=GROUP), :] = gain

    def copy(i):
        part = pl.ds(i * KB, KB)
        return pltpu.make_async_copy(out.at[part], out_hbm.at[part], sems.at[i])

    def add(i, halves):
        for kk in range(KB):
            k = i * KB + kk
            for h, prop in enumerate(halves):
                rows = pl.ds(k * ROWS, ROWS)
                out[k, :, h * 128:(h + 1) * 128] = (
                    prop[rows, :] + wide[h, kk * ROWS:(kk + 1) * ROWS, :]
                )
        copy(i).start()

    def add_early(i, carry):
        spread(i)
        add(i, (early0, early1))
        return carry

    def add_late(i, carry):
        spread(i)
        for copy_in in keep(i):
            copy_in.wait()
        add(i, (prop0, prop1))
        return carry

    lax.fori_loop(0, EARLY, add_early, 0)
    lax.fori_loop(EARLY, LOCAL // KB, add_late, 0)

    def settle(i, carry):
        copy(i).wait()
        return carry

    lax.fori_loop(0, LOCAL // KB, settle, 0)


def finish(back, early0, early1, prop0, prop1):
    vmem = pl.BlockSpec(memory_space=pltpu.VMEM)
    hbm = pl.BlockSpec(memory_space=pltpu.HBM)
    shape = (LOCAL, ROWS, 256)
    return pl.pallas_call(
        finish_kernel,
        in_specs=[vmem, vmem, vmem, hbm, hbm],
        out_specs=hbm,
        out_shape=pltpu.HBM(shape, jnp.float32),
        scratch_shapes=[
            pltpu.VMEM((LOCAL * ROWS, 128), jnp.float32),
            pltpu.VMEM((LOCAL * ROWS, 128), jnp.float32),
            pltpu.VMEM((2, KB * ROWS, 128), jnp.float32),
            pltpu.VMEM(shape, jnp.float32),
            pltpu.SemaphoreType.DMA((LOCAL // KB,)),
            pltpu.SemaphoreType.DMA((2, LOCAL // KB)),
        ],
        compiler_params=pltpu.CompilerParams(vmem_limit_bytes=16 << 20),
        name="finish",
    )(*map(in_vmem, (back, early0, early1)), in_hbm(prop0), in_hbm(prop1))


def from_neighbours(low, high, axis):
    count = lax.axis_size(axis)
    ends = count - 1
    before = lax.ppermute(high, axis, [(i, (i + 1) % count) for i in range(ends)])
    after = lax.ppermute(low, axis, [((i + 1) % count, i) for i in range(ends)])
    return before, after


WIDE = 256


def water_kernel(own_ref, one_ref, two_ref, three_ref, out_ref, whole, result):
    bands = 4
    tile = own_ref.shape[1]
    width = own_ref.shape[2]
    own_cols = width - 2 * MARGIN
    band = lax.axis_index("band")
    comp = lax.axis_index("comp")
    whole[...] = jnp.zeros_like(whole)
    for d, ref in enumerate((own_ref, one_ref, two_ref, three_ref)):
        row = pl.multiple_of((band ^ d) * tile, tile)
        whole[:, pl.ds(row, tile), 0:width] = ref[...]
    shape = (bands * tile, WIDE)
    lane = lax.broadcasted_iota(jnp.int32, shape, 1)
    line = lax.broadcasted_iota(jnp.int32, shape, 0)
    col = comp * own_cols - MARGIN + lane
    inside = (col >= 0) & (col < lax.axis_size("comp") * own_cols) & (lane < width)
    first = line == 0
    last = line == shape[0] - 1

    def dx(f):
        after = jnp.where(last, 0.0, pltpu.roll(f, shape[0] - 1, 0))
        before = jnp.where(first, 0.0, pltpu.roll(f, 1, 0))
        return 0.5 * (after - before)

    def dy(f):
        return 0.5 * (pltpu.roll(f, WIDE - 1, 1) - pltpu.roll(f, 1, 1))

    sxx, sxy, syy = (jnp.where(inside, whole[3 + c], 0.0) for c in range(3))
    force_down = -forcing_gain * (dx(sxx) + dy(sxy))
    force_across = -forcing_gain * (dx(sxy) + dy(syy))
    height, down, across = (whole[c] for c in range(3))
    for _ in range(SW_STEPS):
        height = jnp.where(inside, height - wave_speed * (dx(down) + dy(across)), 0.0)
        down = jnp.where(
            inside, (1.0 - friction) * down - wave_speed * dx(height) + force_down, 0.0
        )
        across = jnp.where(
            inside, (1.0 - friction) * across - wave_speed * dy(height) + force_across, 0.0
        )
    for c, value in enumerate((height, down, across)):
        result[c] = pltpu.roll(value, WIDE - MARGIN, 1)[:, :own_cols]
        out_ref[c] = result[c, pl.ds(pl.multiple_of(band * tile, tile), tile), :]


def shallow_water(tiles):
    vmem = pl.BlockSpec(memory_space=pltpu.VMEM)
    fields, rows, width = tiles[0].shape
    own_cols = width - 2 * MARGIN
    return pl.pallas_call(
        water_kernel,
        in_specs=[vmem] * 4,
        out_specs=vmem,
        out_shape=jax.ShapeDtypeStruct((3, rows, own_cols), jnp.float32),
        scratch_shapes=[
            pltpu.VMEM((fields, 4 * rows, WIDE), jnp.float32),
            pltpu.VMEM((3, 4 * rows, own_cols), jnp.float32),
        ],
        compiler_params=pltpu.CompilerParams(vmem_limit_bytes=4 << 20),
        name="water",
    )(*map(in_vmem, tiles))


def window(spectrum, wet_mask, quad_matrix, dissipation, circulation, source_points):
    offset = lax.axis_index("comp") * LOCAL
    speed_east, speed_north, _ = component_tables(offset, LOCAL)
    speeds = jnp.stack([speed_east, speed_north])
    low, high, wetness, begin = rims(spectrum, wet_mask)
    top, bottom = from_neighbours(low, high, "band")
    prop0, prop1, sent = propagate(speeds, spectrum, top, bottom, wetness, begin)
    received = lax.all_to_all(sent, "comp", 0, 0, tiled=True)

    tile_rows = circulation.shape[1]
    both = jnp.concatenate([circulation, source_points.astype(jnp.float32)], axis=0)
    before, after = from_neighbours(both[:, :, :MARGIN], both[:, :, -MARGIN:], "comp")
    wide = jnp.concatenate([before, both, after], axis=2)
    left_points = before[3:].astype(jnp.int32).reshape(3, 1, 128)
    right_points = after[3:].astype(jnp.int32).reshape(3, 1, 128)
    points = jnp.concatenate([source_points, left_points, right_points], axis=1)
    points = points.reshape(3 * TILES, 128)

    full_coef = component_tables(0, K)[2]
    coef_high = full_coef.astype(jnp.bfloat16).astype(jnp.float32)
    coef_mid = (full_coef - coef_high).astype(jnp.bfloat16).astype(jnp.float32)
    coef_low = full_coef - coef_high - coef_mid
    spare = jnp.zeros((7, K), jnp.float32)
    coef = jnp.concatenate([coef_high, coef_mid, coef_low, spare]).astype(jnp.bfloat16)
    back = sources(
        received.reshape(K * RUN, 128), quad_matrix, dissipation.reshape(K // 128, 128), coef
    )
    back = lax.all_to_all(back, "comp", 0, 0, tiled=True)
    cells, early0, early1 = pick(back, points, prop0, prop1)
    own = cells[:, :tile_rows]
    left = cells[:, tile_rows].reshape(3, tile_rows, MARGIN)
    right = cells[:, tile_rows + 1].reshape(3, tile_rows, MARGIN)
    wide_cells = jnp.concatenate([left, own, right], axis=2)
    tile = jnp.concatenate([wide[:3], wide_cells], axis=0)
    bands = lax.axis_size("band")
    tiles = [tile]
    for d in range(1, bands):
        tiles.append(lax.ppermute(tile, "band", [(i, i ^ d) for i in range(bands)]))
    spectrum_out = finish(back, early0, early1, prop0, prop1)
    circulation_out = shallow_water(tiles)
    return spectrum_out, circulation_out


def solution(mesh):
    in_specs = (
        P("comp", "band", None),
        P("band", None),
        P(),
        P(),
        P(None, "band", "comp"),
        P(None, "band", "comp"),
    )
    out_specs = (P("comp", "band", None), P(None, "band", "comp"))
    return jax.shard_map(window, mesh=mesh, in_specs=in_specs, out_specs=out_specs, check_vma=False)
```

```python
import math

import jax
import jax.numpy as jnp
from jax import lax
from jax.experimental import pallas as pl
from jax.experimental.pallas import tpu as pltpu
from jax.sharding import PartitionSpec as P


NF = 36
ND = 32
K = NF * ND
SUBSTEPS = 4
SRC_STEPS = 4
SW_STEPS = 8

step_source = 0.1
wave_speed = 0.35
friction = 0.05
forcing_gain = 0.15

LOCAL = 36
ROWS = 96
OWNERS = 32
GROUP = 16
RUN = 6
HALO = 4
KB = 4
PAIR = KB
EARLY = 3
MARGIN = 2 * SW_STEPS
TILES = 10


def component_tables(offset, local_count):
    indices = offset + jnp.arange(local_count, dtype=jnp.int32)
    frequency = (indices // ND).astype(jnp.float32)
    heading = (indices % ND).astype(jnp.float32)
    heading_angle = 2.0 * math.pi * (heading + 0.5) / ND
    fraction = (frequency + 0.5) / NF
    group_speed = 0.25 + 0.4 * fraction
    wave_ratio = 0.5 + 0.5 * fraction
    cosine = jnp.cos(heading_angle)
    sine_part = jnp.sin(heading_angle)
    speed_east = group_speed * cosine
    speed_north = group_speed * sine_part
    stress_coef = jnp.stack(
        [
            wave_ratio * (1.0 + cosine * cosine) - 0.5,
            wave_ratio * sine_part * cosine,
            wave_ratio * (1.0 + sine_part * sine_part) - 0.5,
        ]
    )
    return speed_east, speed_north, stress_coef


def in_hbm(array):
    return pltpu.with_memory_space_constraint(array, pltpu.HBM)


def in_vmem(array):
    return pltpu.with_memory_space_constraint(array, pltpu.VMEM)


def rim_kernel(spec_hbm, wet_hbm, low_ref, high_ref, wet_ref, begin_ref, head, tail, mask, sems):
    copies = (
        pltpu.make_async_copy(spec_hbm.at[:, 0:8, :], head, sems.at[0]),
        pltpu.make_async_copy(spec_hbm.at[:, ROWS - 8:ROWS, :], tail, sems.at[1]),
        pltpu.make_async_copy(wet_hbm, mask, sems.at[2]),
        pltpu.make_async_copy(spec_hbm.at[0:KB], begin_ref, sems.at[3]),
    )
    for copy in copies:
        copy.start()
    copies[2].wait()
    wet = mask[...].astype(jnp.float32)
    wet_ref[...] = wet
    low_ref[LOCAL] = wet[0:HALO]
    high_ref[LOCAL] = wet[ROWS - HALO:ROWS]
    copies[0].wait()
    low_ref[0:LOCAL] = head[:, 0:HALO, :]
    copies[1].wait()
    high_ref[0:LOCAL] = tail[:, 8 - HALO:8, :]
    copies[3].wait()


def rims(spectrum, wet_mask):
    cols = spectrum.shape[2]
    vmem = pl.BlockSpec(memory_space=pltpu.VMEM)
    hbm = pl.BlockSpec(memory_space=pltpu.HBM)
    return pl.pallas_call(
        rim_kernel,
        in_specs=[hbm] * 2,
        out_specs=[vmem] * 4,
        out_shape=[
            pltpu.VMEM((LOCAL + 1, HALO, cols), jnp.float32),
            pltpu.VMEM((LOCAL + 1, HALO, cols), jnp.float32),
            pltpu.VMEM((ROWS, cols), jnp.float32),
            pltpu.VMEM((KB, ROWS, cols), jnp.float32),
        ],
        scratch_shapes=[
            pltpu.VMEM((LOCAL, 8, cols), jnp.float32),
            pltpu.VMEM((LOCAL, 8, cols), jnp.float32),
            pltpu.VMEM((ROWS, cols), jnp.int32),
            pltpu.SemaphoreType.DMA((4,)),
        ],
        compiler_params=pltpu.CompilerParams(vmem_limit_bytes=4 << 20),
        name="rims",
    )(in_hbm(spectrum), in_hbm(wet_mask))


def propagate_kernel(
    speeds, spec_hbm, top_ref, bot_ref, wet_ref, begin_ref, prop0_hbm, prop1_hbm, sent_hbm,
    spec_ref, load_sems, prop0, prop1, sent_ref, wet, left_a, right_a, left_b, right_b, keep_sems, sent_sems,
):
    ext = ROWS + 2 * HALO

    def keep(i):
        part = pl.ds(i * KB * ROWS, KB * ROWS)
        return [
            pltpu.make_async_copy(prop.at[part], hbm.at[part], keep_sems.at[h, i])
            for h, (prop, hbm) in enumerate(((prop0, prop0_hbm), (prop1, prop1_hbm)))
        ]

    def give(i):
        rows = pl.ds(i * KB * RUN, KB * RUN)
        return pltpu.make_async_copy(sent_ref.at[i], sent_hbm.at[:, rows, :], sent_sems.at[i])

    def regroup(i):
        for h, prop in enumerate((prop0, prop1)):
            for g in range(GROUP):
                picked = prop[pl.ds(i * KB * ROWS + g, KB * RUN, stride=GROUP), :]
                sent_ref[i, h * GROUP + g] = picked.astype(jnp.bfloat16)

    def load(i):
        part = pl.ds(i * KB, KB)
        return pltpu.make_async_copy(spec_hbm.at[part], spec_ref.at[part], load_sems.at[i])

    def start_load(i, carry):
        load(i).start()
        return carry

    lax.fori_loop(1, LOCAL // KB, start_load, 0)
    spec_ref[0:KB] = begin_ref[...]
    wet[0:ROWS, :] = wet_ref[...]
    wet[ROWS:ROWS + HALO, :] = bot_ref[LOCAL]
    wet[ROWS + HALO:ext, :] = top_ref[LOCAL]
    lane = lax.broadcasted_iota(jnp.int32, (ext, 128), 1)
    fields = [[(left_a.at[q], right_a.at[q]), (left_b.at[q], right_b.at[q])] for q in range(PAIR)]

    def advance(first, north):
        edge = 0 if north else 127
        turn = 1 if north else 127
        ahead, a, b, c, side = [], [], [], [], []
        for q in range(PAIR):
            ax = speeds[0, first + q]
            ahead.append(jnp.where(ax >= 0.0, 7, 9))
            a.append(jnp.abs(ax))
            b.append(jnp.abs(speeds[1, first + q]))
            c.append(1.0 - a[q] - b[q])
            side.append(jnp.where(lane == edge, 0.0, b[q]))
        for s in range(SUBSTEPS):
            for q in range(PAIR):
                count = ext if s + 1 < SUBSTEPS else ROWS
                left_ref, right_ref = fields[q][s % 2]
                left, right = left_ref[8:8 + count, :], right_ref[8:8 + count, :]
                ul = left_ref[pl.ds(ahead[q], count), :]
                ur = right_ref[pl.ds(ahead[q], count), :]
                rl = pltpu.roll(left, turn, 1)
                rr = pltpu.roll(right, turn, 1)
                if north:
                    across_l = side[q][:count] * rl
                    across_r = b[q] * jnp.where(lane[:count] == 0, rl, rr)
                else:
                    across_l = b[q] * jnp.where(lane[:count] == 127, rr, rl)
                    across_r = side[q][:count] * rr
                left = wet[:count, :128] * (c[q] * left + a[q] * ul + across_l)
                right = wet[:count, 128:] * (c[q] * right + a[q] * ur + across_r)
                if s + 1 < SUBSTEPS:
                    for ref, value in zip(fields[q][(s + 1) % 2], (left, right)):
                        ref[8:8 + ext, :] = value
                        ref[7:8, :] = value[ext - 1:]
                        ref[8 + ext:9 + ext, :] = value[0:1]
                else:
                    prop0[pl.ds((first + q) * ROWS, ROWS), :] = left
                    prop1[pl.ds((first + q) * ROWS, ROWS), :] = right

    def some(i, carry):
        first = i * PAIR
        for q in range(PAIR):
            k = first + q
            for h, ref in enumerate(fields[q][0]):
                cols = slice(h * 128, (h + 1) * 128)
                top = top_ref[k, :, cols]
                ref[8:8 + ROWS, :] = spec_ref[k, :, cols]
                ref[8 + ROWS:8 + ROWS + HALO, :] = bot_ref[k, :, cols]
                ref[8 + ROWS + HALO:8 + ext, :] = top
                ref[7:8, :] = top[HALO - 1:]
                ref[8 + ext:9 + ext, :] = spec_ref[k, 0:1, cols]
        ay = speeds[1, first]

        @pl.when(ay >= 0.0)
        def _():
            advance(first, True)

        @pl.when(ay < 0.0)
        def _():
            advance(first, False)

        return carry

    def block(i, carry):
        @pl.when(i > 0)
        def _():
            load(i).wait()

        some(i, 0)
        regroup(i)
        give(i).start()
        for copy in keep(i):
            copy.start()
        return carry

    count = LOCAL // KB
    lax.fori_loop(0, count, block, 0)

    def settle(i, carry):
        for copy in keep(i):
            copy.wait()
        give(i).wait()
        return carry

    lax.fori_loop(0, count, settle, 0)


def propagate(speeds, spectrum, top, bottom, wetness, begin):
    cols = spectrum.shape[2]
    ext = ROWS + 2 * HALO
    vmem = pl.BlockSpec(memory_space=pltpu.VMEM)
    hbm = pl.BlockSpec(memory_space=pltpu.HBM)
    return pl.pallas_call(
        propagate_kernel,
        in_specs=[pl.BlockSpec(memory_space=pltpu.SMEM), hbm] + [vmem] * 4,
        out_specs=[hbm] * 3,
        out_shape=[
            pltpu.HBM((LOCAL * ROWS, 128), jnp.float32),
            pltpu.HBM((LOCAL * ROWS, 128), jnp.float32),
            pltpu.HBM((OWNERS, LOCAL * RUN, 128), jnp.bfloat16),
        ],
        scratch_shapes=[
            pltpu.VMEM((LOCAL, ROWS, cols), jnp.float32),
            pltpu.SemaphoreType.DMA((LOCAL // KB,)),
            pltpu.VMEM((LOCAL * ROWS, 128), jnp.float32),
            pltpu.VMEM((LOCAL * ROWS, 128), jnp.float32),
            pltpu.VMEM((LOCAL // KB, OWNERS, KB * RUN, 128), jnp.bfloat16),
            pltpu.VMEM((ext, cols), jnp.float32),
        ]
        + [pltpu.VMEM((PAIR, ext + 16, 128), jnp.float32)] * 4
        + [pltpu.SemaphoreType.DMA((2, LOCAL // KB)), pltpu.SemaphoreType.DMA((LOCAL // KB,))],
        compiler_params=pltpu.CompilerParams(vmem_limit_bytes=16 << 20),
        name="propagate",
    )(pltpu.with_memory_space_constraint(speeds, pltpu.SMEM), in_hbm(spectrum), *map(in_vmem, (top, bottom, wetness, begin)))


MB = 576
EB = 64
NB = 256
OWN_ROWS = RUN * LOCAL
PIECES = 3
BLOCKS = RUN * 128 // NB
BACK_ROWS = OWN_ROWS + 8 * PIECES


def source_kernel(
    recv_ref, quad_hbm, diss_ref, coef_ref, back_hbm,
    quad_ref, back_ref, prod_a, prod_b, flat, cur, xa, xb, rate, level, quad_sems, out_sem,
):
    halves = K // MB
    points = RUN * 128

    def fetch(m):
        part = pl.ds(m * MB, MB)
        return pltpu.make_async_copy(quad_hbm.at[part], quad_ref.at[part], quad_sems.at[m])

    for m in range(halves):
        fetch(m).start()

    def widen(i, carry):
        flat[pl.ds(i * K, K), :] = recv_ref[pl.ds(i * K, K), :].astype(jnp.float32)
        return carry

    lax.fori_loop(0, RUN, widen, 0)
    for i in range(K // 128):
        rate[i * 128:(i + 1) * 128, :] = jnp.broadcast_to(diss_ref[i:i + 1, :], (128, 128)).T
    coef = coef_ref[...]
    each_block = NB // 128
    stress = []
    rows_of = [[], [], []]

    def prepare(n):
        for j in range(n * each_block, (n + 1) * each_block):
            base = flat[pl.ds(j, K, stride=RUN), :]
            cols = slice(j * 128, (j + 1) * 128)
            cur[:, cols] = base
            xa[:, cols] = base.astype(jnp.bfloat16)
            level[:, cols] = jnp.sum(base, axis=0, keepdims=True)

    def multiply(s, n):
        held = (prod_a, prod_b)[(s * BLOCKS + n) % 2]
        old = (xa, xb)[s % 2]
        for m in range(halves):
            rows = slice(m * MB, (m + 1) * MB)
            held[rows, :] = jnp.dot(
                quad_ref[rows, :], old[:, n * NB:(n + 1) * NB], preferred_element_type=jnp.float32
            )

    def update(s, n):
        held = (prod_a, prod_b)[(s * BLOCKS + n) % 2]
        new = (xb, xa)[s % 2]
        cols = slice(n * NB, (n + 1) * NB)
        mean = level[:, cols] * (1.0 / K)
        sums = jnp.zeros((8, NB), jnp.float32)
        for m in range(K // EB):
            rows = slice(m * EB, (m + 1) * EB)
            each = jnp.concatenate([rate[rows, :]] * each_block, axis=1)
            now = cur[rows, cols]
            now = now + step_source * now * (held[rows, :] - each * mean)
            cur[rows, cols] = now
            if s + 1 < SRC_STEPS:
                new[rows, cols] = now.astype(jnp.bfloat16)
                sums = sums + jnp.sum(now.reshape(EB // 8, 8, NB), axis=0)
        if s + 1 < SRC_STEPS:
            level[:, cols] = jnp.sum(sums, axis=0, keepdims=True)

    def conclude(n):
        for j in range(n * each_block, (n + 1) * each_block):
            base = flat[pl.ds(j, K, stride=RUN), :]
            cols = slice(j * 128, (j + 1) * 128)
            gain = (cur[:, cols] - base).astype(jnp.bfloat16)
            xb[:, cols] = gain
            flat[pl.ds(j, K, stride=RUN), :] = gain.astype(jnp.float32)

    def weigh(n):
        both = stress[n] + jnp.dot(
            coef, xb[:, n * NB:(n + 1) * NB], preferred_element_type=jnp.float32
        )
        for c in range(3):
            row = (both[c:c + 1] + both[3 + c:4 + c] + both[6 + c:7 + c]) * (1.0 / K)
            rows_of[c] += [row[:, i * 128:(i + 1) * 128] for i in range(each_block)]

    for n in range(BLOCKS):
        prepare(n)
    for n in range(BLOCKS):
        stress.append(
            jnp.dot(coef, xa[:, n * NB:(n + 1) * NB], preferred_element_type=jnp.float32)
        )
    for m in range(halves):
        fetch(m).wait()
    turns = [(s, n) for s in range(SRC_STEPS) for n in range(BLOCKS)]
    for i, (s, n) in enumerate(turns):
        multiply(s, n)
        if i > 0:
            update(*turns[i - 1])
    update(*turns[-1])
    for n in range(BLOCKS):
        conclude(n)
    for n in range(BLOCKS):
        weigh(n)
    pieces = []
    for c in range(3):
        whole = jnp.concatenate(rows_of[c], axis=0)
        mean = jnp.sum(jnp.sum(whole, axis=0, keepdims=True), axis=1, keepdims=True)
        mean = jnp.broadcast_to(mean * (1.0 / points), (1, 128))
        high = mean.astype(jnp.bfloat16).astype(jnp.float32)
        low = (mean - high).astype(jnp.bfloat16).astype(jnp.float32)
        pieces += [whole - (high + low), high, low]
    shared = jnp.concatenate(pieces, axis=0).astype(jnp.bfloat16)

    def narrow(o, carry):
        back_ref[o, 0:OWN_ROWS, :] = flat[pl.ds(o * OWN_ROWS, OWN_ROWS), :].astype(jnp.bfloat16)
        back_ref[o, OWN_ROWS:BACK_ROWS, :] = shared
        pltpu.make_async_copy(back_ref.at[o], back_hbm.at[o], out_sem).start()
        return carry

    lax.fori_loop(0, OWNERS, narrow, 0)
    pltpu.make_async_copy(back_ref, back_hbm, out_sem).wait()


def sources(received, quad_matrix, rates, coef):
    points = RUN * 128
    vmem = pl.BlockSpec(memory_space=pltpu.VMEM)
    hbm = pl.BlockSpec(memory_space=pltpu.HBM)
    return pl.pallas_call(
        source_kernel,
        in_specs=[vmem, hbm, vmem, vmem],
        out_specs=hbm,
        out_shape=pltpu.HBM((OWNERS, BACK_ROWS, 128), jnp.bfloat16),
        scratch_shapes=[
            pltpu.VMEM((K, K), jnp.bfloat16),
            pltpu.VMEM((OWNERS, BACK_ROWS, 128), jnp.bfloat16),
            pltpu.VMEM((K, NB), jnp.float32),
            pltpu.VMEM((K, NB), jnp.float32),
            pltpu.VMEM((K * RUN, 128), jnp.float32),
            pltpu.VMEM((K, points), jnp.float32),
            pltpu.VMEM((K, points), jnp.bfloat16),
            pltpu.VMEM((K, points), jnp.bfloat16),
            pltpu.VMEM((K, 128), jnp.float32),
            pltpu.VMEM((1, points), jnp.float32),
            pltpu.SemaphoreType.DMA((K // MB,)),
            pltpu.SemaphoreType.DMA(()),
        ],
        compiler_params=pltpu.CompilerParams(vmem_limit_bytes=30 << 20),
        name="sources",
    )(in_vmem(received), in_hbm(quad_matrix), in_vmem(rates), in_vmem(coef))


def pick_kernel(
    back_ref, points_ref, prop0_hbm, prop1_hbm, out_ref, early0, early1, sems
):
    rows = pl.ds(0, EARLY * KB * ROWS)
    copies = (
        pltpu.make_async_copy(prop0_hbm.at[rows], early0, sems.at[0]),
        pltpu.make_async_copy(prop1_hbm.at[rows], early1, sems.at[1]),
    )
    for copy in copies:
        copy.start()
    pieces = []
    for i in range(PIECES):
        at = OWN_ROWS + 8 * i
        rows = back_ref[:, at:at + 8, :].astype(jnp.float32).reshape(OWNERS * 8, 128)
        pieces.append(rows.T.astype(jnp.bfloat16))
    table = jnp.concatenate(pieces, axis=0)
    kind = lax.broadcasted_iota(jnp.int32, (8, 128), 0)
    slot = lax.broadcasted_iota(jnp.int32, (OWNERS, 8, 128), 0) * 8 + kind
    within = lax.broadcasted_iota(jnp.int32, (128, 128), 0)
    weights = (0.5, 0.3, 0.2)
    for t in range(TILES):
        hots, lows = [], []
        for m in range(3):
            p = points_ref[m * TILES + t:m * TILES + t + 1, :]
            row = p >> 8
            col = p & 255
            hi = (((col >> 7) * GROUP + (row & (GROUP - 1))) << 3) + (row >> 4)
            wanted = jnp.where(kind < RUN, hi, (hi & -8) + kind)
            taken = jnp.where(slot == wanted, 1.0, 0.0).reshape(OWNERS * 8, 128)
            hots.append(taken.astype(jnp.bfloat16))
            lows.append(col & 127)
        hot = jnp.concatenate(hots, axis=1)
        found = jnp.dot(table, hot, preferred_element_type=jnp.float32)
        for c in range(3):
            both = found[c * 128:(c + 1) * 128]
            acc = jnp.zeros((8, 128), jnp.float32)
            for m in range(3):
                kept = jnp.where(within == lows[m], both[:, m * 128:(m + 1) * 128], 0.0)
                acc = acc + weights[m] * jnp.sum(kept.reshape(16, 8, 128), axis=0)
            out_ref[c, t:t + 1, :] = jnp.sum(acc, axis=0, keepdims=True)
    for copy in copies:
        copy.wait()


def pick(back, points, prop0, prop1):
    vmem = pl.BlockSpec(memory_space=pltpu.VMEM)
    hbm = pl.BlockSpec(memory_space=pltpu.HBM)
    early = pltpu.VMEM((EARLY * KB * ROWS, 128), jnp.float32)
    return pl.pallas_call(
        pick_kernel,
        in_specs=[vmem, vmem, hbm, hbm],
        out_specs=[vmem] * 3,
        out_shape=[pltpu.VMEM((3, TILES, 128), jnp.float32), early, early],
        scratch_shapes=[pltpu.SemaphoreType.DMA((2,))],
        compiler_params=pltpu.CompilerParams(vmem_limit_bytes=10 << 20),
        name="pick",
    )(in_vmem(back), in_vmem(points), in_hbm(prop0), in_hbm(prop1))


WIDE = 256


def water(own_ref, one_ref, two_ref, three_ref, out_ref, whole, result):
    bands = 4
    tile = own_ref.shape[1]
    width = own_ref.shape[2]
    own_cols = width - 2 * MARGIN
    band = lax.axis_index("band")
    comp = lax.axis_index("comp")
    whole[...] = jnp.zeros_like(whole)
    for d, ref in enumerate((own_ref, one_ref, two_ref, three_ref)):
        row = pl.multiple_of((band ^ d) * tile, tile)
        whole[:, pl.ds(row, tile), 0:width] = ref[...]
    shape = (bands * tile, WIDE)
    lane = lax.broadcasted_iota(jnp.int32, shape, 1)
    line = lax.broadcasted_iota(jnp.int32, shape, 0)
    col = comp * own_cols - MARGIN + lane
    inside = (col >= 0) & (col < lax.axis_size("comp") * own_cols) & (lane < width)
    first = line == 0
    last = line == shape[0] - 1

    def dx(f):
        after = jnp.where(last, 0.0, pltpu.roll(f, shape[0] - 1, 0))
        before = jnp.where(first, 0.0, pltpu.roll(f, 1, 0))
        return 0.5 * (after - before)

    def dy(f):
        return 0.5 * (pltpu.roll(f, WIDE - 1, 1) - pltpu.roll(f, 1, 1))

    sxx, sxy, syy = (jnp.where(inside, whole[3 + c], 0.0) for c in range(3))
    force_down = -forcing_gain * (dx(sxx) + dy(sxy))
    force_across = -forcing_gain * (dx(sxy) + dy(syy))
    height, down, across = (whole[c] for c in range(3))
    for _ in range(SW_STEPS):
        height = jnp.where(inside, height - wave_speed * (dx(down) + dy(across)), 0.0)
        down = jnp.where(
            inside, (1.0 - friction) * down - wave_speed * dx(height) + force_down, 0.0
        )
        across = jnp.where(
            inside, (1.0 - friction) * across - wave_speed * dy(height) + force_across, 0.0
        )
    for c, value in enumerate((height, down, across)):
        result[c] = pltpu.roll(value, WIDE - MARGIN, 1)[:, :own_cols]
        out_ref[c] = result[c, pl.ds(pl.multiple_of(band * tile, tile), tile), :]


def spread(back_ref, wide, i):
    rows = pl.ds(pl.multiple_of(i * KB * RUN, 8), KB * RUN)
    for h in range(2):
        for g in range(GROUP):
            gain = back_ref[h * GROUP + g, rows, :].astype(jnp.float32)
            wide[h, pl.ds(g, KB * RUN, stride=GROUP), :] = gain


def add(halves, wide, out, i):
    for kk in range(KB):
        k = i * KB + kk
        for h, prop in enumerate(halves):
            rows = pl.ds(k * ROWS, ROWS)
            out[k, :, h * 128:(h + 1) * 128] = (
                prop[rows, :] + wide[h, kk * ROWS:(kk + 1) * ROWS, :]
            )


def group_copy(out, out_hbm, sems, i):
    part = pl.ds(i * KB, KB)
    return pltpu.make_async_copy(out.at[part], out_hbm.at[part], sems.at[i])


def begin_kernel(back_ref, early0, early1, out_hbm, wide, out, sems):
    def one(i, carry):
        spread(back_ref, wide, i)
        add((early0, early1), wide, out, i)
        group_copy(out, out_hbm, sems, i).start()
        return carry

    def settle(i, carry):
        group_copy(out, out_hbm, sems, i).wait()
        return carry

    lax.fori_loop(0, EARLY, one, 0)
    lax.fori_loop(0, EARLY, settle, 0)


def begin_sum(back, early0, early1):
    vmem = pl.BlockSpec(memory_space=pltpu.VMEM)
    hbm = pl.BlockSpec(memory_space=pltpu.HBM)
    return pl.pallas_call(
        begin_kernel,
        in_specs=[vmem] * 3,
        out_specs=hbm,
        out_shape=pltpu.HBM((LOCAL, ROWS, 256), jnp.float32),
        scratch_shapes=[
            pltpu.VMEM((2, KB * ROWS, 128), jnp.float32),
            pltpu.VMEM((EARLY * KB, ROWS, 256), jnp.float32),
            pltpu.SemaphoreType.DMA((EARLY,)),
        ],
        compiler_params=pltpu.CompilerParams(vmem_limit_bytes=8 << 20),
        name="begin",
    )(*map(in_vmem, (back, early0, early1)))


def close_kernel(
    back_ref, prop0_hbm, prop1_hbm, begun_hbm, own_ref, one_ref, two_ref, three_ref,
    out_hbm, water_ref, prop0, prop1, wide, out, sems, keep_sems, whole, result,
):
    count = LOCAL // KB

    def keep(i):
        part = pl.ds(i * KB * ROWS, KB * ROWS)
        return [
            pltpu.make_async_copy(hbm.at[part], prop.at[part], keep_sems.at[h, i])
            for h, (prop, hbm) in enumerate(((prop0, prop0_hbm), (prop1, prop1_hbm)))
        ]

    def load(i, carry):
        for copy in keep(i):
            copy.start()
        return carry

    def one(i, carry):
        spread(back_ref, wide, i)
        for copy in keep(i):
            copy.wait()
        add((prop0, prop1), wide, out, i)
        group_copy(out, out_hbm, sems, i).start()
        return carry

    def settle(i, carry):
        group_copy(out, out_hbm, sems, i).wait()
        return carry

    lax.fori_loop(EARLY, count, load, 0)
    lax.fori_loop(EARLY, count, one, 0)
    water(own_ref, one_ref, two_ref, three_ref, water_ref, whole, result)
    lax.fori_loop(EARLY, count, settle, 0)


def close_sum(back, prop0, prop1, begun, tiles):
    vmem = pl.BlockSpec(memory_space=pltpu.VMEM)
    hbm = pl.BlockSpec(memory_space=pltpu.HBM)
    fields, rows, width = tiles[0].shape
    own_cols = width - 2 * MARGIN
    shape = (LOCAL, ROWS, 256)
    return pl.pallas_call(
        close_kernel,
        in_specs=[vmem, hbm, hbm, hbm] + [vmem] * 4,
        out_specs=[hbm, vmem],
        out_shape=[
            pltpu.HBM(shape, jnp.float32),
            jax.ShapeDtypeStruct((3, rows, own_cols), jnp.float32),
        ],
        input_output_aliases={3: 0},
        scratch_shapes=[
            pltpu.VMEM((LOCAL * ROWS, 128), jnp.float32),
            pltpu.VMEM((LOCAL * ROWS, 128), jnp.float32),
            pltpu.VMEM((2, KB * ROWS, 128), jnp.float32),
            pltpu.VMEM(shape, jnp.float32),
            pltpu.SemaphoreType.DMA((LOCAL // KB,)),
            pltpu.SemaphoreType.DMA((2, LOCAL // KB)),
            pltpu.VMEM((fields, 4 * rows, WIDE), jnp.float32),
            pltpu.VMEM((3, 4 * rows, own_cols), jnp.float32),
        ],
        compiler_params=pltpu.CompilerParams(vmem_limit_bytes=18 << 20),
        name="close",
    )(in_vmem(back), *map(in_hbm, (prop0, prop1, begun)), *map(in_vmem, tiles))


def from_neighbours(low, high, axis):
    count = lax.axis_size(axis)
    ends = count - 1
    before = lax.ppermute(high, axis, [(i, (i + 1) % count) for i in range(ends)])
    after = lax.ppermute(low, axis, [((i + 1) % count, i) for i in range(ends)])
    return before, after


def window(spectrum, wet_mask, quad_matrix, dissipation, circulation, source_points):
    offset = lax.axis_index("comp") * LOCAL
    speed_east, speed_north, _ = component_tables(offset, LOCAL)
    speeds = jnp.stack([speed_east, speed_north])
    low, high, wetness, begin = rims(spectrum, wet_mask)
    top, bottom = from_neighbours(low, high, "band")
    prop0, prop1, sent = propagate(speeds, spectrum, top, bottom, wetness, begin)
    received = lax.all_to_all(sent, "comp", 0, 0, tiled=True)

    tile_rows = circulation.shape[1]
    both = jnp.concatenate([circulation, source_points.astype(jnp.float32)], axis=0)
    before, after = from_neighbours(both[:, :, :MARGIN], both[:, :, -MARGIN:], "comp")
    wide = jnp.concatenate([before, both, after], axis=2)
    left_points = before[3:].astype(jnp.int32).reshape(3, 1, 128)
    right_points = after[3:].astype(jnp.int32).reshape(3, 1, 128)
    points = jnp.concatenate([source_points, left_points, right_points], axis=1)
    points = points.reshape(3 * TILES, 128)

    full_coef = component_tables(0, K)[2]
    coef_high = full_coef.astype(jnp.bfloat16).astype(jnp.float32)
    coef_mid = (full_coef - coef_high).astype(jnp.bfloat16).astype(jnp.float32)
    coef_low = full_coef - coef_high - coef_mid
    spare = jnp.zeros((7, K), jnp.float32)
    coef = jnp.concatenate([coef_high, coef_mid, coef_low, spare]).astype(jnp.bfloat16)
    back = sources(
        received.reshape(K * RUN, 128), quad_matrix, dissipation.reshape(K // 128, 128), coef
    )
    back = lax.all_to_all(back, "comp", 0, 0, tiled=True)
    cells, early0, early1 = pick(back, points, prop0, prop1)
    own = cells[:, :tile_rows]
    left = cells[:, tile_rows].reshape(3, tile_rows, MARGIN)
    right = cells[:, tile_rows + 1].reshape(3, tile_rows, MARGIN)
    wide_cells = jnp.concatenate([left, own, right], axis=2)
    tile = jnp.concatenate([wide[:3], wide_cells], axis=0)
    bands = lax.axis_size("band")
    tiles = [tile]
    for d in range(1, bands):
        tiles.append(lax.ppermute(tile, "band", [(i, i ^ d) for i in range(bands)]))
    begun = begin_sum(back, early0, early1)
    spectrum_out, circulation_out = close_sum(back, prop0, prop1, begun, tiles)
    return spectrum_out, circulation_out


def solution(mesh):
    in_specs = (
        P("comp", "band", None),
        P("band", None),
        P(),
        P(),
        P(None, "band", "comp"),
        P(None, "band", "comp"),
    )
    out_specs = (P("comp", "band", None), P(None, "band", "comp"))
    return jax.shard_map(window, mesh=mesh, in_specs=in_specs, out_specs=out_specs, check_vma=False)
```
